128 devices in a mesh: paths: 16 (over z, y_lo, core), stocks: 8 (over x, y_hi).
Axes of the slice: x: 4, y: 4 (y_hi: 2, y_lo: 2; y = y_hi * 2 + y_lo), z: 4, core: 2. Of those that a mesh axis runs over, the one named last changes fastest.
Arguments:
- prices: bfloat16 [256, 262144], P('stocks', 'paths'), may hold values from -18 to 18
- loadings: bfloat16 [256, 32], P('stocks'), may hold values from -0.25 to 0.25
- basis_w: float32 [32, 512], replicated, may hold values from -1 to 1
- basis_bias: float32 [512], replicated, may hold values from -1 to 1
- payoff: bfloat16 [262144], P('paths'), may hold values from -4 to 4
- in_fit: int32 [262144], P('paths'), may hold values 0 or 1
- cotangent: bfloat16 [256, 262144], P('stocks', 'paths'), may hold values from -6 to 6
- shocks: bfloat16 [4, 256, 262144], P(None, 'stocks', 'paths'), may hold values from -6 to 6
- corr_gen: bfloat16 [256, 256], replicated, may hold values from -0.375 to 0.375
- basket: float32 [256], replicated, may hold values from 0.2 to 2
- exercise: int32 [4, 262144], P(None, 'paths'), may hold values 0 or 1
- bucket: int32 [4, 262144], P(None, 'paths'), may hold values from 0 to 255
Outputs:
- delta_out: float32 [256, 262144], P('stocks', 'paths')
- surface: float32 [256, 256], P('stocks', 'paths')
The draws below stay inside these ranges and needn't reach their ends.
All inputs are finite; a program needn't handle non-finite values. No bound on the sum of `in_fit` or of `exercise` on one device may be relied on, other than what follows from the above.
Results may differ from the reference program's by a relative error of at most 0.003.
Values may be sent and summed in bfloat16 or wider, within the bound.
No kernel may reach another device: no remote copies, remote signals or barrier semaphores. Data moves between devices by JAX's collectives and lax.ppermute only.
A program may use at most 192 MiB of HBM per device.

```python
import jax
import jax.numpy as jnp
from jax import lax

S = 256
K = 32
B = 512
NK = 256
STEPS = 4
PATHS = 262144


def price_state(key):
    price_key = jax.random.fold_in(key, 101)
    position = jnp.arange(PATHS, dtype=jnp.float32) / PATHS
    random_part = jax.random.truncated_normal(price_key, -6.0, 6.0, (S, PATHS), jnp.float32)
    path_scale = jnp.exp(jnp.log(3.0) * position)
    return (random_part * path_scale[None, :]).astype(jnp.bfloat16)


def loading_table(key):
    load_key = jax.random.fold_in(key, 102)
    limit = min(4.0, 0.25 * S ** 0.5)
    values = jax.random.truncated_normal(load_key, -limit, limit, (S, K), jnp.float32) / S ** 0.5
    values = jnp.clip(values, -0.25, 0.25)
    return values.astype(jnp.bfloat16)


def draw_prices(key, part):
    return price_state(key)


def draw_loadings(key, part):
    return loading_table(key)


def draw_payoff(key, part):
    prices = price_state(key)
    loads = loading_table(key)
    factors = lax.dot_general(loads, prices, (((0,), (0,)), ((), ())), preferred_element_type=jnp.float32)
    directions = jax.random.normal(jax.random.fold_in(key, 103), (2, K), jnp.float32) / K ** 0.5
    levels = jnp.dot(directions, factors, preferred_element_type=jnp.float32, precision=lax.Precision.HIGHEST)
    shaped = 2.0 * jnp.tanh(0.7 * levels[0]) + 0.8 * jnp.abs(jnp.tanh(levels[1])) - 0.4
    noise = 0.3 * jax.random.truncated_normal(jax.random.fold_in(key, 104), -3.0, 3.0, (PATHS,), jnp.float32)
    return jnp.clip(shaped + noise, -4.0, 4.0).astype(jnp.bfloat16)


def with_ends(result, key, low, high):
    longest = result.shape.index(max(result.shape))
    spots = []
    for shift in (0, 1):
        where = [jax.random.randint(jax.random.fold_in(key, axis), (), 0, length) for axis, length in enumerate(result.shape)]
        where[longest] = (where[longest] + shift) % result.shape[longest]
        spots.append(tuple(where))
    return result.at[spots[0]].set(low).at[spots[1]].set(high)


def level_of(own_key, dims, shards, least, top_value):
    level = 1.0
    for axis_at, blocks in shards:
        draws = jax.random.uniform(jax.random.fold_in(jax.random.fold_in(own_key, 6), axis_at), (blocks,), jnp.float32, least / len(shards), top_value / len(shards))
        level = level * jnp.repeat(jnp.exp(draws), dims[axis_at] // blocks).reshape((-1,) + (1,) * (len(dims) - 1 - axis_at))
    return level


def scatter_about(key, dims, scale, bound, shards=(), kind=jnp.bfloat16):
    result = scale * jax.random.normal(key, dims, jnp.float32)
    if shards:
        result = result * level_of(key, dims, shards, -0.22, 0.18)
    return jnp.clip(result, -bound, bound).astype(kind)


def setup_inputs(seed: int = 0) -> dict:
    streams_of = jax.random.split(jax.random.key(seed), 13)
    return {
        "prices": draw_prices(jax.random.fold_in(streams_of[12], 71), 0),
        "loadings": draw_loadings(jax.random.fold_in(streams_of[12], 71), 0),
        "basis_w": scatter_about(streams_of[2], (K, B), K ** -0.5, 1.0, (), jnp.float32),
        "basis_bias": jnp.clip(jax.random.uniform(streams_of[3], (B,), jnp.float32, -1.0, 1.0), -1.0, 1.0),
        "payoff": draw_payoff(jax.random.fold_in(streams_of[12], 71), 0),
        "in_fit": with_ends((jax.random.randint(streams_of[5], (PATHS,), 0, 3) < 2).astype(jnp.int32), jax.random.fold_in(streams_of[5], 1), 0, 1),
        "cotangent": scatter_about(streams_of[6], (S, PATHS), 1.0, 6.0, ((0, 8), (1, 16))),
        "shocks": scatter_about(streams_of[7], (STEPS, S, PATHS), 1.0, 6.0, ((1, 8), (2, 16))),
        "corr_gen": scatter_about(streams_of[8], (S, S), S ** -0.5, 0.375),
        "basket": jnp.clip(jax.random.uniform(streams_of[9], (S,), jnp.float32, 0.2, 2.0), 0.2, 2.0),
        "exercise": with_ends((jax.random.randint(streams_of[10], (STEPS, PATHS), 0, 4) < 1).astype(jnp.int32), jax.random.fold_in(streams_of[10], 1), 0, 1),
        "bucket": with_ends(jax.random.randint(streams_of[11], (STEPS, PATHS), 0, NK), jax.random.fold_in(streams_of[11], 1), 0, NK - 1).astype(jnp.int32),
    }


time_step = 0.25
ridge_weight = 0.1

def make_basis(factors, basis_w, basis_bias):
    raised = jnp.dot(basis_w.T.astype(jnp.float32), factors.astype(jnp.float32), preferred_element_type=jnp.float32, precision=lax.Precision.HIGHEST) + basis_bias[:, None]
    return jnp.tanh(raised).astype(jnp.bfloat16)

def regression_sums(basis, payoff, in_fit):
    picked = basis * in_fit.astype(jnp.bfloat16)[None, :]
    gram_sums = lax.dot_general(picked.astype(jnp.float32), basis.astype(jnp.float32), (((1,), (1,)), ((), ())), preferred_element_type=jnp.float32)
    moment = jnp.dot(picked.astype(jnp.float32), payoff.astype(jnp.float32), preferred_element_type=jnp.float32)
    return (gram_sums, moment)

def solve_coefficients(gram_sums, moment, path_count):
    system = gram_sums / path_count + ridge_weight * jnp.eye(gram_sums.shape[0], dtype=jnp.float32)
    cholesky_factor = jnp.linalg.cholesky(system)
    return jax.scipy.linalg.cho_solve((cholesky_factor, True), moment / path_count)

def reference(prices, loadings, basis_w, basis_bias, payoff, in_fit, cotangent, shocks, corr_gen, basket, exercise, bucket):
    factors = lax.dot_general(loadings.astype(jnp.float32), prices.astype(jnp.float32), (((0,), (0,)), ((), ())), preferred_element_type=jnp.float32)
    basis = make_basis(factors, basis_w, basis_bias)
    gram_sums, moment = regression_sums(basis, payoff, in_fit)
    coefficients = solve_coefficients(gram_sums, moment, PATHS * 1.0)
    continuation = jnp.dot(coefficients.astype(jnp.float32), basis.astype(jnp.float32), preferred_element_type=jnp.float32, precision=lax.Precision.HIGHEST)
    adjoint = cotangent.astype(jnp.float32)
    surface = jnp.zeros((S, NK), jnp.float32)
    strikes = jnp.arange(NK, dtype=jnp.int32)
    for date_index in range(STEPS - 1, -1, -1):
        mixed_rows = jnp.dot(corr_gen.astype(jnp.float32), adjoint.astype(jnp.bfloat16).astype(jnp.float32), preferred_element_type=jnp.float32)
        adjoint = adjoint + time_step * mixed_rows + exercise[date_index].astype(jnp.float32)[None, :] * continuation[None, :] * basket[:, None]
        vega_terms = (adjoint * shocks[date_index].astype(jnp.float32)).astype(jnp.bfloat16)
        one_hot = (bucket[date_index][:, None] == strikes[None, :]).astype(jnp.bfloat16)
        surface = surface + jnp.dot(vega_terms.astype(jnp.float32), one_hot.astype(jnp.float32), preferred_element_type=jnp.float32)
    return (adjoint, surface)
```

```python
import jax
import jax.numpy as jnp
from jax import lax
from jax.experimental import pallas as pl
from jax.experimental.pallas import tpu as pltpu
from jax.sharding import Mesh
from jax.sharding import PartitionSpec as P

NK = 256
STEPS = 4
TIME_STEP = 0.25
RIDGE = 0.1
LANES = 128
BLOCK = 128
TILE = 512
PATH_AXES = ("z", "ylo", "core")
STOCK_AXES = ("x", "yhi")
ALL_AXES = PATH_AXES + STOCK_AXES
FINE = (4, 2, 2, 4, 2)
f32 = jnp.float32
bf16 = jnp.bfloat16


def three_terms(x):
    high = x.astype(bf16)
    rest = x - high.astype(f32)
    middle = rest.astype(bf16)
    low = (rest - middle.astype(f32)).astype(bf16)
    return high, middle, low


def left_terms(x, axis):
    high, middle, low = three_terms(x)
    return jnp.concatenate([high, high, middle, high, low, middle], axis=axis)


def right_terms(x, axis):
    high, middle, low = three_terms(x)
    return jnp.concatenate([high, middle, high, low, high, middle], axis=axis)


def exact_dot(left, right):
    return jnp.dot(left_terms(left, 1), right_terms(right, 0), preferred_element_type=f32)


GRAM_BLOCKS = tuple((i, j) for i in range(4) for j in range(i + 1))
MOMENT_ROW = len(GRAM_BLOCKS) * BLOCK
SUM_ROWS = 1344
PIECE = SUM_ROWS // 8


def gram_kernel(slab_ref, moved_ref, table_ref, weight_ref, bias_ref, payoff_ref, fit_ref,
                basis_ref, sums_ref, gram_ref, moment_ref):
    step = pl.program_id(0)
    tile = moved_ref[...].reshape(256, TILE)
    loads = table_ref[...].reshape(256, LANES)[:, :32]
    factors = lax.dot_general(loads, tile, (((0,), (0,)), ((), ())), preferred_element_type=f32)
    raised = lax.dot_general(
        weight_ref[...], right_terms(factors, 0), (((0,), (0,)), ((), ())), preferred_element_type=f32
    )
    basis = jnp.tanh(raised + bias_ref[...]).astype(bf16)
    basis_ref[...] = basis
    picked = basis * fit_ref[...].astype(f32).astype(bf16)
    paid = jnp.broadcast_to(payoff_ref[...].astype(f32), (16, TILE)).astype(bf16)
    contract = (((1,), (1,)), ((), ()))
    first = lax.dot_general(picked[:256], basis[:256], contract, preferred_element_type=f32)
    second = lax.dot_general(picked[256:], basis, contract, preferred_element_type=f32)
    moment = lax.dot_general(paid, picked, contract, preferred_element_type=f32)

    @pl.when(step == 0)
    def _():
        gram_ref[:256, :256] = first
        gram_ref[256:, :] = second
        moment_ref[...] = moment

    @pl.when(step > 0)
    def _():
        gram_ref[:256, :256] += first
        gram_ref[256:, :] += second
        moment_ref[...] += moment

    @pl.when(step == pl.num_programs(0) - 1)
    def _():
        for at, (i, j) in enumerate(GRAM_BLOCKS):
            sums_ref[at * BLOCK:(at + 1) * BLOCK, :] = gram_ref[
                i * BLOCK:(i + 1) * BLOCK, j * BLOCK:(j + 1) * BLOCK
            ]
        sums_ref[MOMENT_ROW:, :] = jnp.zeros((SUM_ROWS - MOMENT_ROW, LANES), f32)
        for i in range(4):
            sums_ref[MOMENT_ROW + 8 * i:MOMENT_ROW + 8 * i + 8, :] = moment_ref[
                :8, i * BLOCK:(i + 1) * BLOCK
            ]


def regression_sums(slab, moved, weights, bias, payoff, fit, slab_part):
    tiles = slab_part // TILE
    table_at = slab_part // LANES

    def own(step, slab_ref):
        return (0, slab_ref[0] * tiles + step)

    return pl.pallas_call(
        gram_kernel,
        out_shape=(
            jax.ShapeDtypeStruct((512, slab_part), bf16),
            jax.ShapeDtypeStruct((SUM_ROWS, LANES), f32),
        ),
        grid_spec=pltpu.PrefetchScalarGridSpec(
            num_scalar_prefetch=1,
            grid=(tiles,),
            in_specs=[
                pl.BlockSpec((8, 32, TILE), lambda i, s: (0, 0, i)),
                pl.BlockSpec((8, 32, LANES), lambda i, s: (0, 0, table_at)),
                pl.BlockSpec((192, 512), lambda i, s: (0, 0)),
                pl.BlockSpec((512, 1), lambda i, s: (0, 0)),
                pl.BlockSpec((1, TILE), own),
                pl.BlockSpec((1, TILE), own),
            ],
            out_specs=(
                pl.BlockSpec((512, TILE), lambda i, s: (0, i)),
                pl.BlockSpec((SUM_ROWS, LANES), lambda i, s: (0, 0)),
            ),
            scratch_shapes=[pltpu.VMEM((512, 512), f32), pltpu.VMEM((16, 512), f32)],
        ),
        compiler_params=pltpu.CompilerParams(vmem_limit_bytes=40 << 20),
        name="regression_sums",
    )(slab, moved, moved, weights, bias, payoff, fit)


def exchange_with_others(x, axes, count, piece_of=None):
    received = []
    for flip in range(1, count):
        sent = x if piece_of is None else piece_of(flip)
        received.append(lax.ppermute(sent, axes, [(i, i ^ flip) for i in range(count)]))
    return received


def all_device_sum(sums):
    core = lax.axis_index("core")
    z = lax.axis_index("z")
    halves = sums.reshape(2, 4, PIECE, LANES)
    mine = lax.dynamic_index_in_dim(halves, core, 0, False)
    other = lax.dynamic_index_in_dim(halves, 1 - core, 0, False)
    mine = mine + exchange_with_others(other, "core", 2)[0]

    def piece_of(flip):
        return lax.dynamic_index_in_dim(mine, z ^ flip, 0, False)

    share = piece_of(0)
    for part in exchange_with_others(None, "z", 4, piece_of):
        share = share + part
    for axes in ("x", ("ylo", "yhi")):
        parts = exchange_with_others(share, axes, 4)
        share = (share + parts[0]) + (parts[1] + parts[2])
    column = jnp.stack([share] + exchange_with_others(share, "z", 4))
    return column, exchange_with_others(column, "core", 2)[0]


def lane_column(x, j):
    return jnp.broadcast_to(x[:, j:j + 1], (8, LANES))


def sublane_row(x, j):
    return jnp.broadcast_to(x[j:j + 1, :], (8, LANES))


def pivot_rows(panel, base, lane, sub):
    inside = (lane >= base) & (lane < base + 8)
    columns = [lane_column(panel, base + j) for j in range(8)]
    d = {(i, j): sublane_row(columns[j], i) for j in range(8) for i in range(j, 8)}
    marked = jnp.where(inside, jnp.where(lane - base == sub, 1.0, 0.0), panel)
    y = [sublane_row(marked, j) for j in range(8)]
    lower = {}
    inverse = []
    for j in range(8):
        inverse.append(1.0 / d[j, j])
        for i in range(j + 1, 8):
            lower[i, j] = d[i, j] * inverse[j]
        for k in range(j + 1, 8):
            for i in range(k, 8):
                d[i, k] = d[i, k] - lower[i, j] * d[k, j]
        for i in range(j + 1, 8):
            y[i] = y[i] - lower[i, j] * y[j]
    y = [y[j] * inverse[j] for j in range(8)]
    for j in range(7, -1, -1):
        for i in range(j):
            y[i] = y[i] - lower[j, i] * y[j]
    return y


def eliminated(x, rows, base, lane):
    inside = (lane >= base) & (lane < base + 8)
    t = [lane_column(x, base + j) * rows[j] for j in range(8)]
    total = ((t[0] + t[1]) + (t[2] + t[3])) + ((t[4] + t[5]) + (t[6] + t[7]))
    return jnp.where(inside, 0.0, x) - total


def inverse_of_block(rows):
    lane = lax.broadcasted_iota(jnp.int32, (8, LANES), 1)
    sub = lax.broadcasted_iota(jnp.int32, (8, LANES), 0)
    rows = list(rows)
    for g in range(16):
        pivots = pivot_rows(rows[g], 8 * g, lane, sub)
        for t in range(1, 16):
            h = (g + t) % 16
            rows[h] = eliminated(rows[h], pivots, 8 * g, lane)
        own = pivots[0]
        for j in range(1, 8):
            own = jnp.where(sub == j, pivots[j], own)
        rows[g] = own
    return rows


def solve_kernel(at_ref, near_ref, far_ref, out_ref, sums_ref, system_ref, inverse_ref, *, scale):
    core = at_ref[0]
    z = at_ref[1]
    for flip in range(4):
        at = pl.multiple_of((core * 4 + (z ^ flip)) * PIECE, 8)
        sums_ref[pl.ds(at, PIECE), :] = near_ref[flip]
        at = pl.multiple_of(((1 - core) * 4 + (z ^ flip)) * PIECE, 8)
        sums_ref[pl.ds(at, PIECE), :] = far_ref[flip]
    diagonal = (
        lax.broadcasted_iota(jnp.int32, (BLOCK, BLOCK), 0)
        == lax.broadcasted_iota(jnp.int32, (BLOCK, BLOCK), 1)
    )
    for at, (i, j) in enumerate(GRAM_BLOCKS):
        block = sums_ref[at * BLOCK:(at + 1) * BLOCK, :] * scale
        if i == j:
            block = block + jnp.where(diagonal, RIDGE, 0.0)
        else:
            system_ref[j * BLOCK:(j + 1) * BLOCK, i * BLOCK:(i + 1) * BLOCK] = block.T
        system_ref[i * BLOCK:(i + 1) * BLOCK, j * BLOCK:(j + 1) * BLOCK] = block
    for i in range(4):
        row = sums_ref[MOMENT_ROW + 8 * i:MOMENT_ROW + 8 * i + 1, :] * scale
        system_ref[i * BLOCK:(i + 1) * BLOCK, 512:] = jnp.broadcast_to(row, (BLOCK, BLOCK)).T

    for i in range(4):
        lo = i * BLOCK
        inverse = inverse_of_block(
            [system_ref[lo + 8 * g:lo + 8 * g + 8, lo:lo + BLOCK] for g in range(16)]
        )
        inverse = jnp.concatenate(inverse, axis=0)
        solved = exact_dot(inverse, system_ref[lo:lo + BLOCK, lo + BLOCK:])
        for j in range(4):
            if j != i:
                system_ref[j * BLOCK:(j + 1) * BLOCK, lo + BLOCK:] -= exact_dot(
                    system_ref[j * BLOCK:(j + 1) * BLOCK, lo:lo + BLOCK], solved
                )
        system_ref[lo:lo + BLOCK, lo + BLOCK:] = solved
    out_ref[...] = system_ref[:, 512:]


def solve_coefficients(near, far, path_count):
    at = jnp.stack([lax.axis_index("core"), lax.axis_index("z")]).astype(jnp.int32)
    whole = pl.BlockSpec((4, PIECE, LANES), lambda i, s: (0, 0, 0))
    return pl.pallas_call(
        lambda *refs: solve_kernel(*refs, scale=1.0 / path_count),
        out_shape=jax.ShapeDtypeStruct((512, LANES), f32),
        grid_spec=pltpu.PrefetchScalarGridSpec(
            num_scalar_prefetch=1,
            grid=(1,),
            in_specs=[whole, whole],
            out_specs=pl.BlockSpec((512, LANES), lambda i, s: (0, 0)),
            scratch_shapes=[
                pltpu.VMEM((SUM_ROWS, LANES), f32),
                pltpu.VMEM((512, 512 + LANES), f32),
                pltpu.VMEM((BLOCK, BLOCK), f32),
            ],
        ),
        compiler_params=pltpu.CompilerParams(vmem_limit_bytes=40 << 20),
        name="solve_coefficients",
    )(at, near, far)


def dates_kernel(slab_ref, coefficient_ref, basis_ref, moved_ref, mixer_ref, basket_ref, exercise_ref,
                 bucket_ref, delta_ref, surface_ref, total_ref):
    step = pl.program_id(0)
    parts = [jnp.zeros((8, TILE), f32) for _ in range(4)]
    for b in range(64):
        weight = jnp.broadcast_to(coefficient_ref[8 * b:8 * b + 8, :1], (8, TILE))
        parts[b % 4] += weight * basis_ref[8 * b:8 * b + 8, :].astype(f32)
    continuation = jnp.sum((parts[0] + parts[1]) + (parts[2] + parts[3]), axis=0, keepdims=True)
    adjoint = moved_ref[:, 0].reshape(256, TILE).astype(f32)
    basket = basket_ref[...]
    strikes = lax.broadcasted_iota(jnp.int32, (NK, TILE), 0)
    total = jnp.zeros((NK, 256), f32)
    for date in range(STEPS - 1, -1, -1):
        mixed = jnp.dot(mixer_ref[...], adjoint.astype(bf16), preferred_element_type=f32)
        held = exercise_ref[date:date + 1, :].astype(f32) * continuation
        adjoint = adjoint + TIME_STEP * mixed + held * basket
        terms = (adjoint * moved_ref[:, date + 1].reshape(256, TILE).astype(f32)).astype(bf16)
        chosen = jnp.where(strikes == bucket_ref[date:date + 1, :], 1.0, 0.0).astype(bf16)
        total = total + lax.dot_general(
            chosen, terms, (((1,), (1,)), ((), ())), preferred_element_type=f32
        )
    delta_ref[...] = adjoint.astype(bf16).reshape(8, 32, TILE)

    @pl.when(step == 0)
    def _():
        total_ref[...] = total

    @pl.when(step > 0)
    def _():
        total_ref[...] += total

    @pl.when(step == pl.num_programs(0) - 1)
    def _():
        grouped = total_ref[...].reshape(16, 16, 256)
        for s in range(8):
            for q in range(4):
                surface_ref[:, s, :, 32 * q:32 * q + 32] = grouped[
                    :, 4 * q:4 * q + 4, 32 * s:32 * s + 32
                ]


def date_loop(slab, coefficients, basis, moved, mixer, basket, exercise, bucket, slab_part):
    tiles = slab_part // TILE

    def own(step, slab_ref):
        return (0, slab_ref[0] * tiles + step)

    return pl.pallas_call(
        dates_kernel,
        out_shape=(
            jax.ShapeDtypeStruct((8, 32, slab_part), bf16),
            jax.ShapeDtypeStruct((16, 8, 4, LANES), f32),
        ),
        grid_spec=pltpu.PrefetchScalarGridSpec(
            num_scalar_prefetch=1,
            grid=(tiles,),
            in_specs=[
                pl.BlockSpec((512, LANES), lambda i, s: (0, 0)),
                pl.BlockSpec((512, TILE), lambda i, s: (0, i)),
                pl.BlockSpec((8, 5, 32, TILE), lambda i, s: (0, 0, 0, i)),
                pl.BlockSpec((256, 256), lambda i, s: (0, 0)),
                pl.BlockSpec((256, 1), lambda i, s: (0, 0)),
                pl.BlockSpec((4, TILE), own),
                pl.BlockSpec((4, TILE), own),
            ],
            out_specs=(
                pl.BlockSpec((8, 32, TILE), lambda i, s: (0, 0, i)),
                pl.BlockSpec((16, 8, 4, LANES), lambda i, s: (0, 0, 0, 0)),
            ),
            scratch_shapes=[pltpu.VMEM((NK, 256), f32)],
        ),
        compiler_params=pltpu.CompilerParams(vmem_limit_bytes=48 << 20),
        name="date_loop",
    )(slab, coefficients, basis, moved, mixer, basket, exercise, bucket)


def per_device(prices, loadings, basis_w, basis_bias, payoff, in_fit, cotangent, shocks, corr_gen,
               basket, exercise, bucket):
    local_paths = prices.shape[1]
    slab_part = local_paths // 8
    path_count = float(local_paths * 16)
    slab = lax.axis_index(STOCK_AXES).astype(jnp.int32).reshape(1)

    pieces = jnp.moveaxis(prices.reshape(32, 8, slab_part), 1, 0)
    table = jnp.broadcast_to(jnp.pad(loadings, ((0, 0), (0, LANES - 32)))[None], (8, 32, LANES))
    moved_prices = lax.all_to_all(
        jnp.concatenate([pieces, table], axis=2), STOCK_AXES, 0, 0, tiled=True
    )
    stacked = jnp.concatenate([cotangent[None], shocks], axis=0)
    stacked = jnp.moveaxis(stacked.reshape(5, 32, 8, slab_part), 2, 0)
    stacked, moved_prices = lax.optimization_barrier((stacked, moved_prices))
    moved = lax.all_to_all(stacked, STOCK_AXES, 0, 0, tiled=True)

    basis, sums = regression_sums(
        slab, moved_prices, left_terms(basis_w, 0), basis_bias[:, None], payoff[None, :],
        in_fit[None, :], slab_part,
    )
    near, far = all_device_sum(sums)
    coefficients = solve_coefficients(near, far, path_count)
    delta, surface = date_loop(
        slab, coefficients, basis, moved, corr_gen, basket[:, None], exercise, bucket, slab_part
    )
    surface = lax.all_to_all(surface.reshape(128, 4, LANES), ALL_AXES, 0, 0, tiled=True)
    surface = jnp.sum(surface, axis=0).reshape(4, 4, 32)
    surface = jnp.transpose(surface, (2, 1, 0)).reshape(32, 16)
    delta = lax.all_to_all(delta, STOCK_AXES, 0, 0, tiled=True)
    delta = jnp.moveaxis(delta, 0, 1).reshape(32, local_paths).astype(f32)
    return delta, surface


def solution(mesh):
    fine = Mesh(mesh.devices.reshape(FINE), ALL_AXES)
    stocks, paths = STOCK_AXES, PATH_AXES
    return jax.shard_map(
        per_device,
        mesh=fine,
        in_specs=(
            P(stocks, paths),
            P(stocks, None),
            P(),
            P(),
            P(paths),
            P(paths),
            P(stocks, paths),
            P(None, stocks, paths),
            P(),
            P(),
            P(None, paths),
            P(None, paths),
        ),
        out_specs=(P(stocks, paths), P(stocks, paths)),
        check_vma=False,
    )
```

```python
import jax
import jax.numpy as jnp
from jax import lax
from jax.experimental import pallas as pl
from jax.experimental.pallas import tpu as pltpu
from jax.sharding import Mesh
from jax.sharding import PartitionSpec as P

NK = 256
STEPS = 4
TIME_STEP = 0.25
RIDGE = 0.1
LANES = 128
BLOCK = 128
TILE = 512
INCREMENT_TILE = 512
DATE_TILE = 1024
PATH_AXES = ("z", "ylo", "core")
STOCK_AXES = ("x", "yhi")
ALL_AXES = PATH_AXES + STOCK_AXES
FINE = (4, 2, 2, 4, 2)
f32 = jnp.float32
bf16 = jnp.bfloat16


def three_terms(x):
    high = x.astype(bf16)
    rest = x - high.astype(f32)
    middle = rest.astype(bf16)
    low = (rest - middle.astype(f32)).astype(bf16)
    return high, middle, low


def left_terms(x, axis):
    high, middle, low = three_terms(x)
    return jnp.concatenate([high, high, middle, high, low, middle], axis=axis)


def right_terms(x, axis):
    high, middle, low = three_terms(x)
    return jnp.concatenate([high, middle, high, low, high, middle], axis=axis)


def exact_dot(left, right):
    return jnp.dot(left_terms(left, 1), right_terms(right, 0), preferred_element_type=f32)


GRAM_BLOCKS = tuple((i, j) for i in range(4) for j in range(i + 1))
MOMENT_ROW = len(GRAM_BLOCKS) * BLOCK
SUM_ROWS = 1344
PIECE = SUM_ROWS // 8


def gram_kernel(slab_ref, moved_ref, table_ref, weight_ref, bias_ref, payoff_ref, fit_ref,
                basis_ref, sums_ref, gram_ref, moment_ref):
    step = pl.program_id(0)
    tile = moved_ref[...].reshape(256, TILE)
    loads = table_ref[...].reshape(256, LANES)[:, :32]
    factors = lax.dot_general(loads, tile, (((0,), (0,)), ((), ())), preferred_element_type=f32)
    raised = lax.dot_general(
        weight_ref[...], right_terms(factors, 0), (((0,), (0,)), ((), ())), preferred_element_type=f32
    )
    basis = jnp.tanh(raised + bias_ref[...]).astype(bf16)
    basis_ref[...] = basis
    picked = basis * fit_ref[...].astype(f32).astype(bf16)
    paid = jnp.broadcast_to(payoff_ref[...].astype(f32), (16, TILE)).astype(bf16)
    contract = (((1,), (1,)), ((), ()))
    first = lax.dot_general(picked[:256], basis[:256], contract, preferred_element_type=f32)
    second = lax.dot_general(picked[256:], basis, contract, preferred_element_type=f32)
    moment = lax.dot_general(paid, picked, contract, preferred_element_type=f32)

    @pl.when(step == 0)
    def _():
        gram_ref[:256, :256] = first
        gram_ref[256:, :] = second
        moment_ref[...] = moment

    @pl.when(step > 0)
    def _():
        gram_ref[:256, :256] += first
        gram_ref[256:, :] += second
        moment_ref[...] += moment

    @pl.when(step == pl.num_programs(0) - 1)
    def _():
        for at, (i, j) in enumerate(GRAM_BLOCKS):
            sums_ref[at * BLOCK:(at + 1) * BLOCK, :] = gram_ref[
                i * BLOCK:(i + 1) * BLOCK, j * BLOCK:(j + 1) * BLOCK
            ]
        sums_ref[MOMENT_ROW:, :] = jnp.zeros((SUM_ROWS - MOMENT_ROW, LANES), f32)
        for i in range(4):
            sums_ref[MOMENT_ROW + 8 * i:MOMENT_ROW + 8 * i + 8, :] = moment_ref[
                :8, i * BLOCK:(i + 1) * BLOCK
            ]


def regression_sums(slab, moved, weights, bias, payoff, fit, slab_part):
    tiles = slab_part // TILE
    table_at = slab_part // LANES

    def own(step, slab_ref):
        return (0, slab_ref[0] * tiles + step)

    return pl.pallas_call(
        gram_kernel,
        out_shape=(
            jax.ShapeDtypeStruct((512, slab_part), bf16),
            jax.ShapeDtypeStruct((SUM_ROWS, LANES), f32),
        ),
        grid_spec=pltpu.PrefetchScalarGridSpec(
            num_scalar_prefetch=1,
            grid=(tiles,),
            in_specs=[
                pl.BlockSpec((8, 32, TILE), lambda i, s: (0, 0, i)),
                pl.BlockSpec((8, 32, LANES), lambda i, s: (0, 0, table_at)),
                pl.BlockSpec((192, 512), lambda i, s: (0, 0)),
                pl.BlockSpec((512, 1), lambda i, s: (0, 0)),
                pl.BlockSpec((1, TILE), own),
                pl.BlockSpec((1, TILE), own),
            ],
            out_specs=(
                pl.BlockSpec((512, TILE), lambda i, s: (0, i)),
                pl.BlockSpec((SUM_ROWS, LANES), lambda i, s: (0, 0)),
            ),
            scratch_shapes=[pltpu.VMEM((512, 512), f32), pltpu.VMEM((16, 512), f32)],
        ),
        compiler_params=pltpu.CompilerParams(vmem_limit_bytes=40 << 20),
        name="regression_sums",
    )(slab, moved, moved, weights, bias, payoff, fit)


def exchange_with_others(x, axes, count, piece_of=None):
    received = []
    for flip in range(1, count):
        sent = x if piece_of is None else piece_of(flip)
        received.append(lax.ppermute(sent, axes, [(i, i ^ flip) for i in range(count)]))
    return received


def all_device_sum(sums, beside):
    core = lax.axis_index("core")
    z = lax.axis_index("z")
    halves = sums.reshape(2, 4, PIECE, LANES)
    mine = lax.dynamic_index_in_dim(halves, core, 0, False)
    other = lax.dynamic_index_in_dim(halves, 1 - core, 0, False)
    mine = mine + exchange_with_others(other, "core", 2)[0]

    def piece_of(flip):
        return lax.dynamic_index_in_dim(mine, z ^ flip, 0, False)

    share = piece_of(0)
    for part in exchange_with_others(None, "z", 4, piece_of):
        share = share + part
    share, beside = lax.optimization_barrier((share, beside))
    for axes in ("x", ("ylo", "yhi")):
        parts = exchange_with_others(share, axes, 4)
        share = (share + parts[0]) + (parts[1] + parts[2])
    return lax.optimization_barrier((share, beside))


def gathered_sum(share):
    column = jnp.stack([share] + exchange_with_others(share, "z", 4))
    return column, exchange_with_others(column, "core", 2)[0]


def lane_column(x, j):
    return jnp.broadcast_to(x[:, j:j + 1], (8, LANES))


def sublane_row(x, j):
    return jnp.broadcast_to(x[j:j + 1, :], (8, LANES))


def pivot_rows(panel, base, lane, sub):
    inside = (lane >= base) & (lane < base + 8)
    columns = [lane_column(panel, base + j) for j in range(8)]
    d = {(i, j): sublane_row(columns[j], i) for j in range(8) for i in range(j, 8)}
    marked = jnp.where(inside, jnp.where(lane - base == sub, 1.0, 0.0), panel)
    y = [sublane_row(marked, j) for j in range(8)]
    lower = {}
    inverse = []
    for j in range(8):
        inverse.append(1.0 / d[j, j])
        for i in range(j + 1, 8):
            lower[i, j] = d[i, j] * inverse[j]
        for k in range(j + 1, 8):
            for i in range(k, 8):
                d[i, k] = d[i, k] - lower[i, j] * d[k, j]
        for i in range(j + 1, 8):
            y[i] = y[i] - lower[i, j] * y[j]
    y = [y[j] * inverse[j] for j in range(8)]
    for j in range(7, -1, -1):
        for i in range(j):
            y[i] = y[i] - lower[j, i] * y[j]
    return y


def eliminated(x, rows, base, lane):
    inside = (lane >= base) & (lane < base + 8)
    t = [lane_column(x, base + j) * rows[j] for j in range(8)]
    total = ((t[0] + t[1]) + (t[2] + t[3])) + ((t[4] + t[5]) + (t[6] + t[7]))
    return jnp.where(inside, 0.0, x) - total


def inverse_of_block(rows):
    lane = lax.broadcasted_iota(jnp.int32, (8, LANES), 1)
    sub = lax.broadcasted_iota(jnp.int32, (8, LANES), 0)
    rows = list(rows)
    for g in range(16):
        pivots = pivot_rows(rows[g], 8 * g, lane, sub)
        for t in range(1, 16):
            h = (g + t) % 16
            rows[h] = eliminated(rows[h], pivots, 8 * g, lane)
        own = pivots[0]
        for j in range(1, 8):
            own = jnp.where(sub == j, pivots[j], own)
        rows[g] = own
    return rows


def solve_kernel(at_ref, near_ref, far_ref, basis_ref, out_ref, sums_ref, system_ref, *, scale):
    core = at_ref[0]
    z = at_ref[1]
    for flip in range(4):
        at = pl.multiple_of((core * 4 + (z ^ flip)) * PIECE, 8)
        sums_ref[pl.ds(at, PIECE), :] = near_ref[flip]
        at = pl.multiple_of(((1 - core) * 4 + (z ^ flip)) * PIECE, 8)
        sums_ref[pl.ds(at, PIECE), :] = far_ref[flip]
    diagonal = (
        lax.broadcasted_iota(jnp.int32, (BLOCK, BLOCK), 0)
        == lax.broadcasted_iota(jnp.int32, (BLOCK, BLOCK), 1)
    )
    for at, (i, j) in enumerate(GRAM_BLOCKS):
        block = sums_ref[at * BLOCK:(at + 1) * BLOCK, :] * scale
        if i == j:
            block = block + jnp.where(diagonal, RIDGE, 0.0)
        else:
            system_ref[j * BLOCK:(j + 1) * BLOCK, i * BLOCK:(i + 1) * BLOCK] = block.T
        system_ref[i * BLOCK:(i + 1) * BLOCK, j * BLOCK:(j + 1) * BLOCK] = block
    for i in range(4):
        row = sums_ref[MOMENT_ROW + 8 * i:MOMENT_ROW + 8 * i + 1, :] * scale
        system_ref[i * BLOCK:(i + 1) * BLOCK, 512:] = jnp.broadcast_to(row, (BLOCK, BLOCK)).T

    for i in range(4):
        lo = i * BLOCK
        inverse = inverse_of_block(
            [system_ref[lo + 8 * g:lo + 8 * g + 8, lo:lo + BLOCK] for g in range(16)]
        )
        inverse = jnp.concatenate(inverse, axis=0)
        solved = exact_dot(inverse, system_ref[lo:lo + BLOCK, lo + BLOCK:])
        for j in range(4):
            if j != i:
                system_ref[j * BLOCK:(j + 1) * BLOCK, lo + BLOCK:] -= exact_dot(
                    system_ref[j * BLOCK:(j + 1) * BLOCK, lo:lo + BLOCK], solved
                )
        system_ref[lo:lo + BLOCK, lo + BLOCK:] = solved
    width = basis_ref.shape[1]
    for lo in range(0, width, 512):
        parts = [jnp.zeros((8, 512), f32) for _ in range(4)]
        for b in range(64):
            coefficient = jnp.tile(system_ref[8 * b:8 * b + 8, 512:], (1, 4))
            parts[b % 4] += coefficient * basis_ref[8 * b:8 * b + 8, lo:lo + 512].astype(f32)
        out_ref[:, lo:lo + 512] = jnp.sum(
            (parts[0] + parts[1]) + (parts[2] + parts[3]), axis=0, keepdims=True
        )


def solve_continuation(near, far, basis, path_count):
    at = jnp.stack([lax.axis_index("core"), lax.axis_index("z")]).astype(jnp.int32)
    whole = pl.BlockSpec((4, PIECE, LANES), lambda i, s: (0, 0, 0))
    return pl.pallas_call(
        lambda *refs: solve_kernel(*refs, scale=1.0 / path_count),
        out_shape=jax.ShapeDtypeStruct((1, basis.shape[1]), f32),
        grid_spec=pltpu.PrefetchScalarGridSpec(
            num_scalar_prefetch=1,
            grid=(1,),
            in_specs=[whole, whole, pl.BlockSpec(basis.shape, lambda i, s: (0, 0))],
            out_specs=pl.BlockSpec((1, basis.shape[1]), lambda i, s: (0, 0)),
            scratch_shapes=[
                pltpu.VMEM((SUM_ROWS, LANES), f32),
                pltpu.VMEM((512, 512 + LANES), f32),
            ],
        ),
        compiler_params=pltpu.CompilerParams(vmem_limit_bytes=40 << 20),
        name="solve_continuation",
    )(at, near, far, basis)


def increments_kernel(moved_ref, mixer_ref, basket_ref, sent_ref, weights_ref):
    adjoint = moved_ref[...].reshape(256, INCREMENT_TILE).astype(f32)
    for date in range(STEPS - 1, -1, -1):
        gain = TIME_STEP * jnp.dot(mixer_ref[...], adjoint.astype(bf16), preferred_element_type=f32)
        sent_ref[:, date] = gain.astype(bf16).reshape(8, 32, INCREMENT_TILE)
        if date:
            adjoint = adjoint + gain

    @pl.when(pl.program_id(0) == 0)
    def _():
        lane = lax.broadcasted_iota(jnp.int32, (256, LANES), 1)
        weight = jnp.broadcast_to(basket_ref[...], (256, LANES))
        table = weight
        for later in range(1, STEPS):
            gain = sum(
                jnp.dot(mixer_ref[...], part, preferred_element_type=f32)
                for part in three_terms(weight)
            )
            weight = weight + TIME_STEP * gain
            table = jnp.where(lane == later, weight, table)
        weights_ref[...] = table


def increments(moved, mixer, basket, slab_part):
    return pl.pallas_call(
        increments_kernel,
        out_shape=(
            jax.ShapeDtypeStruct((8, STEPS, 32, slab_part), bf16),
            jax.ShapeDtypeStruct((256, LANES), f32),
        ),
        grid=(slab_part // INCREMENT_TILE,),
        in_specs=[
            pl.BlockSpec((8, 32, INCREMENT_TILE), lambda i: (0, 0, i)),
            pl.BlockSpec((256, 256), lambda i: (0, 0)),
            pl.BlockSpec((256, 1), lambda i: (0, 0)),
        ],
        out_specs=(
            pl.BlockSpec((8, STEPS, 32, INCREMENT_TILE), lambda i: (0, 0, 0, i)),
            pl.BlockSpec((256, LANES), lambda i: (0, 0)),
        ),
        compiler_params=pltpu.CompilerParams(vmem_limit_bytes=40 << 20),
        name="increments",
    )(moved, mixer, basket)


def surface_kernel(slab_ref, *refs):
    continuation_refs = refs[:8]
    (cotangent_ref, gain_ref, shock_ref, weight_ref, exercise_ref, bucket_ref, delta_ref, share_ref,
     continuation_ref, total_ref) = refs[8:]
    step = pl.program_id(0)

    @pl.when(step == 0)
    def _():
        for flip in range(8):
            at = slab_ref[0] ^ flip
            for part in range(2):
                continuation_ref[pl.ds(2 * at + part, 1), :] = continuation_refs[flip][
                    :, part * DATE_TILE:(part + 1) * DATE_TILE
                ]
        total_ref[...] = jnp.zeros(total_ref.shape, f32)

    continuation = continuation_ref[pl.ds(step, 1), :]
    held = [exercise_ref[date:date + 1, :].astype(f32) * continuation for date in range(STEPS)]
    weights = [weight_ref[:, later:later + 1] for later in range(STEPS)]
    strikes = lax.broadcasted_iota(jnp.int32, (NK, DATE_TILE), 0)
    base = cotangent_ref[...].astype(f32)
    total = total_ref[...]
    for date in range(STEPS - 1, -1, -1):
        base = base + gain_ref[0, date].astype(f32)
        adjoint = base
        for later in range(STEPS - date):
            adjoint = adjoint + held[date + later] * weights[later]
        terms = (adjoint * shock_ref[date].astype(f32)).astype(bf16)
        chosen = jnp.where(strikes == bucket_ref[date:date + 1, :], 1.0, 0.0).astype(bf16)
        total = total + lax.dot_general(
            chosen, terms, (((1,), (1,)), ((), ())), preferred_element_type=f32
        )
    delta_ref[...] = adjoint
    total_ref[...] = total

    @pl.when(step == pl.num_programs(0) - 1)
    def _():
        grouped = total.reshape(16, 16, 32)
        for q in range(4):
            share_ref[:, :, 32 * q:32 * q + 32] = grouped[:, 4 * q:4 * q + 4, :]


def surface_and_delta(slab, continuations, cotangent, gains, shocks, weights, exercise, bucket):
    local_paths = cotangent.shape[1]
    whole = pl.BlockSpec((1, local_paths // 8), lambda i, s: (0, 0))
    return pl.pallas_call(
        surface_kernel,
        out_shape=(
            jax.ShapeDtypeStruct((32, local_paths), f32),
            jax.ShapeDtypeStruct((16, 4, LANES), f32),
        ),
        grid_spec=pltpu.PrefetchScalarGridSpec(
            num_scalar_prefetch=1,
            grid=(local_paths // DATE_TILE,),
            in_specs=[whole] * 8 + [
                pl.BlockSpec((32, DATE_TILE), lambda i, s: (0, i)),
                pl.BlockSpec((1, STEPS, 32, DATE_TILE), lambda i, s: (i // 2, 0, 0, i % 2)),
                pl.BlockSpec((STEPS, 32, DATE_TILE), lambda i, s: (0, 0, i)),
                pl.BlockSpec((32, LANES), lambda i, s: (s[0], 0)),
                pl.BlockSpec((STEPS, DATE_TILE), lambda i, s: (0, i)),
                pl.BlockSpec((STEPS, DATE_TILE), lambda i, s: (0, i)),
            ],
            out_specs=(
                pl.BlockSpec((32, DATE_TILE), lambda i, s: (0, i)),
                pl.BlockSpec((16, 4, LANES), lambda i, s: (0, 0, 0)),
            ),
            scratch_shapes=[pltpu.VMEM((16, DATE_TILE), f32), pltpu.VMEM((NK, 32), f32)],
        ),
        compiler_params=pltpu.CompilerParams(vmem_limit_bytes=48 << 20),
        name="surface_and_delta",
    )(slab, *continuations, cotangent, gains, shocks, weights, exercise, bucket)


def per_device(prices, loadings, basis_w, basis_bias, payoff, in_fit, cotangent, shocks, corr_gen,
               basket, exercise, bucket):
    local_paths = prices.shape[1]
    slab_part = local_paths // 8
    path_count = float(local_paths * 16)
    slab = lax.axis_index(STOCK_AXES).astype(jnp.int32).reshape(1)

    pieces = jnp.moveaxis(prices.reshape(32, 8, slab_part), 1, 0)
    table = jnp.broadcast_to(jnp.pad(loadings, ((0, 0), (0, LANES - 32)))[None], (8, 32, LANES))
    moved_prices = lax.all_to_all(
        jnp.concatenate([pieces, table], axis=2), STOCK_AXES, 0, 0, tiled=True
    )
    slabs = jnp.moveaxis(cotangent.reshape(32, 8, slab_part), 1, 0)
    slabs, moved_prices = lax.optimization_barrier((slabs, moved_prices))
    moved = lax.all_to_all(slabs, STOCK_AXES, 0, 0, tiled=True)
    basis, sums = regression_sums(
        slab, moved_prices, left_terms(basis_w, 0), basis_bias[:, None], payoff[None, :],
        in_fit[None, :], slab_part,
    )
    sent, weights = increments(moved, corr_gen, basket[:, None], slab_part)
    share, sent = all_device_sum(sums, sent)
    gains = lax.all_to_all(sent, STOCK_AXES, 0, 0, tiled=True)
    near, far = gathered_sum(share)
    continuation = solve_continuation(near, far, basis, path_count)
    continuations = [continuation] + exchange_with_others(continuation, STOCK_AXES, 8)
    delta, surface = surface_and_delta(
        slab, continuations, cotangent, gains, shocks, weights, exercise, bucket
    )
    surface = lax.all_to_all(surface, PATH_AXES, 0, 0, tiled=True)
    surface = jnp.sum(surface, axis=0).reshape(4, 4, 32)
    surface = jnp.transpose(surface, (2, 1, 0)).reshape(32, 16)
    return delta, surface


def solution(mesh):
    fine = Mesh(mesh.devices.reshape(FINE), ALL_AXES)
    stocks, paths = STOCK_AXES, PATH_AXES
    return jax.shard_map(
        per_device,
        mesh=fine,
        in_specs=(
            P(stocks, paths),
            P(stocks, None),
            P(),
            P(),
            P(paths),
            P(paths),
            P(stocks, paths),
            P(None, stocks, paths),
            P(),
            P(),
            P(None, paths),
            P(None, paths),
        ),
        out_specs=(P(stocks, paths), P(stocks, paths)),
        check_vma=False,
    )
```

```python
import jax
import jax.numpy as jnp
from jax import lax
from jax.experimental import pallas as pl
from jax.experimental.pallas import tpu as pltpu
from jax.sharding import Mesh
from jax.sharding import PartitionSpec as P

NK = 256
STEPS = 4
TIME_STEP = 0.25
RIDGE = 0.1
LANES = 128
BLOCK = 128
TILE = 512
INCREMENT_TILE = 512
DATE_TILE = 2048
PATH_AXES = ("z", "ylo", "core")
STOCK_AXES = ("x", "yhi")
ALL_AXES = PATH_AXES + STOCK_AXES
FINE = (4, 2, 2, 4, 2)
f32 = jnp.float32
bf16 = jnp.bfloat16


def three_terms(x):
    high = x.astype(bf16)
    rest = x - high.astype(f32)
    middle = rest.astype(bf16)
    low = (rest - middle.astype(f32)).astype(bf16)
    return high, middle, low


def left_terms(x, axis):
    high, middle, low = three_terms(x)
    return jnp.concatenate([high, high, middle, high, low, middle], axis=axis)


def right_terms(x, axis):
    high, middle, low = three_terms(x)
    return jnp.concatenate([high, middle, high, low, high, middle], axis=axis)


def exact_dot(left, right):
    return jnp.dot(left_terms(left, 1), right_terms(right, 0), preferred_element_type=f32)


GRAM_BLOCKS = tuple((i, j) for i in range(4) for j in range(i + 1))
MOMENT_ROW = len(GRAM_BLOCKS) * BLOCK
SUM_ROWS = 1344
PIECE = SUM_ROWS // 8


def gram_kernel(slab_ref, moved_ref, table_ref, weight_ref, bias_ref, payoff_ref, fit_ref,
                basis_ref, sums_ref, gram_ref, moment_ref):
    step = pl.program_id(0)
    tile = moved_ref[...].reshape(256, TILE)
    loads = table_ref[...].reshape(256, LANES)[:, :32]
    factors = lax.dot_general(loads, tile, (((0,), (0,)), ((), ())), preferred_element_type=f32)
    raised = lax.dot_general(
        weight_ref[...], right_terms(factors, 0), (((0,), (0,)), ((), ())), preferred_element_type=f32
    )
    basis = jnp.tanh(raised + bias_ref[...]).astype(bf16)
    basis_ref[...] = basis
    picked = basis * fit_ref[...].astype(f32).astype(bf16)
    paid = jnp.broadcast_to(payoff_ref[...].astype(f32), (16, TILE)).astype(bf16)
    contract = (((1,), (1,)), ((), ()))
    first = lax.dot_general(picked[:256], basis[:256], contract, preferred_element_type=f32)
    second = lax.dot_general(picked[256:], basis, contract, preferred_element_type=f32)
    moment = lax.dot_general(paid, picked, contract, preferred_element_type=f32)

    @pl.when(step == 0)
    def _():
        gram_ref[:256, :256] = first
        gram_ref[256:, :] = second
        moment_ref[...] = moment

    @pl.when(step > 0)
    def _():
        gram_ref[:256, :256] += first
        gram_ref[256:, :] += second
        moment_ref[...] += moment

    @pl.when(step == pl.num_programs(0) - 1)
    def _():
        for at, (i, j) in enumerate(GRAM_BLOCKS):
            sums_ref[at * BLOCK:(at + 1) * BLOCK, :] = gram_ref[
                i * BLOCK:(i + 1) * BLOCK, j * BLOCK:(j + 1) * BLOCK
            ]
        sums_ref[MOMENT_ROW:, :] = jnp.zeros((SUM_ROWS - MOMENT_ROW, LANES), f32)
        for i in range(4):
            sums_ref[MOMENT_ROW + 8 * i:MOMENT_ROW + 8 * i + 8, :] = moment_ref[
                :8, i * BLOCK:(i + 1) * BLOCK
            ]


def regression_sums(slab, moved, weights, bias, payoff, fit, slab_part):
    tiles = slab_part // TILE
    table_at = slab_part // LANES

    def own(step, slab_ref):
        return (0, slab_ref[0] * tiles + step)

    return pl.pallas_call(
        gram_kernel,
        out_shape=(
            jax.ShapeDtypeStruct((512, slab_part), bf16),
            jax.ShapeDtypeStruct((SUM_ROWS, LANES), f32),
        ),
        grid_spec=pltpu.PrefetchScalarGridSpec(
            num_scalar_prefetch=1,
            grid=(tiles,),
            in_specs=[
                pl.BlockSpec((8, 32, TILE), lambda i, s: (0, 0, i)),
                pl.BlockSpec((8, 32, LANES), lambda i, s: (0, 0, table_at)),
                pl.BlockSpec((192, 512), lambda i, s: (0, 0)),
                pl.BlockSpec((512, 1), lambda i, s: (0, 0)),
                pl.BlockSpec((1, TILE), own),
                pl.BlockSpec((1, TILE), own),
            ],
            out_specs=(
                pl.BlockSpec((512, TILE), lambda i, s: (0, i)),
                pl.BlockSpec((SUM_ROWS, LANES), lambda i, s: (0, 0)),
            ),
            scratch_shapes=[pltpu.VMEM((512, 512), f32), pltpu.VMEM((16, 512), f32)],
        ),
        compiler_params=pltpu.CompilerParams(vmem_limit_bytes=40 << 20),
        name="regression_sums",
    )(slab, moved, moved, weights, bias, payoff, fit)


def exchange_with_others(x, axes, count, piece_of=None):
    received = []
    for flip in range(1, count):
        sent = x if piece_of is None else piece_of(flip)
        received.append(lax.ppermute(sent, axes, [(i, i ^ flip) for i in range(count)]))
    return received


def all_device_sum(sums, beside):
    core = lax.axis_index("core")
    z = lax.axis_index("z")
    halves = sums.reshape(2, 4, PIECE, LANES)
    mine = lax.dynamic_index_in_dim(halves, core, 0, False)
    other = lax.dynamic_index_in_dim(halves, 1 - core, 0, False)
    mine = mine + exchange_with_others(other, "core", 2)[0]

    def piece_of(flip):
        return lax.dynamic_index_in_dim(mine, z ^ flip, 0, False)

    parts, beside = lax.optimization_barrier((exchange_with_others(None, "z", 4, piece_of), beside))
    share = (piece_of(0) + parts[0]) + (parts[1] + parts[2])
    parts = exchange_with_others(share, "x", 4)
    share = (share + parts[0]) + (parts[1] + parts[2])
    parts = exchange_with_others(share, ("ylo", "yhi"), 4)
    parts, beside = lax.optimization_barrier((parts, beside))
    return (share + parts[0]) + (parts[1] + parts[2]), beside


def gathered_sum(share):
    column = jnp.stack([share] + exchange_with_others(share, "z", 4))
    return column, exchange_with_others(column, "core", 2)[0]


def lane_column(x, j):
    return jnp.broadcast_to(x[:, j:j + 1], (8, LANES))


def sublane_row(x, j):
    return jnp.broadcast_to(x[j:j + 1, :], (8, LANES))


def pivot_rows(panel, base, lane, sub):
    inside = (lane >= base) & (lane < base + 8)
    columns = [lane_column(panel, base + j) for j in range(8)]
    d = {(i, j): sublane_row(columns[j], i) for j in range(8) for i in range(j, 8)}
    marked = jnp.where(inside, jnp.where(lane - base == sub, 1.0, 0.0), panel)
    y = [sublane_row(marked, j) for j in range(8)]
    lower = {}
    inverse = []
    for j in range(8):
        inverse.append(1.0 / d[j, j])
        for i in range(j + 1, 8):
            lower[i, j] = d[i, j] * inverse[j]
        for k in range(j + 1, 8):
            for i in range(k, 8):
                d[i, k] = d[i, k] - lower[i, j] * d[k, j]
        for i in range(j + 1, 8):
            y[i] = y[i] - lower[i, j] * y[j]
    y = [y[j] * inverse[j] for j in range(8)]
    for j in range(7, -1, -1):
        for i in range(j):
            y[i] = y[i] - lower[j, i] * y[j]
    return y


def eliminated(x, rows, base, lane):
    inside = (lane >= base) & (lane < base + 8)
    t = [lane_column(x, base + j) * rows[j] for j in range(8)]
    total = ((t[0] + t[1]) + (t[2] + t[3])) + ((t[4] + t[5]) + (t[6] + t[7]))
    return jnp.where(inside, 0.0, x) - total


def inverse_of_block(rows):
    lane = lax.broadcasted_iota(jnp.int32, (8, LANES), 1)
    sub = lax.broadcasted_iota(jnp.int32, (8, LANES), 0)
    rows = list(rows)
    for g in range(16):
        pivots = pivot_rows(rows[g], 8 * g, lane, sub)
        for t in range(1, 16):
            h = (g + t) % 16
            rows[h] = eliminated(rows[h], pivots, 8 * g, lane)
        own = pivots[0]
        for j in range(1, 8):
            own = jnp.where(sub == j, pivots[j], own)
        rows[g] = own
    return rows


def solve_kernel(at_ref, near_ref, far_ref, basis_ref, out_ref, sums_ref, system_ref, *, scale):
    core = at_ref[0]
    z = at_ref[1]
    for flip in range(4):
        at = pl.multiple_of((core * 4 + (z ^ flip)) * PIECE, 8)
        sums_ref[pl.ds(at, PIECE), :] = near_ref[flip]
        at = pl.multiple_of(((1 - core) * 4 + (z ^ flip)) * PIECE, 8)
        sums_ref[pl.ds(at, PIECE), :] = far_ref[flip]
    diagonal = (
        lax.broadcasted_iota(jnp.int32, (BLOCK, BLOCK), 0)
        == lax.broadcasted_iota(jnp.int32, (BLOCK, BLOCK), 1)
    )
    for at, (i, j) in enumerate(GRAM_BLOCKS):
        block = sums_ref[at * BLOCK:(at + 1) * BLOCK, :] * scale
        if i == j:
            block = block + jnp.where(diagonal, RIDGE, 0.0)
        else:
            system_ref[j * BLOCK:(j + 1) * BLOCK, i * BLOCK:(i + 1) * BLOCK] = block.T
        system_ref[i * BLOCK:(i + 1) * BLOCK, j * BLOCK:(j + 1) * BLOCK] = block
    for i in range(4):
        row = sums_ref[MOMENT_ROW + 8 * i:MOMENT_ROW + 8 * i + 1, :] * scale
        system_ref[i * BLOCK:(i + 1) * BLOCK, 512:] = jnp.broadcast_to(row, (BLOCK, BLOCK)).T

    for i in range(4):
        lo = i * BLOCK
        inverse = inverse_of_block(
            [system_ref[lo + 8 * g:lo + 8 * g + 8, lo:lo + BLOCK] for g in range(16)]
        )
        inverse = jnp.concatenate(inverse, axis=0)
        solved = exact_dot(inverse, system_ref[lo:lo + BLOCK, lo + BLOCK:])
        for j in range(4):
            if j != i:
                system_ref[j * BLOCK:(j + 1) * BLOCK, lo + BLOCK:] -= exact_dot(
                    system_ref[j * BLOCK:(j + 1) * BLOCK, lo:lo + BLOCK], solved
                )
        system_ref[lo:lo + BLOCK, lo + BLOCK:] = solved
    width = basis_ref.shape[1]
    for lo in range(0, width, 512):
        parts = [jnp.zeros((8, 512), f32) for _ in range(4)]
        for b in range(64):
            coefficient = jnp.tile(system_ref[8 * b:8 * b + 8, 512:], (1, 4))
            parts[b % 4] += coefficient * basis_ref[8 * b:8 * b + 8, lo:lo + 512].astype(f32)
        out_ref[:, lo:lo + 512] = jnp.sum(
            (parts[0] + parts[1]) + (parts[2] + parts[3]), axis=0, keepdims=True
        )


def solve_continuation(near, far, basis, path_count):
    at = jnp.stack([lax.axis_index("core"), lax.axis_index("z")]).astype(jnp.int32)
    whole = pl.BlockSpec((4, PIECE, LANES), lambda i, s: (0, 0, 0))
    return pl.pallas_call(
        lambda *refs: solve_kernel(*refs, scale=1.0 / path_count),
        out_shape=jax.ShapeDtypeStruct((1, basis.shape[1]), f32),
        grid_spec=pltpu.PrefetchScalarGridSpec(
            num_scalar_prefetch=1,
            grid=(1,),
            in_specs=[whole, whole, pl.BlockSpec(basis.shape, lambda i, s: (0, 0))],
            out_specs=pl.BlockSpec((1, basis.shape[1]), lambda i, s: (0, 0)),
            scratch_shapes=[
                pltpu.VMEM((SUM_ROWS, LANES), f32),
                pltpu.VMEM((512, 512 + LANES), f32),
            ],
        ),
        compiler_params=pltpu.CompilerParams(vmem_limit_bytes=40 << 20),
        name="solve_continuation",
    )(at, near, far, basis)


def increments_kernel(moved_ref, mixer_ref, basket_ref, sent_ref, weights_ref):
    adjoint = moved_ref[...].reshape(256, INCREMENT_TILE).astype(f32)
    for date in range(STEPS - 1, -1, -1):
        gain = TIME_STEP * jnp.dot(mixer_ref[...], adjoint.astype(bf16), preferred_element_type=f32)
        sent_ref[:, date] = gain.astype(bf16).reshape(8, 32, INCREMENT_TILE)
        if date:
            adjoint = adjoint + gain

    @pl.when(pl.program_id(0) == 0)
    def _():
        lane = lax.broadcasted_iota(jnp.int32, (256, LANES), 1)
        weight = jnp.broadcast_to(basket_ref[...], (256, LANES))
        table = weight
        for later in range(1, STEPS):
            gain = sum(
                jnp.dot(mixer_ref[...], part, preferred_element_type=f32)
                for part in three_terms(weight)
            )
            weight = weight + TIME_STEP * gain
            table = jnp.where(lane == later, weight, table)
        weights_ref[...] = table


def increments(moved, mixer, basket, slab_part):
    return pl.pallas_call(
        increments_kernel,
        out_shape=(
            jax.ShapeDtypeStruct((8, STEPS, 32, slab_part), bf16),
            jax.ShapeDtypeStruct((256, LANES), f32),
        ),
        grid=(slab_part // INCREMENT_TILE,),
        in_specs=[
            pl.BlockSpec((8, 32, INCREMENT_TILE), lambda i: (0, 0, i)),
            pl.BlockSpec((256, 256), lambda i: (0, 0)),
            pl.BlockSpec((256, 1), lambda i: (0, 0)),
        ],
        out_specs=(
            pl.BlockSpec((8, STEPS, 32, INCREMENT_TILE), lambda i: (0, 0, 0, i)),
            pl.BlockSpec((256, LANES), lambda i: (0, 0)),
        ),
        compiler_params=pltpu.CompilerParams(vmem_limit_bytes=40 << 20),
        name="increments",
    )(moved, mixer, basket)


def surface_kernel(slab_ref, *refs):
    continuation_refs = refs[:4]
    (cotangent_ref, gain_ref, shock_ref, weight_ref, exercise_ref, bucket_ref, delta_ref, share_ref,
     continuation_ref, total_ref) = refs[4:]
    step = pl.program_id(0)

    @pl.when(step == 0)
    def _():
        for flip in range(8):
            continuation_ref[pl.ds(slab_ref[0] ^ flip, 1), :] = continuation_refs[flip // 2][
                flip % 2:flip % 2 + 1, :
            ]
        total_ref[...] = jnp.zeros(total_ref.shape, f32)

    continuation = continuation_ref[pl.ds(step, 1), :]
    held = [exercise_ref[date:date + 1, :].astype(f32) * continuation for date in range(STEPS)]
    weights = [weight_ref[:, later:later + 1] for later in range(STEPS)]
    strikes = lax.broadcasted_iota(jnp.int32, (NK, DATE_TILE), 0)
    base = cotangent_ref[...].astype(f32)
    total = total_ref[...]
    for date in range(STEPS - 1, -1, -1):
        base = base + gain_ref[0, date].astype(f32)
        adjoint = base
        for later in range(STEPS - date):
            adjoint = adjoint + held[date + later] * weights[later]
        terms = (adjoint * shock_ref[date].astype(f32)).astype(bf16)
        chosen = jnp.where(strikes == bucket_ref[date:date + 1, :], 1.0, 0.0).astype(bf16)
        total = total + lax.dot_general(
            chosen, terms, (((1,), (1,)), ((), ())), preferred_element_type=f32
        )
    delta_ref[...] = adjoint
    total_ref[...] = total

    @pl.when(step == pl.num_programs(0) - 1)
    def _():
        grouped = total.reshape(16, 16, 32)
        for q in range(4):
            share_ref[:, :, 32 * q:32 * q + 32] = grouped[:, 4 * q:4 * q + 4, :]


def surface_and_delta(slab, continuations, cotangent, gains, shocks, weights, exercise, bucket):
    local_paths = cotangent.shape[1]
    whole = pl.BlockSpec((2, DATE_TILE), lambda i, s: (0, 0))
    return pl.pallas_call(
        surface_kernel,
        out_shape=(
            jax.ShapeDtypeStruct((32, local_paths), f32),
            jax.ShapeDtypeStruct((16, 4, LANES), f32),
        ),
        grid_spec=pltpu.PrefetchScalarGridSpec(
            num_scalar_prefetch=1,
            grid=(local_paths // DATE_TILE,),
            in_specs=[whole] * 4 + [
                pl.BlockSpec((32, DATE_TILE), lambda i, s: (0, i)),
                pl.BlockSpec((1, STEPS, 32, DATE_TILE), lambda i, s: (i, 0, 0, 0)),
                pl.BlockSpec((STEPS, 32, DATE_TILE), lambda i, s: (0, 0, i)),
                pl.BlockSpec((32, LANES), lambda i, s: (s[0], 0)),
                pl.BlockSpec((STEPS, DATE_TILE), lambda i, s: (0, i)),
                pl.BlockSpec((STEPS, DATE_TILE), lambda i, s: (0, i)),
            ],
            out_specs=(
                pl.BlockSpec((32, DATE_TILE), lambda i, s: (0, i)),
                pl.BlockSpec((16, 4, LANES), lambda i, s: (0, 0, 0)),
            ),
            scratch_shapes=[pltpu.VMEM((8, DATE_TILE), f32), pltpu.VMEM((NK, 32), f32)],
        ),
        compiler_params=pltpu.CompilerParams(vmem_limit_bytes=48 << 20),
        name="surface_and_delta",
    )(slab, *continuations, cotangent, gains, shocks, weights, exercise, bucket)


def per_device(prices, loadings, basis_w, basis_bias, payoff, in_fit, cotangent, shocks, corr_gen,
               basket, exercise, bucket):
    local_paths = prices.shape[1]
    slab_part = local_paths // 8
    path_count = float(local_paths * 16)
    slab = lax.axis_index(STOCK_AXES).astype(jnp.int32).reshape(1)

    pieces = jnp.moveaxis(prices.reshape(32, 8, slab_part), 1, 0)
    table = jnp.broadcast_to(jnp.pad(loadings, ((0, 0), (0, LANES - 32)))[None], (8, 32, LANES))
    moved_prices = lax.all_to_all(
        jnp.concatenate([pieces, table], axis=2), STOCK_AXES, 0, 0, tiled=True
    )
    slabs = jnp.moveaxis(cotangent.reshape(32, 8, slab_part), 1, 0)
    slabs, moved_prices = lax.optimization_barrier((slabs, moved_prices))
    moved = lax.all_to_all(slabs, STOCK_AXES, 0, 0, tiled=True)
    basis, sums = regression_sums(
        slab, moved_prices, left_terms(basis_w, 0), basis_bias[:, None], payoff[None, :],
        in_fit[None, :], slab_part,
    )
    sent, weights = increments(moved, corr_gen, basket[:, None], slab_part)
    share, sent = all_device_sum(sums, sent)
    gains = lax.all_to_all(sent, STOCK_AXES, 0, 0, tiled=True)
    near, far = gathered_sum(share)
    continuation = solve_continuation(near, far, basis, path_count)
    pair = jnp.concatenate([continuation] + exchange_with_others(continuation, "yhi", 2), axis=0)
    continuations = [pair] + exchange_with_others(pair, "x", 4)
    delta, surface = surface_and_delta(
        slab, continuations, cotangent, gains, shocks, weights, exercise, bucket
    )
    surface = lax.all_to_all(surface, PATH_AXES, 0, 0, tiled=True)
    surface = jnp.sum(surface, axis=0).reshape(4, 4, 32)
    surface = jnp.transpose(surface, (2, 1, 0)).reshape(32, 16)
    return delta, surface


def solution(mesh):
    fine = Mesh(mesh.devices.reshape(FINE), ALL_AXES)
    stocks, paths = STOCK_AXES, PATH_AXES
    return jax.shard_map(
        per_device,
        mesh=fine,
        in_specs=(
            P(stocks, paths),
            P(stocks, None),
            P(),
            P(),
            P(paths),
            P(paths),
            P(stocks, paths),
            P(None, stocks, paths),
            P(),
            P(),
            P(None, paths),
            P(None, paths),
        ),
        out_specs=(P(stocks, paths), P(stocks, paths)),
        check_vma=False,
    )
```

```python
import jax
import jax.numpy as jnp
from jax import lax
from jax.experimental import pallas as pl
from jax.experimental.pallas import tpu as pltpu
from jax.sharding import Mesh
from jax.sharding import PartitionSpec as P

NK = 256
STEPS = 4
TIME_STEP = 0.25
RIDGE = 0.1
LANES = 128
BLOCK = 128
TILE = 512
INCREMENT_TILE = 512
DATE_TILE = 2048
STRIKE_BITS = 7
STRIKE_ROWS = 1 << STRIKE_BITS
PATH_AXES = ("z", "ylo", "core")
STOCK_AXES = ("x", "yhi")
ALL_AXES = PATH_AXES + STOCK_AXES
FINE = (4, 2, 2, 4, 2)
f32 = jnp.float32
bf16 = jnp.bfloat16


def three_terms(x):
    high = x.astype(bf16)
    rest = x - high.astype(f32)
    middle = rest.astype(bf16)
    low = (rest - middle.astype(f32)).astype(bf16)
    return high, middle, low


def left_terms(x, axis):
    high, middle, low = three_terms(x)
    return jnp.concatenate([high, high, middle, high, low, middle], axis=axis)


def right_terms(x, axis):
    high, middle, low = three_terms(x)
    return jnp.concatenate([high, middle, high, low, high, middle], axis=axis)


def exact_dot(left, right):
    return jnp.dot(left_terms(left, 1), right_terms(right, 0), preferred_element_type=f32)


GRAM_BLOCKS = tuple((i, j) for i in range(4) for j in range(i + 1))
MOMENT_ROW = len(GRAM_BLOCKS) * BLOCK
SUM_ROWS = 1344
PIECE = SUM_ROWS // 8


def gram_kernel(slab_ref, moved_ref, table_ref, weight_ref, bias_ref, payoff_ref, fit_ref,
                basis_ref, kept_ref, sent_ref, gram_ref, moment_ref, sums_ref):
    step = pl.program_id(0)
    tile = moved_ref[...].reshape(256, TILE)
    loads = table_ref[...].reshape(256, LANES)[:, :32]
    factors = lax.dot_general(loads, tile, (((0,), (0,)), ((), ())), preferred_element_type=f32)
    raised = lax.dot_general(
        weight_ref[...], right_terms(factors, 0), (((0,), (0,)), ((), ())), preferred_element_type=f32
    )
    basis = jnp.tanh(raised + bias_ref[...]).astype(bf16)
    basis_ref[...] = basis
    picked = basis * fit_ref[...].astype(f32).astype(bf16)
    paid = jnp.broadcast_to(payoff_ref[...].astype(f32), (16, TILE)).astype(bf16)
    contract = (((1,), (1,)), ((), ()))
    first = lax.dot_general(picked[:256], basis[:256], contract, preferred_element_type=f32)
    second = lax.dot_general(picked[256:], basis, contract, preferred_element_type=f32)
    moment = lax.dot_general(paid, picked, contract, preferred_element_type=f32)

    @pl.when(step == 0)
    def _():
        gram_ref[:256, :256] = first
        gram_ref[256:, :] = second
        moment_ref[...] = moment

    @pl.when(step > 0)
    def _():
        gram_ref[:256, :256] += first
        gram_ref[256:, :] += second
        moment_ref[...] += moment

    @pl.when(step == pl.num_programs(0) - 1)
    def _():
        for at, (i, j) in enumerate(GRAM_BLOCKS):
            sums_ref[at * BLOCK:(at + 1) * BLOCK, :] = gram_ref[
                i * BLOCK:(i + 1) * BLOCK, j * BLOCK:(j + 1) * BLOCK
            ]
        sums_ref[MOMENT_ROW:, :] = jnp.zeros((SUM_ROWS - MOMENT_ROW, LANES), f32)
        for i in range(4):
            sums_ref[MOMENT_ROW + 8 * i:MOMENT_ROW + 8 * i + 8, :] = moment_ref[
                :8, i * BLOCK:(i + 1) * BLOCK
            ]
        half = 4 * PIECE
        kept_ref[...] = sums_ref[pl.ds(pl.multiple_of(slab_ref[1] * half, 8), half), :]
        sent_ref[...] = sums_ref[pl.ds(pl.multiple_of((1 - slab_ref[1]) * half, 8), half), :]


def regression_sums(slab, moved, weights, bias, payoff, fit, slab_part):
    tiles = slab_part // TILE
    table_at = slab_part // LANES

    def own(step, slab_ref):
        return (0, slab_ref[0] * tiles + step)

    return pl.pallas_call(
        gram_kernel,
        out_shape=(
            jax.ShapeDtypeStruct((512, slab_part), bf16),
            jax.ShapeDtypeStruct((SUM_ROWS // 2, LANES), f32),
            jax.ShapeDtypeStruct((SUM_ROWS // 2, LANES), f32),
        ),
        grid_spec=pltpu.PrefetchScalarGridSpec(
            num_scalar_prefetch=1,
            grid=(tiles,),
            in_specs=[
                pl.BlockSpec((8, 32, TILE), lambda i, s: (0, 0, i)),
                pl.BlockSpec((8, 32, LANES), lambda i, s: (0, 0, table_at)),
                pl.BlockSpec((192, 512), lambda i, s: (0, 0)),
                pl.BlockSpec((512, 1), lambda i, s: (0, 0)),
                pl.BlockSpec((1, TILE), own),
                pl.BlockSpec((1, TILE), own),
            ],
            out_specs=(
                pl.BlockSpec((512, TILE), lambda i, s: (0, i)),
                pl.BlockSpec((SUM_ROWS // 2, LANES), lambda i, s: (0, 0)),
                pl.BlockSpec((SUM_ROWS // 2, LANES), lambda i, s: (0, 0)),
            ),
            scratch_shapes=[
                pltpu.VMEM((512, 512), f32),
                pltpu.VMEM((16, 512), f32),
                pltpu.VMEM((SUM_ROWS, LANES), f32),
            ],
        ),
        compiler_params=pltpu.CompilerParams(vmem_limit_bytes=40 << 20),
        name="regression_sums",
    )(slab, moved, moved, weights, bias, payoff, fit)


def exchange_with_others(x, axes, count, piece_of=None):
    received = []
    for flip in range(1, count):
        sent = x if piece_of is None else piece_of(flip)
        received.append(lax.ppermute(sent, axes, [(i, i ^ flip) for i in range(count)]))
    return received


def sum_over_cores_and_z(kept, sent, beside):
    z = lax.axis_index("z")
    mine = (kept + exchange_with_others(sent, "core", 2)[0]).reshape(4, PIECE, LANES)

    def piece_of(flip):
        return lax.dynamic_index_in_dim(mine, z ^ flip, 0, False)

    parts, beside = lax.optimization_barrier((exchange_with_others(None, "z", 4, piece_of), beside))
    return (piece_of(0) + parts[0]) + (parts[1] + parts[2]), beside


def sum_over_others(share, axes, beside):
    parts, beside = lax.optimization_barrier((exchange_with_others(share, axes, 4), beside))
    return (share + parts[0]) + (parts[1] + parts[2]), beside


def gathered_sum(share):
    column = jnp.stack([share] + exchange_with_others(share, "z", 4))
    return column, exchange_with_others(column, "core", 2)[0]


def lane_column(x, j):
    return jnp.broadcast_to(x[:, j:j + 1], (8, LANES))


def sublane_row(x, j):
    return jnp.broadcast_to(x[j:j + 1, :], (8, LANES))


def pivot_rows(panel, base, lane, sub):
    inside = (lane >= base) & (lane < base + 8)
    columns = [lane_column(panel, base + j) for j in range(8)]
    d = {(i, j): sublane_row(columns[j], i) for j in range(8) for i in range(j, 8)}
    marked = jnp.where(inside, jnp.where(lane - base == sub, 1.0, 0.0), panel)
    y = [sublane_row(marked, j) for j in range(8)]
    lower = {}
    inverse = []
    for j in range(8):
        inverse.append(1.0 / d[j, j])
        for i in range(j + 1, 8):
            lower[i, j] = d[i, j] * inverse[j]
        for k in range(j + 1, 8):
            for i in range(k, 8):
                d[i, k] = d[i, k] - lower[i, j] * d[k, j]
        for i in range(j + 1, 8):
            y[i] = y[i] - lower[i, j] * y[j]
    y = [y[j] * inverse[j] for j in range(8)]
    for j in range(7, -1, -1):
        for i in range(j):
            y[i] = y[i] - lower[j, i] * y[j]
    return y


def eliminated(x, rows, base, lane):
    inside = (lane >= base) & (lane < base + 8)
    t = [lane_column(x, base + j) * rows[j] for j in range(8)]
    total = ((t[0] + t[1]) + (t[2] + t[3])) + ((t[4] + t[5]) + (t[6] + t[7]))
    return jnp.where(inside, 0.0, x) - total


def inverse_of_block(rows):
    lane = lax.broadcasted_iota(jnp.int32, (8, LANES), 1)
    sub = lax.broadcasted_iota(jnp.int32, (8, LANES), 0)
    rows = list(rows)
    for g in range(16):
        pivots = pivot_rows(rows[g], 8 * g, lane, sub)
        for t in range(1, 16):
            h = (g + t) % 16
            rows[h] = eliminated(rows[h], pivots, 8 * g, lane)
        own = pivots[0]
        for j in range(1, 8):
            own = jnp.where(sub == j, pivots[j], own)
        rows[g] = own
    return rows


def solve_kernel(at_ref, near_ref, far_ref, basis_ref, out_ref, sums_ref, system_ref, *, scale):
    core = at_ref[0]
    z = at_ref[1]
    for flip in range(4):
        at = pl.multiple_of((core * 4 + (z ^ flip)) * PIECE, 8)
        sums_ref[pl.ds(at, PIECE), :] = near_ref[flip]
        at = pl.multiple_of(((1 - core) * 4 + (z ^ flip)) * PIECE, 8)
        sums_ref[pl.ds(at, PIECE), :] = far_ref[flip]
    diagonal = (
        lax.broadcasted_iota(jnp.int32, (BLOCK, BLOCK), 0)
        == lax.broadcasted_iota(jnp.int32, (BLOCK, BLOCK), 1)
    )
    for at, (i, j) in enumerate(GRAM_BLOCKS):
        block = sums_ref[at * BLOCK:(at + 1) * BLOCK, :] * scale
        if i == j:
            block = block + jnp.where(diagonal, RIDGE, 0.0)
        else:
            system_ref[j * BLOCK:(j + 1) * BLOCK, i * BLOCK:(i + 1) * BLOCK] = block.T
        system_ref[i * BLOCK:(i + 1) * BLOCK, j * BLOCK:(j + 1) * BLOCK] = block
    for i in range(4):
        row = sums_ref[MOMENT_ROW + 8 * i:MOMENT_ROW + 8 * i + 1, :] * scale
        system_ref[i * BLOCK:(i + 1) * BLOCK, 512:] = jnp.broadcast_to(row, (BLOCK, BLOCK)).T

    for i in range(4):
        lo = i * BLOCK
        inverse = inverse_of_block(
            [system_ref[lo + 8 * g:lo + 8 * g + 8, lo:lo + BLOCK] for g in range(16)]
        )
        inverse = jnp.concatenate(inverse, axis=0)
        solved = exact_dot(inverse, system_ref[lo:lo + BLOCK, lo + BLOCK:])
        for j in range(4):
            if j != i:
                system_ref[j * BLOCK:(j + 1) * BLOCK, lo + BLOCK:] -= exact_dot(
                    system_ref[j * BLOCK:(j + 1) * BLOCK, lo:lo + BLOCK], solved
                )
        system_ref[lo:lo + BLOCK, lo + BLOCK:] = solved
    width = basis_ref.shape[1]
    for lo in range(0, width, 512):
        parts = [jnp.zeros((8, 512), f32) for _ in range(4)]
        for b in range(64):
            coefficient = jnp.tile(system_ref[8 * b:8 * b + 8, 512:], (1, 4))
            parts[b % 4] += coefficient * basis_ref[8 * b:8 * b + 8, lo:lo + 512].astype(f32)
        out_ref[:, lo:lo + 512] = jnp.sum(
            (parts[0] + parts[1]) + (parts[2] + parts[3]), axis=0, keepdims=True
        )


def solve_continuation(near, far, basis, path_count):
    at = jnp.stack([lax.axis_index("core"), lax.axis_index("z")]).astype(jnp.int32)
    whole = pl.BlockSpec((4, PIECE, LANES), lambda i, s: (0, 0, 0))
    return pl.pallas_call(
        lambda *refs: solve_kernel(*refs, scale=1.0 / path_count),
        out_shape=jax.ShapeDtypeStruct((1, basis.shape[1]), f32),
        grid_spec=pltpu.PrefetchScalarGridSpec(
            num_scalar_prefetch=1,
            grid=(1,),
            in_specs=[whole, whole, pl.BlockSpec(basis.shape, lambda i, s: (0, 0))],
            out_specs=pl.BlockSpec((1, basis.shape[1]), lambda i, s: (0, 0)),
            scratch_shapes=[
                pltpu.VMEM((SUM_ROWS, LANES), f32),
                pltpu.VMEM((512, 512 + LANES), f32),
            ],
        ),
        compiler_params=pltpu.CompilerParams(vmem_limit_bytes=40 << 20),
        name="solve_continuation",
    )(at, near, far, basis)


def increments_kernel(moved_ref, mixer_ref, basket_ref, sent_ref, weights_ref, buffer_ref, copied):
    copies = []
    for tile in range(moved_ref.shape[2] // INCREMENT_TILE):
        span = pl.ds(tile * INCREMENT_TILE, INCREMENT_TILE)
        adjoint = moved_ref[:, :, span].reshape(256, INCREMENT_TILE).astype(f32)
        for date in range(STEPS - 1, -1, -1):
            gain = TIME_STEP * jnp.dot(
                mixer_ref[...], adjoint.astype(bf16), preferred_element_type=f32
            )
            buffer_ref[tile, :, date] = gain.astype(bf16).reshape(8, 32, INCREMENT_TILE)
            if date:
                adjoint = adjoint + gain
        copies.append(
            pltpu.make_async_copy(buffer_ref.at[tile], sent_ref.at[:, :, :, span], copied.at[tile])
        )
        copies[-1].start()
    lane = lax.broadcasted_iota(jnp.int32, (256, LANES), 1)
    weight = jnp.broadcast_to(basket_ref[...], (256, LANES))
    table = weight
    for later in range(1, STEPS):
        gain = sum(
            jnp.dot(mixer_ref[...], part, preferred_element_type=f32) for part in three_terms(weight)
        )
        weight = weight + TIME_STEP * gain
        table = jnp.where(lane == later, weight, table)
    weights_ref[...] = table
    for copy in copies:
        copy.wait()


def increments(moved, mixer, basket, slab_part):
    tiles = slab_part // INCREMENT_TILE
    return pl.pallas_call(
        increments_kernel,
        out_shape=(
            pltpu.HBM((8, STEPS, 32, slab_part), bf16),
            jax.ShapeDtypeStruct((256, LANES), f32),
        ),
        out_specs=(
            pl.BlockSpec(memory_space=pltpu.HBM),
            pl.BlockSpec(memory_space=pltpu.VMEM),
        ),
        scratch_shapes=[
            pltpu.VMEM((tiles, 8, STEPS, 32, INCREMENT_TILE), bf16),
            pltpu.SemaphoreType.DMA((tiles,)),
        ],
        compiler_params=pltpu.CompilerParams(vmem_limit_bytes=40 << 20),
        name="increments",
    )(moved, mixer, basket)


def surface_kernel(slab_ref, *refs):
    continuation_refs = refs[:2]
    (cotangent_ref, gain_ref, shock_ref, weight_ref, exercise_ref, bucket_ref, delta_ref, share_ref,
     continuation_ref, total_ref) = refs[2:]
    step = pl.program_id(0)

    @pl.when(step == 0)
    def _():
        for flip in range(8):
            continuation_ref[pl.ds(slab_ref[0] ^ flip, 1), :] = continuation_refs[flip % 2][
                flip // 2:flip // 2 + 1, :
            ]
        total_ref[...] = jnp.zeros(total_ref.shape, f32)

    continuation = continuation_ref[pl.ds(step, 1), :]
    held = [exercise_ref[date:date + 1, :].astype(f32) * continuation for date in range(STEPS)]
    weights = [weight_ref[:, later:later + 1] for later in range(STEPS)]
    strikes = lax.broadcasted_iota(jnp.int32, (STRIKE_ROWS, DATE_TILE), 0).astype(f32).astype(bf16)
    base = cotangent_ref[...].astype(f32)
    total = total_ref[...]
    for date in range(STEPS - 1, -1, -1):
        base = base + gain_ref[0, date].astype(f32)
        adjoint = base
        for later in range(STEPS - date):
            adjoint = adjoint + held[date + later] * weights[later]
        terms = (adjoint * shock_ref[date].astype(f32)).astype(bf16).astype(f32)
        bucket = bucket_ref[date:date + 1, :]
        column = (bucket & (STRIKE_ROWS - 1)).astype(f32).astype(bf16)
        chosen = jnp.where(strikes == column, jnp.bfloat16(1), jnp.bfloat16(0))
        group = bucket >> STRIKE_BITS
        terms = jnp.concatenate(
            [jnp.where(group == g, terms, 0.0).astype(bf16) for g in range(NK // STRIKE_ROWS)], axis=0
        )
        total = total + lax.dot_general(
            chosen, terms, (((1,), (1,)), ((), ())), preferred_element_type=f32
        )
    delta_ref[...] = adjoint
    total_ref[...] = total

    @pl.when(step == pl.num_programs(0) - 1)
    def _():
        owners = STRIKE_ROWS // 16
        for g in range(NK // STRIKE_ROWS):
            grouped = total[:, 32 * g:32 * g + 32].reshape(owners, 16, 32)
            for q in range(4):
                share_ref[g * owners:(g + 1) * owners, :, 32 * q:32 * q + 32] = grouped[
                    :, 4 * q:4 * q + 4, :
                ]


def surface_and_delta(slab, continuations, cotangent, gains, shocks, weights, exercise, bucket):
    local_paths = cotangent.shape[1]
    whole = pl.BlockSpec((4, DATE_TILE), lambda i, s: (0, 0))
    return pl.pallas_call(
        surface_kernel,
        out_shape=(
            jax.ShapeDtypeStruct((32, local_paths), f32),
            jax.ShapeDtypeStruct((16, 4, LANES), f32),
        ),
        grid_spec=pltpu.PrefetchScalarGridSpec(
            num_scalar_prefetch=1,
            grid=(local_paths // DATE_TILE,),
            in_specs=[whole] * 2 + [
                pl.BlockSpec((32, DATE_TILE), lambda i, s: (0, i)),
                pl.BlockSpec((1, STEPS, 32, DATE_TILE), lambda i, s: (i, 0, 0, 0)),
                pl.BlockSpec((STEPS, 32, DATE_TILE), lambda i, s: (0, 0, i)),
                pl.BlockSpec((32, LANES), lambda i, s: (s[0], 0)),
                pl.BlockSpec((STEPS, DATE_TILE), lambda i, s: (0, i)),
                pl.BlockSpec((STEPS, DATE_TILE), lambda i, s: (0, i)),
            ],
            out_specs=(
                pl.BlockSpec((32, DATE_TILE), lambda i, s: (0, i)),
                pl.BlockSpec((16, 4, LANES), lambda i, s: (0, 0, 0)),
            ),
            scratch_shapes=[pltpu.VMEM((8, DATE_TILE), f32), pltpu.VMEM((STRIKE_ROWS, 32 * (NK // STRIKE_ROWS)), f32)],
        ),
        compiler_params=pltpu.CompilerParams(vmem_limit_bytes=48 << 20),
        name="surface_and_delta",
    )(slab, *continuations, cotangent, gains, shocks, weights, exercise, bucket)


def per_device(prices, loadings, basis_w, basis_bias, payoff, in_fit, cotangent, shocks, corr_gen,
               basket, exercise, bucket):
    local_paths = prices.shape[1]
    slab_part = local_paths // 8
    path_count = float(local_paths * 16)
    slab = lax.axis_index(STOCK_AXES).astype(jnp.int32).reshape(1)

    pieces = jnp.moveaxis(prices.reshape(32, 8, slab_part), 1, 0)
    table = jnp.broadcast_to(jnp.pad(loadings, ((0, 0), (0, LANES - 32)))[None], (8, 32, LANES))
    moved_prices = lax.all_to_all(
        jnp.concatenate([pieces, table], axis=2), STOCK_AXES, 0, 0, tiled=True
    )
    slabs = jnp.moveaxis(cotangent.reshape(32, 8, slab_part), 1, 0)
    small = (left_terms(basis_w, 0), basis_bias[:, None], payoff[None, :], in_fit[None, :],
             basket[:, None])
    slabs, moved_prices, small = lax.optimization_barrier((slabs, moved_prices, small))
    weight_terms, bias, payoff, in_fit, basket = small
    moved = lax.all_to_all(slabs, STOCK_AXES, 0, 0, tiled=True)
    place = jnp.stack([slab[0], lax.axis_index("core").astype(jnp.int32)])
    basis, kept, other = regression_sums(
        place, moved_prices, weight_terms, bias, payoff, in_fit, slab_part
    )
    share, moved = sum_over_cores_and_z(kept, other, moved)
    sent, weights = increments(moved, corr_gen, basket, slab_part)
    share, sent = sum_over_others(share, "x", sent)
    share, sent = sum_over_others(share, ("ylo", "yhi"), sent)
    gains = lax.all_to_all(sent, STOCK_AXES, 0, 0, tiled=True)
    near, far = gathered_sum(share)
    continuation = solve_continuation(near, far, basis, path_count)
    column = jnp.concatenate([continuation] + exchange_with_others(continuation, "x", 4), axis=0)
    continuations = [column] + exchange_with_others(column, "yhi", 2)
    delta, surface = surface_and_delta(
        slab, continuations, cotangent, gains, shocks, weights, exercise, bucket
    )
    surface = lax.all_to_all(surface, PATH_AXES, 0, 0, tiled=True)
    surface = jnp.sum(surface, axis=0).reshape(4, 4, 32)
    surface = jnp.transpose(surface, (2, 1, 0)).reshape(32, 16)
    return delta, surface


def solution(mesh):
    fine = Mesh(mesh.devices.reshape(FINE), ALL_AXES)
    stocks, paths = STOCK_AXES, PATH_AXES
    return jax.shard_map(
        per_device,
        mesh=fine,
        in_specs=(
            P(stocks, paths),
            P(stocks, None),
            P(),
            P(),
            P(paths),
            P(paths),
            P(stocks, paths),
            P(None, stocks, paths),
            P(),
            P(),
            P(None, paths),
            P(None, paths),
        ),
        out_specs=(P(stocks, paths), P(stocks, paths)),
        check_vma=False,
    )
```

```python
import jax
import jax.numpy as jnp
from jax import lax
from jax.experimental import pallas as pl
from jax.experimental.pallas import tpu as pltpu
from jax.sharding import Mesh
from jax.sharding import PartitionSpec as P

NK = 256
STEPS = 4
TIME_STEP = 0.25
RIDGE = 0.1
LANES = 128
BLOCK = 128
TILE = 512
INCREMENT_TILE = 512
DATE_TILE = 2048
STRIKE_BITS = 7
STRIKE_ROWS = 1 << STRIKE_BITS
PATH_AXES = ("z", "ylo", "core")
STOCK_AXES = ("x", "yhi")
ALL_AXES = PATH_AXES + STOCK_AXES
FINE = (4, 2, 2, 4, 2)
f32 = jnp.float32
bf16 = jnp.bfloat16


def three_terms(x):
    high = x.astype(bf16)
    rest = x - high.astype(f32)
    middle = rest.astype(bf16)
    low = (rest - middle.astype(f32)).astype(bf16)
    return high, middle, low


def left_terms(x, axis):
    high, middle, low = three_terms(x)
    return jnp.concatenate([high, high, middle, high, low, middle], axis=axis)


def right_terms(x, axis):
    high, middle, low = three_terms(x)
    return jnp.concatenate([high, middle, high, low, high, middle], axis=axis)


def exact_dot(left, right):
    return jnp.dot(left_terms(left, 1), right_terms(right, 0), preferred_element_type=f32)


GRAM_BLOCKS = tuple((i, j) for i in range(4) for j in range(i + 1))
MOMENT_ROW = len(GRAM_BLOCKS) * BLOCK
SUM_ROWS = 1344
PIECE = SUM_ROWS // 8


def gram_kernel(slab_ref, moved_ref, table_ref, weight_ref, bias_ref, payoff_ref, fit_ref,
                basis_ref, kept_ref, sent_ref, gram_ref, moment_ref, sums_ref):
    step = pl.program_id(0)
    tile = moved_ref[...].reshape(256, TILE)
    loads = table_ref[...].reshape(256, LANES)[:, :32]
    factors = lax.dot_general(loads, tile, (((0,), (0,)), ((), ())), preferred_element_type=f32)
    raised = lax.dot_general(
        left_terms(weight_ref[...], 0), right_terms(factors, 0), (((0,), (0,)), ((), ())), preferred_element_type=f32
    )
    basis = jnp.tanh(raised + bias_ref[...]).astype(bf16)
    basis_ref[...] = basis
    picked = basis * fit_ref[...].astype(f32).astype(bf16)
    paid = jnp.broadcast_to(payoff_ref[...].astype(f32), (16, TILE)).astype(bf16)
    contract = (((1,), (1,)), ((), ()))
    first = lax.dot_general(picked[:256], basis[:256], contract, preferred_element_type=f32)
    second = lax.dot_general(picked[256:], basis, contract, preferred_element_type=f32)
    moment = lax.dot_general(paid, picked, contract, preferred_element_type=f32)

    @pl.when(step == 0)
    def _():
        gram_ref[:256, :256] = first
        gram_ref[256:, :] = second
        moment_ref[...] = moment

    @pl.when(step > 0)
    def _():
        gram_ref[:256, :256] += first
        gram_ref[256:, :] += second
        moment_ref[...] += moment

    @pl.when(step == pl.num_programs(0) - 1)
    def _():
        for at, (i, j) in enumerate(GRAM_BLOCKS):
            sums_ref[at * BLOCK:(at + 1) * BLOCK, :] = gram_ref[
                i * BLOCK:(i + 1) * BLOCK, j * BLOCK:(j + 1) * BLOCK
            ]
        sums_ref[MOMENT_ROW:, :] = jnp.zeros((SUM_ROWS - MOMENT_ROW, LANES), f32)
        for i in range(4):
            sums_ref[MOMENT_ROW + 8 * i:MOMENT_ROW + 8 * i + 8, :] = moment_ref[
                :8, i * BLOCK:(i + 1) * BLOCK
            ]
        half = 4 * PIECE
        kept_ref[...] = sums_ref[pl.ds(pl.multiple_of(slab_ref[1] * half, 8), half), :]
        sent_ref[...] = sums_ref[pl.ds(pl.multiple_of((1 - slab_ref[1]) * half, 8), half), :]


def regression_sums(slab, moved, weights, bias, payoff, fit, slab_part):
    tiles = slab_part // TILE
    table_at = slab_part // LANES

    def own(step, slab_ref):
        return (0, slab_ref[0] * tiles + step)

    return pl.pallas_call(
        gram_kernel,
        out_shape=(
            pltpu.HBM((512, slab_part), bf16),
            pltpu.HBM((SUM_ROWS // 2, LANES), f32),
            pltpu.HBM((SUM_ROWS // 2, LANES), f32),
        ),
        grid_spec=pltpu.PrefetchScalarGridSpec(
            num_scalar_prefetch=1,
            grid=(tiles,),
            in_specs=[
                pl.BlockSpec((8, 32, TILE), lambda i, s: (0, 0, i)),
                pl.BlockSpec((8, 32, LANES), lambda i, s: (0, 0, table_at)),
                pl.BlockSpec((32, 512), lambda i, s: (0, 0)),
                pl.BlockSpec((512, 1), lambda i, s: (0, 0)),
                pl.BlockSpec((1, TILE), own),
                pl.BlockSpec((1, TILE), own),
            ],
            out_specs=(
                pl.BlockSpec((512, TILE), lambda i, s: (0, i)),
                pl.BlockSpec((SUM_ROWS // 2, LANES), lambda i, s: (0, 0)),
                pl.BlockSpec((SUM_ROWS // 2, LANES), lambda i, s: (0, 0)),
            ),
            scratch_shapes=[
                pltpu.VMEM((512, 512), f32),
                pltpu.VMEM((16, 512), f32),
                pltpu.VMEM((SUM_ROWS, LANES), f32),
            ],
        ),
        compiler_params=pltpu.CompilerParams(vmem_limit_bytes=20 << 20),
        name="regression_sums",
    )(slab, moved, moved, weights, bias, payoff, fit)


def exchange_with_others(x, axes, count, piece_of=None):
    received = []
    for flip in range(1, count):
        sent = x if piece_of is None else piece_of(flip)
        received.append(lax.ppermute(sent, axes, [(i, i ^ flip) for i in range(count)]))
    return received


def sum_over_cores_and_z(kept, sent, beside):
    z = lax.axis_index("z")
    mine = (kept + exchange_with_others(sent, "core", 2)[0]).reshape(4, PIECE, LANES)

    def piece_of(flip):
        return lax.dynamic_index_in_dim(mine, z ^ flip, 0, False)

    parts, beside = lax.optimization_barrier((exchange_with_others(None, "z", 4, piece_of), beside))
    return (piece_of(0) + parts[0]) + (parts[1] + parts[2]), beside


def sum_over_others(share, axes, beside):
    parts, beside = lax.optimization_barrier((exchange_with_others(share, axes, 4), beside))
    return (share + parts[0]) + (parts[1] + parts[2]), beside


def gathered_sum(share):
    column = jnp.stack([share] + exchange_with_others(share, "z", 4))
    return column, exchange_with_others(column, "core", 2)[0]


def lane_column(x, j):
    return jnp.broadcast_to(x[:, j:j + 1], (8, LANES))


def sublane_row(x, j):
    return jnp.broadcast_to(x[j:j + 1, :], (8, LANES))


def pivot_rows(panel, base, lane, sub):
    inside = (lane >= base) & (lane < base + 8)
    columns = [lane_column(panel, base + j) for j in range(8)]
    d = {(i, j): sublane_row(columns[j], i) for j in range(8) for i in range(j, 8)}
    marked = jnp.where(inside, jnp.where(lane - base == sub, 1.0, 0.0), panel)
    y = [sublane_row(marked, j) for j in range(8)]
    lower = {}
    inverse = []
    for j in range(8):
        inverse.append(1.0 / d[j, j])
        for i in range(j + 1, 8):
            lower[i, j] = d[i, j] * inverse[j]
        for k in range(j + 1, 8):
            for i in range(k, 8):
                d[i, k] = d[i, k] - lower[i, j] * d[k, j]
        for i in range(j + 1, 8):
            y[i] = y[i] - lower[i, j] * y[j]
    y = [y[j] * inverse[j] for j in range(8)]
    for j in range(7, -1, -1):
        for i in range(j):
            y[i] = y[i] - lower[j, i] * y[j]
    return y


def eliminated(x, rows, base, lane):
    inside = (lane >= base) & (lane < base + 8)
    t = [lane_column(x, base + j) * rows[j] for j in range(8)]
    total = ((t[0] + t[1]) + (t[2] + t[3])) + ((t[4] + t[5]) + (t[6] + t[7]))
    return jnp.where(inside, 0.0, x) - total


def inverse_of_block(rows):
    lane = lax.broadcasted_iota(jnp.int32, (8, LANES), 1)
    sub = lax.broadcasted_iota(jnp.int32, (8, LANES), 0)
    rows = list(rows)
    for g in range(16):
        pivots = pivot_rows(rows[g], 8 * g, lane, sub)
        for t in range(1, 16):
            h = (g + t) % 16
            rows[h] = eliminated(rows[h], pivots, 8 * g, lane)
        own = pivots[0]
        for j in range(1, 8):
            own = jnp.where(sub == j, pivots[j], own)
        rows[g] = own
    return rows


def solve_kernel(at_ref, near_ref, far_ref, basis_ref, out_ref, sums_ref, system_ref, *, scale):
    core = at_ref[0]
    z = at_ref[1]
    for flip in range(4):
        at = pl.multiple_of((core * 4 + (z ^ flip)) * PIECE, 8)
        sums_ref[pl.ds(at, PIECE), :] = near_ref[flip]
        at = pl.multiple_of(((1 - core) * 4 + (z ^ flip)) * PIECE, 8)
        sums_ref[pl.ds(at, PIECE), :] = far_ref[flip]
    diagonal = (
        lax.broadcasted_iota(jnp.int32, (BLOCK, BLOCK), 0)
        == lax.broadcasted_iota(jnp.int32, (BLOCK, BLOCK), 1)
    )
    for at, (i, j) in enumerate(GRAM_BLOCKS):
        block = sums_ref[at * BLOCK:(at + 1) * BLOCK, :] * scale
        if i == j:
            block = block + jnp.where(diagonal, RIDGE, 0.0)
        else:
            system_ref[j * BLOCK:(j + 1) * BLOCK, i * BLOCK:(i + 1) * BLOCK] = block.T
        system_ref[i * BLOCK:(i + 1) * BLOCK, j * BLOCK:(j + 1) * BLOCK] = block
    for i in range(4):
        row = sums_ref[MOMENT_ROW + 8 * i:MOMENT_ROW + 8 * i + 1, :] * scale
        system_ref[i * BLOCK:(i + 1) * BLOCK, 512:] = jnp.broadcast_to(row, (BLOCK, BLOCK)).T

    for i in range(4):
        lo = i * BLOCK
        inverse = inverse_of_block(
            [system_ref[lo + 8 * g:lo + 8 * g + 8, lo:lo + BLOCK] for g in range(16)]
        )
        inverse = jnp.concatenate(inverse, axis=0)
        solved = exact_dot(inverse, system_ref[lo:lo + BLOCK, lo + BLOCK:])
        for j in range(4):
            if j != i:
                system_ref[j * BLOCK:(j + 1) * BLOCK, lo + BLOCK:] -= exact_dot(
                    system_ref[j * BLOCK:(j + 1) * BLOCK, lo:lo + BLOCK], solved
                )
        system_ref[lo:lo + BLOCK, lo + BLOCK:] = solved
    width = basis_ref.shape[1]
    for lo in range(0, width, 512):
        parts = [jnp.zeros((8, 512), f32) for _ in range(4)]
        for b in range(64):
            coefficient = jnp.tile(system_ref[8 * b:8 * b + 8, 512:], (1, 4))
            parts[b % 4] += coefficient * basis_ref[8 * b:8 * b + 8, lo:lo + 512].astype(f32)
        out_ref[:, lo:lo + 512] = jnp.sum(
            (parts[0] + parts[1]) + (parts[2] + parts[3]), axis=0, keepdims=True
        )


def solve_continuation(near, far, basis, path_count):
    at = jnp.stack([lax.axis_index("core"), lax.axis_index("z")]).astype(jnp.int32)
    whole = pl.BlockSpec((4, PIECE, LANES), lambda i, s: (0, 0, 0))
    return pl.pallas_call(
        lambda *refs: solve_kernel(*refs, scale=1.0 / path_count),
        out_shape=jax.ShapeDtypeStruct((1, basis.shape[1]), f32),
        grid_spec=pltpu.PrefetchScalarGridSpec(
            num_scalar_prefetch=1,
            grid=(1,),
            in_specs=[whole, whole, pl.BlockSpec(basis.shape, lambda i, s: (0, 0))],
            out_specs=pl.BlockSpec((1, basis.shape[1]), lambda i, s: (0, 0)),
            scratch_shapes=[
                pltpu.VMEM((SUM_ROWS, LANES), f32),
                pltpu.VMEM((512, 512 + LANES), f32),
            ],
        ),
        compiler_params=pltpu.CompilerParams(vmem_limit_bytes=20 << 20),
        name="solve_continuation",
    )(at, near, far, basis)


def increments_kernel(moved_ref, mixer_ref, basket_ref, sent_ref, weights_ref, buffer_ref, copied):
    copies = []
    for tile in range(moved_ref.shape[2] // INCREMENT_TILE):
        span = pl.ds(tile * INCREMENT_TILE, INCREMENT_TILE)
        adjoint = moved_ref[:, :, span].reshape(256, INCREMENT_TILE).astype(f32)
        for date in range(STEPS - 1, -1, -1):
            gain = TIME_STEP * jnp.dot(
                mixer_ref[...], adjoint.astype(bf16), preferred_element_type=f32
            )
            buffer_ref[tile, :, date] = gain.astype(bf16).reshape(8, 32, INCREMENT_TILE)
            if date:
                adjoint = adjoint + gain
        copies.append(
            pltpu.make_async_copy(buffer_ref.at[tile], sent_ref.at[:, :, :, span], copied.at[tile])
        )
        copies[-1].start()
    lane = lax.broadcasted_iota(jnp.int32, (256, LANES), 1)
    weight = jnp.broadcast_to(basket_ref[...], (256, LANES))
    table = weight
    for later in range(1, STEPS):
        gain = sum(
            jnp.dot(mixer_ref[...], part, preferred_element_type=f32) for part in three_terms(weight)
        )
        weight = weight + TIME_STEP * gain
        table = jnp.where(lane == later, weight, table)
    weights_ref[...] = table
    for copy in copies:
        copy.wait()


def increments(moved, mixer, basket, slab_part):
    tiles = slab_part // INCREMENT_TILE
    return pl.pallas_call(
        increments_kernel,
        out_shape=(
            pltpu.HBM((8, STEPS, 32, slab_part), bf16),
            jax.ShapeDtypeStruct((256, LANES), f32),
        ),
        out_specs=(
            pl.BlockSpec(memory_space=pltpu.HBM),
            pl.BlockSpec(memory_space=pltpu.VMEM),
        ),
        scratch_shapes=[
            pltpu.VMEM((tiles, 8, STEPS, 32, INCREMENT_TILE), bf16),
            pltpu.SemaphoreType.DMA((tiles,)),
        ],
        compiler_params=pltpu.CompilerParams(vmem_limit_bytes=20 << 20),
        name="increments",
    )(moved, mixer, basket)


def surface_kernel(slab_ref, *refs):
    continuation_refs = refs[:4]
    (cotangent_ref, gain_ref, shock_ref, weight_ref, exercise_ref, bucket_ref, delta_ref, share_ref,
     continuation_ref, total_ref) = refs[4:]
    step = pl.program_id(0)

    @pl.when(step == 0)
    def _():
        for flip in range(8):
            continuation_ref[pl.ds(slab_ref[0] ^ flip, 1), :] = continuation_refs[flip // 2][
                flip % 2:flip % 2 + 1, :
            ]
        total_ref[...] = jnp.zeros(total_ref.shape, f32)

    continuation = continuation_ref[pl.ds(step, 1), :]
    held = [exercise_ref[date:date + 1, :].astype(f32) * continuation for date in range(STEPS)]
    weights = [weight_ref[:, later:later + 1] for later in range(STEPS)]
    strikes = lax.broadcasted_iota(jnp.int32, (STRIKE_ROWS, DATE_TILE), 0).astype(f32).astype(bf16)
    base = cotangent_ref[...].astype(f32)
    total = total_ref[...]
    for date in range(STEPS - 1, -1, -1):
        base = base + gain_ref[0, date].astype(f32)
        adjoint = base
        for later in range(STEPS - date):
            adjoint = adjoint + held[date + later] * weights[later]
        terms = (adjoint * shock_ref[date].astype(f32)).astype(bf16).astype(f32)
        bucket = bucket_ref[date:date + 1, :]
        column = (bucket & (STRIKE_ROWS - 1)).astype(f32).astype(bf16)
        chosen = jnp.where(strikes == column, jnp.bfloat16(1), jnp.bfloat16(0))
        group = bucket >> STRIKE_BITS
        terms = jnp.concatenate(
            [jnp.where(group == g, terms, 0.0).astype(bf16) for g in range(NK // STRIKE_ROWS)], axis=0
        )
        total = total + lax.dot_general(
            chosen, terms, (((1,), (1,)), ((), ())), preferred_element_type=f32
        )
    delta_ref[...] = adjoint
    total_ref[...] = total

    @pl.when(step == pl.num_programs(0) - 1)
    def _():
        owners = STRIKE_ROWS // 16
        for g in range(NK // STRIKE_ROWS):
            grouped = total[:, 32 * g:32 * g + 32].reshape(owners, 16, 32)
            for q in range(4):
                share_ref[g * owners:(g + 1) * owners, :, 32 * q:32 * q + 32] = grouped[
                    :, 4 * q:4 * q + 4, :
                ]


def surface_and_delta(slab, continuations, cotangent, gains, shocks, weights, exercise, bucket):
    local_paths = cotangent.shape[1]
    whole = pl.BlockSpec((2, DATE_TILE), lambda i, s: (0, 0))
    return pl.pallas_call(
        surface_kernel,
        out_shape=(
            jax.ShapeDtypeStruct((32, local_paths), f32),
            jax.ShapeDtypeStruct((16, 4, LANES), f32),
        ),
        grid_spec=pltpu.PrefetchScalarGridSpec(
            num_scalar_prefetch=1,
            grid=(local_paths // DATE_TILE,),
            in_specs=[whole] * 4 + [
                pl.BlockSpec((32, DATE_TILE), lambda i, s: (0, i)),
                pl.BlockSpec((1, STEPS, 32, DATE_TILE), lambda i, s: (i, 0, 0, 0)),
                pl.BlockSpec((STEPS, 32, DATE_TILE), lambda i, s: (0, 0, i)),
                pl.BlockSpec((32, LANES), lambda i, s: (s[0], 0)),
                pl.BlockSpec((STEPS, DATE_TILE), lambda i, s: (0, i)),
                pl.BlockSpec((STEPS, DATE_TILE), lambda i, s: (0, i)),
            ],
            out_specs=(
                pl.BlockSpec((32, DATE_TILE), lambda i, s: (0, i)),
                pl.BlockSpec((16, 4, LANES), lambda i, s: (0, 0, 0)),
            ),
            scratch_shapes=[pltpu.VMEM((8, DATE_TILE), f32), pltpu.VMEM((STRIKE_ROWS, 32 * (NK // STRIKE_ROWS)), f32)],
        ),
        compiler_params=pltpu.CompilerParams(vmem_limit_bytes=32 << 20),
        name="surface_and_delta",
    )(slab, *continuations, cotangent, gains, shocks, weights, exercise, bucket)


def per_device(prices, loadings, basis_w, basis_bias, payoff, in_fit, cotangent, shocks, corr_gen,
               basket, exercise, bucket):
    local_paths = prices.shape[1]
    slab_part = local_paths // 8
    path_count = float(local_paths * 16)
    slab = lax.axis_index(STOCK_AXES).astype(jnp.int32).reshape(1)

    pieces = jnp.moveaxis(prices.reshape(32, 8, slab_part), 1, 0)
    table = jnp.broadcast_to(jnp.pad(loadings, ((0, 0), (0, LANES - 32)))[None], (8, 32, LANES))
    moved_prices = lax.all_to_all(
        jnp.concatenate([pieces, table], axis=2), STOCK_AXES, 0, 0, tiled=True
    )
    slabs = jnp.moveaxis(cotangent.reshape(32, 8, slab_part), 1, 0)
    small = (basis_w, basis_bias[:, None], payoff[None, :], in_fit[None, :],
             basket[:, None])
    slabs, moved_prices, small = lax.optimization_barrier((slabs, moved_prices, small))
    basis_w, bias, payoff, in_fit, basket = small
    moved = lax.all_to_all(slabs, STOCK_AXES, 0, 0, tiled=True)
    basis_w = pltpu.with_memory_space_constraint(basis_w, pltpu.HBM)
    in_fit = pltpu.with_memory_space_constraint(in_fit, pltpu.HBM)
    place = jnp.stack([slab[0], lax.axis_index("core").astype(jnp.int32)])
    basis, kept, other = regression_sums(
        place, moved_prices, basis_w, bias, payoff, in_fit, slab_part
    )
    share, moved = sum_over_cores_and_z(kept, other, moved)
    sent, weights = increments(moved, corr_gen, basket, slab_part)
    share, sent = sum_over_others(share, "x", sent)
    share, sent = sum_over_others(share, ("ylo", "yhi"), sent)
    gains = lax.all_to_all(sent, STOCK_AXES, 0, 0, tiled=True)
    near, far = gathered_sum(share)
    continuation = solve_continuation(near, far, basis, path_count)
    pair = jnp.concatenate([continuation] + exchange_with_others(continuation, "yhi", 2), axis=0)
    continuations = [pair] + exchange_with_others(pair, "x", 4)
    delta, surface = surface_and_delta(
        slab, continuations, cotangent, gains, shocks, weights, exercise, bucket
    )
    surface = lax.all_to_all(surface, PATH_AXES, 0, 0, tiled=True)
    surface = jnp.sum(surface, axis=0).reshape(4, 4, 32)
    surface = jnp.transpose(surface, (2, 1, 0)).reshape(32, 16)
    return delta, surface


def solution(mesh):
    fine = Mesh(mesh.devices.reshape(FINE), ALL_AXES)
    stocks, paths = STOCK_AXES, PATH_AXES
    return jax.shard_map(
        per_device,
        mesh=fine,
        in_specs=(
            P(stocks, paths),
            P(stocks, None),
            P(),
            P(),
            P(paths),
            P(paths),
            P(stocks, paths),
            P(None, stocks, paths),
            P(),
            P(),
            P(None, paths),
            P(None, paths),
        ),
        out_specs=(P(stocks, paths), P(stocks, paths)),
        check_vma=False,
    )
```

```python
import jax
import jax.numpy as jnp
from jax import lax
from jax.experimental import pallas as pl
from jax.experimental.pallas import tpu as pltpu
from jax.sharding import Mesh
from jax.sharding import PartitionSpec as P

NK = 256
STEPS = 4
TIME_STEP = 0.25
RIDGE = 0.1
LANES = 128
BLOCK = 128
TILE = 2048
INCREMENT_TILE = 1024
DATE_TILE = 2048
STRIKE_BITS = 7
STRIKE_ROWS = 1 << STRIKE_BITS
PATH_AXES = ("z", "ylo", "core")
STOCK_AXES = ("x", "yhi")
ALL_AXES = PATH_AXES + STOCK_AXES
FINE = (4, 2, 2, 4, 2)
f32 = jnp.float32
bf16 = jnp.bfloat16


def three_terms(x):
    high = x.astype(bf16)
    rest = x - high.astype(f32)
    middle = rest.astype(bf16)
    low = (rest - middle.astype(f32)).astype(bf16)
    return high, middle, low


def left_terms(x, axis):
    high, middle, low = three_terms(x)
    return jnp.concatenate([high, high, middle, high, low, middle], axis=axis)


def right_terms(x, axis):
    high, middle, low = three_terms(x)
    return jnp.concatenate([high, middle, high, low, high, middle], axis=axis)


def exact_dot(left, right):
    return jnp.dot(left_terms(left, 1), right_terms(right, 0), preferred_element_type=f32)


GRAM_BLOCKS = tuple((i, j) for i in range(4) for j in range(i + 1))
MOMENT_ROW = len(GRAM_BLOCKS) * BLOCK
SUM_ROWS = 1344
PIECE = SUM_ROWS // 8


def gram_kernel(slab_ref, moved_ref, table_ref, weight_ref, bias_ref, payoff_ref, fit_ref,
                basis_ref, kept_ref, sent_ref, gram_ref, moment_ref, sums_ref):
    step = pl.program_id(0)
    tile = moved_ref[...].reshape(256, TILE)
    loads = table_ref[...].reshape(256, LANES)[:, :32]
    factors = lax.dot_general(loads, tile, (((0,), (0,)), ((), ())), preferred_element_type=f32)
    raised = lax.dot_general(
        left_terms(weight_ref[...], 0), right_terms(factors, 0), (((0,), (0,)), ((), ())), preferred_element_type=f32
    )
    basis = jnp.tanh(raised + bias_ref[...]).astype(bf16)
    basis_ref[...] = basis
    picked = basis * fit_ref[...].astype(f32).astype(bf16)
    paid = jnp.broadcast_to(payoff_ref[...].astype(f32), (16, TILE)).astype(bf16)
    contract = (((1,), (1,)), ((), ()))
    first = lax.dot_general(picked[:256], basis[:256], contract, preferred_element_type=f32)
    second = lax.dot_general(picked[256:], basis, contract, preferred_element_type=f32)
    moment = lax.dot_general(paid, picked, contract, preferred_element_type=f32)

    @pl.when(step == 0)
    def _():
        gram_ref[:256, :256] = first
        gram_ref[256:, :] = second
        moment_ref[...] = moment

    @pl.when(step > 0)
    def _():
        gram_ref[:256, :256] += first
        gram_ref[256:, :] += second
        moment_ref[...] += moment

    @pl.when(step == pl.num_programs(0) - 1)
    def _():
        for at, (i, j) in enumerate(GRAM_BLOCKS):
            sums_ref[at * BLOCK:(at + 1) * BLOCK, :] = gram_ref[
                i * BLOCK:(i + 1) * BLOCK, j * BLOCK:(j + 1) * BLOCK
            ]
        sums_ref[MOMENT_ROW:, :] = jnp.zeros((SUM_ROWS - MOMENT_ROW, LANES), f32)
        for i in range(4):
            sums_ref[MOMENT_ROW + 8 * i:MOMENT_ROW + 8 * i + 8, :] = moment_ref[
                :8, i * BLOCK:(i + 1) * BLOCK
            ]
        half = 4 * PIECE
        kept_ref[...] = sums_ref[pl.ds(pl.multiple_of(slab_ref[1] * half, 8), half), :]
        sent_ref[...] = sums_ref[pl.ds(pl.multiple_of((1 - slab_ref[1]) * half, 8), half), :]


def regression_sums(slab, moved, weights, bias, payoff, fit, slab_part):
    tiles = slab_part // TILE
    table_at = slab_part // LANES

    def own(step, slab_ref):
        return (0, slab_ref[0] * tiles + step)

    return pl.pallas_call(
        gram_kernel,
        out_shape=(
            pltpu.HBM((512, slab_part), bf16),
            pltpu.HBM((SUM_ROWS // 2, LANES), f32),
            pltpu.HBM((SUM_ROWS // 2, LANES), f32),
        ),
        grid_spec=pltpu.PrefetchScalarGridSpec(
            num_scalar_prefetch=1,
            grid=(tiles,),
            in_specs=[
                pl.BlockSpec((8, 32, TILE), lambda i, s: (0, 0, i)),
                pl.BlockSpec((8, 32, LANES), lambda i, s: (0, 0, table_at)),
                pl.BlockSpec((32, 512), lambda i, s: (0, 0)),
                pl.BlockSpec((512, 1), lambda i, s: (0, 0)),
                pl.BlockSpec((1, TILE), own),
                pl.BlockSpec((1, TILE), own),
            ],
            out_specs=(
                pl.BlockSpec((512, TILE), lambda i, s: (0, i)),
                pl.BlockSpec((SUM_ROWS // 2, LANES), lambda i, s: (0, 0)),
                pl.BlockSpec((SUM_ROWS // 2, LANES), lambda i, s: (0, 0)),
            ),
            scratch_shapes=[
                pltpu.VMEM((512, 512), f32),
                pltpu.VMEM((16, 512), f32),
                pltpu.VMEM((SUM_ROWS, LANES), f32),
            ],
        ),
        compiler_params=pltpu.CompilerParams(vmem_limit_bytes=20 << 20),
        name="regression_sums",
    )(slab, moved, moved, weights, bias, payoff, fit)


def exchange_with_others(x, axes, count, piece_of=None):
    received = []
    for flip in range(1, count):
        sent = x if piece_of is None else piece_of(flip)
        received.append(lax.ppermute(sent, axes, [(i, i ^ flip) for i in range(count)]))
    return received


def sum_over_cores_and_z(kept, sent, beside):
    z = lax.axis_index("z")
    mine = (kept + exchange_with_others(sent, "core", 2)[0]).reshape(4, PIECE, LANES)

    def piece_of(flip):
        return lax.dynamic_index_in_dim(mine, z ^ flip, 0, False)

    parts, beside = lax.optimization_barrier((exchange_with_others(None, "z", 4, piece_of), beside))
    return (piece_of(0) + parts[0]) + (parts[1] + parts[2]), beside


def sum_of_exchange(share, axes):
    parts = exchange_with_others(share, axes, 4)
    return (share + parts[0]) + (parts[1] + parts[2])


def gathered_sum(share):
    column = jnp.stack([share] + exchange_with_others(share, "z", 4))
    return column, exchange_with_others(column, "core", 2)[0]


def lane_column(x, j):
    return jnp.broadcast_to(x[:, j:j + 1], (8, LANES))


def sublane_row(x, j):
    return jnp.broadcast_to(x[j:j + 1, :], (8, LANES))


def pivot_rows(panel, base, lane, sub):
    inside = (lane >= base) & (lane < base + 8)
    columns = [lane_column(panel, base + j) for j in range(8)]
    d = {(i, j): sublane_row(columns[j], i) for j in range(8) for i in range(j, 8)}
    marked = jnp.where(inside, jnp.where(lane - base == sub, 1.0, 0.0), panel)
    y = [sublane_row(marked, j) for j in range(8)]
    lower = {}
    inverse = []
    for j in range(8):
        inverse.append(1.0 / d[j, j])
        for i in range(j + 1, 8):
            lower[i, j] = d[i, j] * inverse[j]
        for k in range(j + 1, 8):
            for i in range(k, 8):
                d[i, k] = d[i, k] - lower[i, j] * d[k, j]
        for i in range(j + 1, 8):
            y[i] = y[i] - lower[i, j] * y[j]
    y = [y[j] * inverse[j] for j in range(8)]
    for j in range(7, -1, -1):
        for i in range(j):
            y[i] = y[i] - lower[j, i] * y[j]
    return y


def eliminated(x, rows, base, lane):
    inside = (lane >= base) & (lane < base + 8)
    t = [lane_column(x, base + j) * rows[j] for j in range(8)]
    total = ((t[0] + t[1]) + (t[2] + t[3])) + ((t[4] + t[5]) + (t[6] + t[7]))
    return jnp.where(inside, 0.0, x) - total


def inverse_of_block(rows):
    lane = lax.broadcasted_iota(jnp.int32, (8, LANES), 1)
    sub = lax.broadcasted_iota(jnp.int32, (8, LANES), 0)
    rows = list(rows)
    for g in range(16):
        pivots = pivot_rows(rows[g], 8 * g, lane, sub)
        for t in range(1, 16):
            h = (g + t) % 16
            rows[h] = eliminated(rows[h], pivots, 8 * g, lane)
        own = pivots[0]
        for j in range(1, 8):
            own = jnp.where(sub == j, pivots[j], own)
        rows[g] = own
    return rows


def solve_kernel(at_ref, near_ref, far_ref, basis_ref, out_ref, sums_ref, system_ref, *, scale):
    core = at_ref[0]
    z = at_ref[1]
    for flip in range(4):
        at = pl.multiple_of((core * 4 + (z ^ flip)) * PIECE, 8)
        sums_ref[pl.ds(at, PIECE), :] = near_ref[flip]
        at = pl.multiple_of(((1 - core) * 4 + (z ^ flip)) * PIECE, 8)
        sums_ref[pl.ds(at, PIECE), :] = far_ref[flip]
    diagonal = (
        lax.broadcasted_iota(jnp.int32, (BLOCK, BLOCK), 0)
        == lax.broadcasted_iota(jnp.int32, (BLOCK, BLOCK), 1)
    )
    for at, (i, j) in enumerate(GRAM_BLOCKS):
        block = sums_ref[at * BLOCK:(at + 1) * BLOCK, :] * scale
        if i == j:
            block = block + jnp.where(diagonal, RIDGE, 0.0)
        else:
            system_ref[j * BLOCK:(j + 1) * BLOCK, i * BLOCK:(i + 1) * BLOCK] = block.T
        system_ref[i * BLOCK:(i + 1) * BLOCK, j * BLOCK:(j + 1) * BLOCK] = block
    for i in range(4):
        row = sums_ref[MOMENT_ROW + 8 * i:MOMENT_ROW + 8 * i + 1, :] * scale
        system_ref[i * BLOCK:(i + 1) * BLOCK, 512:] = jnp.broadcast_to(row, (BLOCK, BLOCK)).T

    for i in range(4):
        lo = i * BLOCK
        inverse = inverse_of_block(
            [system_ref[lo + 8 * g:lo + 8 * g + 8, lo:lo + BLOCK] for g in range(16)]
        )
        inverse = jnp.concatenate(inverse, axis=0)
        solved = exact_dot(inverse, system_ref[lo:lo + BLOCK, lo + BLOCK:])
        for j in range(4):
            if j != i:
                system_ref[j * BLOCK:(j + 1) * BLOCK, lo + BLOCK:] -= exact_dot(
                    system_ref[j * BLOCK:(j + 1) * BLOCK, lo:lo + BLOCK], solved
                )
        system_ref[lo:lo + BLOCK, lo + BLOCK:] = solved
    width = basis_ref.shape[1]
    for lo in range(0, width, 512):
        parts = [jnp.zeros((8, 512), f32) for _ in range(4)]
        for b in range(64):
            coefficient = jnp.tile(system_ref[8 * b:8 * b + 8, 512:], (1, 4))
            parts[b % 4] += coefficient * basis_ref[8 * b:8 * b + 8, lo:lo + 512].astype(f32)
        out_ref[:, lo:lo + 512] = jnp.sum(
            (parts[0] + parts[1]) + (parts[2] + parts[3]), axis=0, keepdims=True
        )


def solve_continuation(near, far, basis, path_count):
    at = jnp.stack([lax.axis_index("core"), lax.axis_index("z")]).astype(jnp.int32)
    whole = pl.BlockSpec((4, PIECE, LANES), lambda i, s: (0, 0, 0))
    return pl.pallas_call(
        lambda *refs: solve_kernel(*refs, scale=1.0 / path_count),
        out_shape=jax.ShapeDtypeStruct((1, basis.shape[1]), f32),
        grid_spec=pltpu.PrefetchScalarGridSpec(
            num_scalar_prefetch=1,
            grid=(1,),
            in_specs=[whole, whole, pl.BlockSpec(basis.shape, lambda i, s: (0, 0))],
            out_specs=pl.BlockSpec((1, basis.shape[1]), lambda i, s: (0, 0)),
            scratch_shapes=[
                pltpu.VMEM((SUM_ROWS, LANES), f32),
                pltpu.VMEM((512, 512 + LANES), f32),
            ],
        ),
        compiler_params=pltpu.CompilerParams(vmem_limit_bytes=20 << 20),
        name="solve_continuation",
    )(at, near, far, basis)


def increments_kernel(moved_ref, mixer_ref, basket_ref, sent_ref, weights_ref, buffer_ref, copied):
    copies = []
    for tile in range(moved_ref.shape[2] // INCREMENT_TILE):
        span = pl.ds(tile * INCREMENT_TILE, INCREMENT_TILE)
        adjoint = moved_ref[:, :, span].reshape(256, INCREMENT_TILE).astype(f32)
        for date in range(STEPS - 1, -1, -1):
            gain = TIME_STEP * jnp.dot(
                mixer_ref[...], adjoint.astype(bf16), preferred_element_type=f32
            )
            buffer_ref[tile, :, date] = gain.astype(bf16).reshape(8, 32, INCREMENT_TILE)
            if date:
                adjoint = adjoint + gain
        copies.append(
            pltpu.make_async_copy(buffer_ref.at[tile], sent_ref.at[:, :, :, span], copied.at[tile])
        )
        copies[-1].start()
    lane = lax.broadcasted_iota(jnp.int32, (256, LANES), 1)
    weight = jnp.broadcast_to(basket_ref[...], (256, LANES))
    table = weight
    for later in range(1, STEPS):
        gain = sum(
            jnp.dot(mixer_ref[...], part, preferred_element_type=f32) for part in three_terms(weight)
        )
        weight = weight + TIME_STEP * gain
        table = jnp.where(lane == later, weight, table)
    weights_ref[...] = table
    for copy in copies:
        copy.wait()


def increments(moved, mixer, basket, slab_part):
    tiles = slab_part // INCREMENT_TILE
    return pl.pallas_call(
        increments_kernel,
        out_shape=(
            pltpu.HBM((8, STEPS, 32, slab_part), bf16),
            jax.ShapeDtypeStruct((256, LANES), f32),
        ),
        out_specs=(
            pl.BlockSpec(memory_space=pltpu.HBM),
            pl.BlockSpec(memory_space=pltpu.VMEM),
        ),
        scratch_shapes=[
            pltpu.VMEM((tiles, 8, STEPS, 32, INCREMENT_TILE), bf16),
            pltpu.SemaphoreType.DMA((tiles,)),
        ],
        compiler_params=pltpu.CompilerParams(vmem_limit_bytes=20 << 20),
        name="increments",
    )(moved, mixer, basket)


def surface_kernel(slab_ref, *refs):
    continuation_refs = refs[:4]
    (cotangent_ref, gain_ref, shock_ref, weight_ref, exercise_ref, bucket_ref, delta_ref, share_ref,
     continuation_ref, total_ref) = refs[4:]
    step = pl.program_id(0)

    @pl.when(step == 0)
    def _():
        for flip in range(8):
            continuation_ref[pl.ds(slab_ref[0] ^ flip, 1), :] = continuation_refs[flip // 2][
                flip % 2:flip % 2 + 1, :
            ]
        total_ref[...] = jnp.zeros(total_ref.shape, f32)

    continuation = continuation_ref[pl.ds(step, 1), :]
    held = [exercise_ref[date:date + 1, :].astype(f32) * continuation for date in range(STEPS)]
    weights = [weight_ref[:, later:later + 1] for later in range(STEPS)]
    strikes = lax.broadcasted_iota(jnp.int32, (STRIKE_ROWS, DATE_TILE), 0).astype(f32).astype(bf16)
    base = cotangent_ref[...].astype(f32)
    total = total_ref[...]
    for date in range(STEPS - 1, -1, -1):
        base = base + gain_ref[0, date].astype(f32)
        adjoint = base
        for later in range(STEPS - date):
            adjoint = adjoint + held[date + later] * weights[later]
        terms = (adjoint * shock_ref[date].astype(f32)).astype(bf16).astype(f32)
        bucket = bucket_ref[date:date + 1, :]
        column = (bucket & (STRIKE_ROWS - 1)).astype(f32).astype(bf16)
        chosen = jnp.where(strikes == column, jnp.bfloat16(1), jnp.bfloat16(0))
        group = bucket >> STRIKE_BITS
        terms = jnp.concatenate(
            [jnp.where(group == g, terms, 0.0).astype(bf16) for g in range(NK // STRIKE_ROWS)], axis=0
        )
        total = total + lax.dot_general(
            chosen, terms, (((1,), (1,)), ((), ())), preferred_element_type=f32
        )
    delta_ref[...] = adjoint
    total_ref[...] = total

    @pl.when(step == pl.num_programs(0) - 1)
    def _():
        owners = STRIKE_ROWS // 16
        for g in range(NK // STRIKE_ROWS):
            grouped = total[:, 32 * g:32 * g + 32].reshape(owners, 16, 32)
            for q in range(4):
                share_ref[g * owners:(g + 1) * owners, :, 32 * q:32 * q + 32] = grouped[
                    :, 4 * q:4 * q + 4, :
                ]


def surface_and_delta(slab, continuations, cotangent, gains, shocks, weights, exercise, bucket):
    local_paths = cotangent.shape[1]
    whole = pl.BlockSpec((2, DATE_TILE), lambda i, s: (0, 0))
    return pl.pallas_call(
        surface_kernel,
        out_shape=(
            jax.ShapeDtypeStruct((32, local_paths), f32),
            jax.ShapeDtypeStruct((16, 4, LANES), f32),
        ),
        grid_spec=pltpu.PrefetchScalarGridSpec(
            num_scalar_prefetch=1,
            grid=(local_paths // DATE_TILE,),
            in_specs=[whole] * 4 + [
                pl.BlockSpec((32, DATE_TILE), lambda i, s: (0, i)),
                pl.BlockSpec((1, STEPS, 32, DATE_TILE), lambda i, s: (i, 0, 0, 0)),
                pl.BlockSpec((STEPS, 32, DATE_TILE), lambda i, s: (0, 0, i)),
                pl.BlockSpec((32, LANES), lambda i, s: (s[0], 0)),
                pl.BlockSpec((STEPS, DATE_TILE), lambda i, s: (0, i)),
                pl.BlockSpec((STEPS, DATE_TILE), lambda i, s: (0, i)),
            ],
            out_specs=(
                pl.BlockSpec((32, DATE_TILE), lambda i, s: (0, i)),
                pl.BlockSpec((16, 4, LANES), lambda i, s: (0, 0, 0)),
            ),
            scratch_shapes=[pltpu.VMEM((8, DATE_TILE), f32), pltpu.VMEM((STRIKE_ROWS, 32 * (NK // STRIKE_ROWS)), f32)],
        ),
        compiler_params=pltpu.CompilerParams(vmem_limit_bytes=32 << 20),
        name="surface_and_delta",
    )(slab, *continuations, cotangent, gains, shocks, weights, exercise, bucket)


def per_device(prices, loadings, basis_w, basis_bias, payoff, in_fit, cotangent, shocks, corr_gen,
               basket, exercise, bucket):
    local_paths = prices.shape[1]
    slab_part = local_paths // 8
    path_count = float(local_paths * 16)
    slab = lax.axis_index(STOCK_AXES).astype(jnp.int32).reshape(1)

    pieces = jnp.moveaxis(prices.reshape(32, 8, slab_part), 1, 0)
    table = jnp.broadcast_to(jnp.pad(loadings, ((0, 0), (0, LANES - 32)))[None], (8, 32, LANES))
    moved_prices = lax.all_to_all(
        jnp.concatenate([pieces, table], axis=2), STOCK_AXES, 0, 0, tiled=True
    )
    slabs = jnp.moveaxis(cotangent.reshape(32, 8, slab_part), 1, 0)
    small = (basis_w, basis_bias[:, None], payoff[None, :], in_fit[None, :],
             basket[:, None])
    slabs, moved_prices, small = lax.optimization_barrier((slabs, moved_prices, small))
    basis_w, bias, payoff, in_fit, basket = small
    moved = lax.all_to_all(slabs, STOCK_AXES, 0, 0, tiled=True)
    basis_w = pltpu.with_memory_space_constraint(basis_w, pltpu.HBM)
    in_fit = pltpu.with_memory_space_constraint(in_fit, pltpu.HBM)
    place = jnp.stack([slab[0], lax.axis_index("core").astype(jnp.int32)])
    basis, kept, other = regression_sums(
        place, moved_prices, basis_w, bias, payoff, in_fit, slab_part
    )
    share, moved = sum_over_cores_and_z(kept, other, moved)
    sent, weights = increments(moved, corr_gen, basket, slab_part)
    share = sum_of_exchange(share, "x")
    parts = exchange_with_others(share, ("ylo", "yhi"), 4)
    parts, sent = lax.optimization_barrier((parts, sent))
    share = (share + parts[0]) + (parts[1] + parts[2])
    gains = lax.all_to_all(sent, STOCK_AXES, 0, 0, tiled=True)
    near, far = gathered_sum(share)
    continuation = solve_continuation(near, far, basis, path_count)
    pair = jnp.concatenate([continuation] + exchange_with_others(continuation, "yhi", 2), axis=0)
    continuations = [pair] + exchange_with_others(pair, "x", 4)
    delta, surface = surface_and_delta(
        slab, continuations, cotangent, gains, shocks, weights, exercise, bucket
    )
    surface = lax.all_to_all(surface, PATH_AXES, 0, 0, tiled=True)
    surface = jnp.sum(surface, axis=0).reshape(4, 4, 32)
    surface = jnp.transpose(surface, (2, 1, 0)).reshape(32, 16)
    return delta, surface


def solution(mesh):
    fine = Mesh(mesh.devices.reshape(FINE), ALL_AXES)
    stocks, paths = STOCK_AXES, PATH_AXES
    return jax.shard_map(
        per_device,
        mesh=fine,
        in_specs=(
            P(stocks, paths),
            P(stocks, None),
            P(),
            P(),
            P(paths),
            P(paths),
            P(stocks, paths),
            P(None, stocks, paths),
            P(),
            P(),
            P(None, paths),
            P(None, paths),
        ),
        out_specs=(P(stocks, paths), P(stocks, paths)),
        check_vma=False,
    )
```

```python
import jax
import jax.numpy as jnp
from jax import lax
from jax.experimental import pallas as pl
from jax.experimental.pallas import tpu as pltpu
from jax.sharding import Mesh
from jax.sharding import PartitionSpec as P

NK = 256
STEPS = 4
TIME_STEP = 0.25
RIDGE = 0.1
LANES = 128
BLOCK = 128
TILE = 2048
INCREMENT_TILE = 1024
DATE_TILE = 2048
STRIKE_BITS = 7
STRIKE_ROWS = 1 << STRIKE_BITS
PATH_AXES = ("z", "ylo", "core")
STOCK_AXES = ("x", "yhi")
ALL_AXES = PATH_AXES + STOCK_AXES
FINE = (4, 2, 2, 4, 2)
f32 = jnp.float32
bf16 = jnp.bfloat16


def three_terms(x):
    high = x.astype(bf16)
    rest = x - high.astype(f32)
    middle = rest.astype(bf16)
    low = (rest - middle.astype(f32)).astype(bf16)
    return high, middle, low


def left_terms(x, axis):
    high, middle, low = three_terms(x)
    return jnp.concatenate([high, high, middle, high, low, middle], axis=axis)


def right_terms(x, axis):
    high, middle, low = three_terms(x)
    return jnp.concatenate([high, middle, high, low, high, middle], axis=axis)


def exact_dot(left, right):
    return jnp.dot(left_terms(left, 1), right_terms(right, 0), preferred_element_type=f32)


GRAM_BLOCKS = tuple((i, j) for i in range(4) for j in range(i + 1))
MOMENT_ROW = len(GRAM_BLOCKS) * BLOCK
SUM_ROWS = 1344
PIECE = SUM_ROWS // 8


def gram_kernel(slab_ref, moved_ref, table_ref, weight_ref, bias_ref, payoff_ref, fit_ref,
                basis_ref, kept_ref, sent_ref, gram_ref, moment_ref, sums_ref):
    step = pl.program_id(0)
    tile = moved_ref[...].reshape(256, TILE)
    loads = table_ref[...].reshape(256, LANES)[:, :32]
    factors = lax.dot_general(loads, tile, (((0,), (0,)), ((), ())), preferred_element_type=f32)
    raised = lax.dot_general(
        left_terms(weight_ref[...], 0), right_terms(factors, 0), (((0,), (0,)), ((), ())), preferred_element_type=f32
    )
    basis = jnp.tanh(raised + bias_ref[...]).astype(bf16)
    basis_ref[...] = basis
    picked = basis * fit_ref[...].astype(f32).astype(bf16)
    paid = jnp.broadcast_to(payoff_ref[...].astype(f32), (16, TILE)).astype(bf16)
    contract = (((1,), (1,)), ((), ()))
    first = lax.dot_general(picked[:256], basis[:256], contract, preferred_element_type=f32)
    second = lax.dot_general(picked[256:], basis, contract, preferred_element_type=f32)
    moment = lax.dot_general(paid, picked, contract, preferred_element_type=f32)

    @pl.when(step == 0)
    def _():
        gram_ref[:256, :256] = first
        gram_ref[256:, :] = second
        moment_ref[...] = moment

    @pl.when(step > 0)
    def _():
        gram_ref[:256, :256] += first
        gram_ref[256:, :] += second
        moment_ref[...] += moment

    @pl.when(step == pl.num_programs(0) - 1)
    def _():
        for at, (i, j) in enumerate(GRAM_BLOCKS):
            sums_ref[at * BLOCK:(at + 1) * BLOCK, :] = gram_ref[
                i * BLOCK:(i + 1) * BLOCK, j * BLOCK:(j + 1) * BLOCK
            ]
        sums_ref[MOMENT_ROW:, :] = jnp.zeros((SUM_ROWS - MOMENT_ROW, LANES), f32)
        for i in range(4):
            sums_ref[MOMENT_ROW + 8 * i:MOMENT_ROW + 8 * i + 8, :] = moment_ref[
                :8, i * BLOCK:(i + 1) * BLOCK
            ]
        half = 4 * PIECE
        kept_ref[...] = sums_ref[pl.ds(pl.multiple_of(slab_ref[1] * half, 8), half), :]
        sent_ref[...] = sums_ref[pl.ds(pl.multiple_of((1 - slab_ref[1]) * half, 8), half), :]


def regression_sums(slab, moved, weights, bias, payoff, fit, slab_part):
    tiles = slab_part // TILE
    table_at = slab_part // LANES

    def own(step, slab_ref):
        return (0, slab_ref[0] * tiles + step)

    return pl.pallas_call(
        gram_kernel,
        out_shape=(
            pltpu.HBM((512, slab_part), bf16),
            pltpu.HBM((SUM_ROWS // 2, LANES), f32),
            pltpu.HBM((SUM_ROWS // 2, LANES), f32),
        ),
        grid_spec=pltpu.PrefetchScalarGridSpec(
            num_scalar_prefetch=1,
            grid=(tiles,),
            in_specs=[
                pl.BlockSpec((8, 32, TILE), lambda i, s: (0, 0, i)),
                pl.BlockSpec((8, 32, LANES), lambda i, s: (0, 0, table_at)),
                pl.BlockSpec((32, 512), lambda i, s: (0, 0)),
                pl.BlockSpec((512, 1), lambda i, s: (0, 0)),
                pl.BlockSpec((1, TILE), own),
                pl.BlockSpec((1, TILE), own),
            ],
            out_specs=(
                pl.BlockSpec((512, TILE), lambda i, s: (0, i)),
                pl.BlockSpec((SUM_ROWS // 2, LANES), lambda i, s: (0, 0)),
                pl.BlockSpec((SUM_ROWS // 2, LANES), lambda i, s: (0, 0)),
            ),
            scratch_shapes=[
                pltpu.VMEM((512, 512), f32),
                pltpu.VMEM((16, 512), f32),
                pltpu.VMEM((SUM_ROWS, LANES), f32),
            ],
        ),
        compiler_params=pltpu.CompilerParams(vmem_limit_bytes=20 << 20),
        name="regression_sums",
    )(slab, moved, moved, weights, bias, payoff, fit)


def exchange_with_others(x, axes, count, piece_of=None):
    received = []
    for flip in range(1, count):
        sent = x if piece_of is None else piece_of(flip)
        received.append(lax.ppermute(sent, axes, [(i, i ^ flip) for i in range(count)]))
    return received


def sum_over_cores_and_z(kept, sent, beside):
    z = lax.axis_index("z")
    mine = (kept + exchange_with_others(sent, "core", 2)[0]).reshape(4, PIECE, LANES)

    def piece_of(flip):
        return lax.dynamic_index_in_dim(mine, z ^ flip, 0, False)

    parts, beside = lax.optimization_barrier((exchange_with_others(None, "z", 4, piece_of), beside))
    return (piece_of(0) + parts[0]) + (parts[1] + parts[2]), beside


def sum_of_exchange(share, axes):
    parts = exchange_with_others(share, axes, 4)
    return (share + parts[0]) + (parts[1] + parts[2])


def gathered_sum(share):
    column = jnp.stack([share] + exchange_with_others(share, "z", 4))
    return column, exchange_with_others(column, "core", 2)[0]


def lane_column(x, j):
    return jnp.broadcast_to(x[:, j:j + 1], (8, LANES))


def sublane_row(x, j):
    return jnp.broadcast_to(x[j:j + 1, :], (8, LANES))


def pivot_rows(panel, base, lane, sub):
    inside = (lane >= base) & (lane < base + 8)
    columns = [lane_column(panel, base + j) for j in range(8)]
    d = {(i, j): sublane_row(columns[j], i) for j in range(8) for i in range(j, 8)}
    marked = jnp.where(inside, jnp.where(lane - base == sub, 1.0, 0.0), panel)
    y = [sublane_row(marked, j) for j in range(8)]
    lower = {}
    inverse = []
    for j in range(8):
        inverse.append(1.0 / d[j, j])
        for i in range(j + 1, 8):
            lower[i, j] = d[i, j] * inverse[j]
        for k in range(j + 1, 8):
            for i in range(k, 8):
                d[i, k] = d[i, k] - lower[i, j] * d[k, j]
        for i in range(j + 1, 8):
            y[i] = y[i] - lower[i, j] * y[j]
    y = [y[j] * inverse[j] for j in range(8)]
    for j in range(7, -1, -1):
        for i in range(j):
            y[i] = y[i] - lower[j, i] * y[j]
    return y


def eliminated(x, rows, base, lane):
    inside = (lane >= base) & (lane < base + 8)
    t = [lane_column(x, base + j) * rows[j] for j in range(8)]
    total = ((t[0] + t[1]) + (t[2] + t[3])) + ((t[4] + t[5]) + (t[6] + t[7]))
    return jnp.where(inside, 0.0, x) - total


def inverse_of_block(rows):
    lane = lax.broadcasted_iota(jnp.int32, (8, LANES), 1)
    sub = lax.broadcasted_iota(jnp.int32, (8, LANES), 0)
    rows = list(rows)
    for g in range(16):
        pivots = pivot_rows(rows[g], 8 * g, lane, sub)
        for t in range(1, 16):
            h = (g + t) % 16
            rows[h] = eliminated(rows[h], pivots, 8 * g, lane)
        own = pivots[0]
        for j in range(1, 8):
            own = jnp.where(sub == j, pivots[j], own)
        rows[g] = own
    return rows


def solve_kernel(at_ref, near_ref, far_ref, basis_ref, out_ref, sums_ref, system_ref, *, scale):
    core = at_ref[0]
    z = at_ref[1]
    for flip in range(4):
        at = pl.multiple_of((core * 4 + (z ^ flip)) * PIECE, 8)
        sums_ref[pl.ds(at, PIECE), :] = near_ref[flip]
        at = pl.multiple_of(((1 - core) * 4 + (z ^ flip)) * PIECE, 8)
        sums_ref[pl.ds(at, PIECE), :] = far_ref[flip]
    diagonal = (
        lax.broadcasted_iota(jnp.int32, (BLOCK, BLOCK), 0)
        == lax.broadcasted_iota(jnp.int32, (BLOCK, BLOCK), 1)
    )
    for at, (i, j) in enumerate(GRAM_BLOCKS):
        block = sums_ref[at * BLOCK:(at + 1) * BLOCK, :] * scale
        if i == j:
            block = block + jnp.where(diagonal, RIDGE, 0.0)
        else:
            system_ref[j * BLOCK:(j + 1) * BLOCK, i * BLOCK:(i + 1) * BLOCK] = block.T
        system_ref[i * BLOCK:(i + 1) * BLOCK, j * BLOCK:(j + 1) * BLOCK] = block
    for i in range(4):
        row = sums_ref[MOMENT_ROW + 8 * i:MOMENT_ROW + 8 * i + 1, :] * scale
        system_ref[i * BLOCK:(i + 1) * BLOCK, 512:] = jnp.broadcast_to(row, (BLOCK, BLOCK)).T

    for i in range(4):
        lo = i * BLOCK
        inverse = inverse_of_block(
            [system_ref[lo + 8 * g:lo + 8 * g + 8, lo:lo + BLOCK] for g in range(16)]
        )
        inverse = jnp.concatenate(inverse, axis=0)
        solved = exact_dot(inverse, system_ref[lo:lo + BLOCK, lo + BLOCK:])
        for j in range(4):
            if j != i:
                system_ref[j * BLOCK:(j + 1) * BLOCK, lo + BLOCK:] -= exact_dot(
                    system_ref[j * BLOCK:(j + 1) * BLOCK, lo:lo + BLOCK], solved
                )
        system_ref[lo:lo + BLOCK, lo + BLOCK:] = solved
    width = basis_ref.shape[1]
    for lo in range(0, width, 512):
        parts = [jnp.zeros((8, 512), f32) for _ in range(4)]
        for b in range(64):
            coefficient = jnp.tile(system_ref[8 * b:8 * b + 8, 512:], (1, 4))
            parts[b % 4] += coefficient * basis_ref[8 * b:8 * b + 8, lo:lo + 512].astype(f32)
        out_ref[:, lo:lo + 512] = jnp.sum(
            (parts[0] + parts[1]) + (parts[2] + parts[3]), axis=0, keepdims=True
        )


def solve_continuation(near, far, basis, path_count):
    at = jnp.stack([lax.axis_index("core"), lax.axis_index("z")]).astype(jnp.int32)
    whole = pl.BlockSpec((4, PIECE, LANES), lambda i, s: (0, 0, 0))
    return pl.pallas_call(
        lambda *refs: solve_kernel(*refs, scale=1.0 / path_count),
        out_shape=jax.ShapeDtypeStruct((1, basis.shape[1]), f32),
        grid_spec=pltpu.PrefetchScalarGridSpec(
            num_scalar_prefetch=1,
            grid=(1,),
            in_specs=[whole, whole, pl.BlockSpec(basis.shape, lambda i, s: (0, 0))],
            out_specs=pl.BlockSpec((1, basis.shape[1]), lambda i, s: (0, 0)),
            scratch_shapes=[
                pltpu.VMEM((SUM_ROWS, LANES), f32),
                pltpu.VMEM((512, 512 + LANES), f32),
            ],
        ),
        compiler_params=pltpu.CompilerParams(vmem_limit_bytes=20 << 20),
        name="solve_continuation",
    )(at, near, far, basis)


def in_hbm(x):
    return pltpu.with_memory_space_constraint(x, pltpu.HBM)


def increments_kernel(moved_ref, mixer_ref, basket_ref, sent_ref, weights_ref, buffer_ref, copied):
    copies = []
    for tile in range(moved_ref.shape[2] // INCREMENT_TILE):
        span = pl.ds(tile * INCREMENT_TILE, INCREMENT_TILE)
        adjoint = moved_ref[:, :, span].reshape(256, INCREMENT_TILE).astype(f32)
        for date in range(STEPS - 1, -1, -1):
            gain = TIME_STEP * jnp.dot(
                mixer_ref[...], adjoint.astype(bf16), preferred_element_type=f32
            )
            buffer_ref[tile, :, date] = gain.astype(bf16).reshape(8, 32, INCREMENT_TILE)
            if date:
                adjoint = adjoint + gain
        copies.append(
            pltpu.make_async_copy(buffer_ref.at[tile], sent_ref.at[:, :, :, span], copied.at[tile])
        )
        copies[-1].start()
    lane = lax.broadcasted_iota(jnp.int32, (256, LANES), 1)
    weight = jnp.broadcast_to(basket_ref[...], (256, LANES))
    table = weight
    for later in range(1, STEPS):
        gain = sum(
            jnp.dot(mixer_ref[...], part, preferred_element_type=f32) for part in three_terms(weight)
        )
        weight = weight + TIME_STEP * gain
        table = jnp.where(lane == later, weight, table)
    weights_ref[...] = table
    for copy in copies:
        copy.wait()


def increments(moved, mixer, basket, slab_part):
    tiles = slab_part // INCREMENT_TILE
    return pl.pallas_call(
        increments_kernel,
        out_shape=(
            pltpu.HBM((8, STEPS, 32, slab_part), bf16),
            jax.ShapeDtypeStruct((256, LANES), f32),
        ),
        out_specs=(
            pl.BlockSpec(memory_space=pltpu.HBM),
            pl.BlockSpec(memory_space=pltpu.VMEM),
        ),
        scratch_shapes=[
            pltpu.VMEM((tiles, 8, STEPS, 32, INCREMENT_TILE), bf16),
            pltpu.SemaphoreType.DMA((tiles,)),
        ],
        compiler_params=pltpu.CompilerParams(vmem_limit_bytes=20 << 20),
        name="increments",
    )(moved, mixer, basket)


def surface_kernel(slab_ref, *refs):
    continuation_refs = refs[:4]
    (cotangent_ref, gain_ref, shock_ref, weight_ref, exercise_ref, bucket_ref, delta_ref, share_ref,
     continuation_ref, total_ref) = refs[4:]
    step = pl.program_id(0)

    @pl.when(step == 0)
    def _():
        for flip in range(8):
            continuation_ref[pl.ds(slab_ref[0] ^ flip, 1), :] = continuation_refs[flip // 2][
                flip % 2:flip % 2 + 1, :
            ]
        total_ref[...] = jnp.zeros(total_ref.shape, f32)

    continuation = continuation_ref[pl.ds(step, 1), :]
    held = [exercise_ref[date:date + 1, :].astype(f32) * continuation for date in range(STEPS)]
    weights = [weight_ref[:, later:later + 1] for later in range(STEPS)]
    strikes = lax.broadcasted_iota(jnp.int32, (STRIKE_ROWS, DATE_TILE), 0).astype(f32).astype(bf16)
    base = cotangent_ref[...].astype(f32)
    total = total_ref[...]
    for date in range(STEPS - 1, -1, -1):
        base = base + gain_ref[0, date].astype(f32)
        adjoint = base
        for later in range(STEPS - date):
            adjoint = adjoint + held[date + later] * weights[later]
        terms = (adjoint * shock_ref[date].astype(f32)).astype(bf16).astype(f32)
        bucket = bucket_ref[date:date + 1, :]
        column = (bucket & (STRIKE_ROWS - 1)).astype(f32).astype(bf16)
        chosen = jnp.where(strikes == column, jnp.bfloat16(1), jnp.bfloat16(0))
        group = bucket >> STRIKE_BITS
        terms = jnp.concatenate(
            [jnp.where(group == g, terms, 0.0).astype(bf16) for g in range(NK // STRIKE_ROWS)], axis=0
        )
        total = total + lax.dot_general(
            chosen, terms, (((1,), (1,)), ((), ())), preferred_element_type=f32
        )
    delta_ref[...] = adjoint
    total_ref[...] = total

    @pl.when(step == pl.num_programs(0) - 1)
    def _():
        owners = STRIKE_ROWS // 16
        for g in range(NK // STRIKE_ROWS):
            grouped = total[:, 32 * g:32 * g + 32].reshape(owners, 16, 32)
            for q in range(4):
                share_ref[g * owners:(g + 1) * owners, :, 32 * q:32 * q + 32] = grouped[
                    :, 4 * q:4 * q + 4, :
                ]


def surface_and_delta(slab, continuations, cotangent, gains, shocks, weights, exercise, bucket):
    local_paths = cotangent.shape[1]
    whole = pl.BlockSpec((2, DATE_TILE), lambda i, s: (0, 0))
    return pl.pallas_call(
        surface_kernel,
        out_shape=(
            jax.ShapeDtypeStruct((32, local_paths), f32),
            jax.ShapeDtypeStruct((16, 4, LANES), f32),
        ),
        grid_spec=pltpu.PrefetchScalarGridSpec(
            num_scalar_prefetch=1,
            grid=(local_paths // DATE_TILE,),
            in_specs=[whole] * 4 + [
                pl.BlockSpec((32, DATE_TILE), lambda i, s: (0, i)),
                pl.BlockSpec((1, STEPS, 32, DATE_TILE), lambda i, s: (i, 0, 0, 0)),
                pl.BlockSpec((STEPS, 32, DATE_TILE), lambda i, s: (0, 0, i)),
                pl.BlockSpec((32, LANES), lambda i, s: (s[0], 0)),
                pl.BlockSpec((STEPS, DATE_TILE), lambda i, s: (0, i)),
                pl.BlockSpec((STEPS, DATE_TILE), lambda i, s: (0, i)),
            ],
            out_specs=(
                pl.BlockSpec((32, DATE_TILE), lambda i, s: (0, i)),
                pl.BlockSpec((16, 4, LANES), lambda i, s: (0, 0, 0)),
            ),
            scratch_shapes=[pltpu.VMEM((8, DATE_TILE), f32), pltpu.VMEM((STRIKE_ROWS, 32 * (NK // STRIKE_ROWS)), f32)],
        ),
        compiler_params=pltpu.CompilerParams(vmem_limit_bytes=32 << 20),
        name="surface_and_delta",
    )(slab, *continuations, cotangent, gains, in_hbm(shocks), weights, exercise, bucket)


def per_device(prices, loadings, basis_w, basis_bias, payoff, in_fit, cotangent, shocks, corr_gen,
               basket, exercise, bucket):
    local_paths = prices.shape[1]
    slab_part = local_paths // 8
    path_count = float(local_paths * 16)
    slab = lax.axis_index(STOCK_AXES).astype(jnp.int32).reshape(1)

    pieces = jnp.moveaxis(prices.reshape(32, 8, slab_part), 1, 0)
    table = jnp.broadcast_to(jnp.pad(loadings, ((0, 0), (0, LANES - 32)))[None], (8, 32, LANES))
    moved_prices = lax.all_to_all(
        jnp.concatenate([pieces, table], axis=2), STOCK_AXES, 0, 0, tiled=True
    )
    slabs = jnp.moveaxis(cotangent.reshape(32, 8, slab_part), 1, 0)
    small = (basis_w, basis_bias[:, None], payoff[None, :], in_fit[None, :],
             basket[:, None])
    slabs, moved_prices, small = lax.optimization_barrier((slabs, moved_prices, small))
    basis_w, bias, payoff, in_fit, basket = small
    moved = lax.all_to_all(slabs, STOCK_AXES, 0, 0, tiled=True)
    basis_w = in_hbm(basis_w)
    in_fit = in_hbm(in_fit)
    place = jnp.stack([slab[0], lax.axis_index("core").astype(jnp.int32)])
    basis, kept, other = regression_sums(
        place, moved_prices, basis_w, bias, payoff, in_fit, slab_part
    )
    share, moved = sum_over_cores_and_z(kept, other, moved)
    sent, weights = increments(moved, corr_gen, basket, slab_part)
    share = sum_of_exchange(share, "x")
    parts = exchange_with_others(share, ("ylo", "yhi"), 4)
    parts, sent = lax.optimization_barrier((parts, sent))
    share = (share + parts[0]) + (parts[1] + parts[2])
    gains = lax.all_to_all(sent, STOCK_AXES, 0, 0, tiled=True)
    near, far = gathered_sum(share)
    continuation = solve_continuation(near, far, basis, path_count)
    pair = jnp.concatenate([continuation] + exchange_with_others(continuation, "yhi", 2), axis=0)
    continuations = [pair] + exchange_with_others(pair, "x", 4)
    delta, surface = surface_and_delta(
        slab, continuations, cotangent, gains, shocks, weights, exercise, bucket
    )
    surface = lax.all_to_all(surface, PATH_AXES, 0, 0, tiled=True)
    surface = jnp.sum(surface, axis=0).reshape(4, 4, 32)
    surface = jnp.transpose(surface, (2, 1, 0)).reshape(32, 16)
    return delta, surface


def solution(mesh):
    fine = Mesh(mesh.devices.reshape(FINE), ALL_AXES)
    stocks, paths = STOCK_AXES, PATH_AXES
    return jax.shard_map(
        per_device,
        mesh=fine,
        in_specs=(
            P(stocks, paths),
            P(stocks, None),
            P(),
            P(),
            P(paths),
            P(paths),
            P(stocks, paths),
            P(None, stocks, paths),
            P(),
            P(),
            P(None, paths),
            P(None, paths),
        ),
        out_specs=(P(stocks, paths), P(stocks, paths)),
        check_vma=False,
    )
```

```python
import jax
import jax.numpy as jnp
from jax import lax
from jax.experimental import pallas as pl
from jax.experimental.pallas import tpu as pltpu
from jax.sharding import Mesh
from jax.sharding import PartitionSpec as P

NK = 256
STEPS = 4
TIME_STEP = 0.25
RIDGE = 0.1
LANES = 128
BLOCK = 128
TILE = 2048
INCREMENT_TILE = 1024
DATE_TILE = 2048
STRIKE_BITS = 7
STRIKE_ROWS = 1 << STRIKE_BITS
PATH_AXES = ("z", "ylo", "core")
STOCK_AXES = ("x", "yhi")
ALL_AXES = PATH_AXES + STOCK_AXES
FINE = (4, 2, 2, 4, 2)
f32 = jnp.float32
bf16 = jnp.bfloat16


def three_terms(x):
    high = x.astype(bf16)
    rest = x - high.astype(f32)
    middle = rest.astype(bf16)
    low = (rest - middle.astype(f32)).astype(bf16)
    return high, middle, low


def left_terms(x, axis):
    high, middle, low = three_terms(x)
    return jnp.concatenate([high, high, middle, high, low, middle], axis=axis)


def right_terms(x, axis):
    high, middle, low = three_terms(x)
    return jnp.concatenate([high, middle, high, low, high, middle], axis=axis)


def exact_dot(left, right):
    return jnp.dot(left_terms(left, 1), right_terms(right, 0), preferred_element_type=f32)


GRAM_BLOCKS = tuple((i, j) for i in range(4) for j in range(i + 1))
MOMENT_ROW = len(GRAM_BLOCKS) * BLOCK
SUM_ROWS = 1344
PIECE = SUM_ROWS // 8


def gram_kernel(slab_ref, moved_ref, table_ref, weight_ref, bias_ref, payoff_ref, fit_ref,
                basis_ref, kept_ref, sent_ref, gram_ref, moment_ref, sums_ref):
    step = pl.program_id(0)
    tile = moved_ref[...].reshape(256, TILE)
    loads = table_ref[...].reshape(256, LANES)[:, :32]
    factors = lax.dot_general(loads, tile, (((0,), (0,)), ((), ())), preferred_element_type=f32)
    raised = lax.dot_general(
        left_terms(weight_ref[...], 0), right_terms(factors, 0), (((0,), (0,)), ((), ())), preferred_element_type=f32
    )
    basis = jnp.tanh(raised + bias_ref[...]).astype(bf16)
    basis_ref[...] = basis
    picked = basis * fit_ref[...].astype(f32).astype(bf16)
    paid = jnp.broadcast_to(payoff_ref[...].astype(f32), (16, TILE)).astype(bf16)
    contract = (((1,), (1,)), ((), ()))
    first = lax.dot_general(picked[:256], basis[:256], contract, preferred_element_type=f32)
    second = lax.dot_general(picked[256:], basis, contract, preferred_element_type=f32)
    moment = lax.dot_general(paid, picked, contract, preferred_element_type=f32)

    @pl.when(step == 0)
    def _():
        gram_ref[:256, :256] = first
        gram_ref[256:, :] = second
        moment_ref[...] = moment

    @pl.when(step > 0)
    def _():
        gram_ref[:256, :256] += first
        gram_ref[256:, :] += second
        moment_ref[...] += moment

    @pl.when(step == pl.num_programs(0) - 1)
    def _():
        for at, (i, j) in enumerate(GRAM_BLOCKS):
            sums_ref[at * BLOCK:(at + 1) * BLOCK, :] = gram_ref[
                i * BLOCK:(i + 1) * BLOCK, j * BLOCK:(j + 1) * BLOCK
            ]
        sums_ref[MOMENT_ROW:, :] = jnp.zeros((SUM_ROWS - MOMENT_ROW, LANES), f32)
        for i in range(4):
            sums_ref[MOMENT_ROW + 8 * i:MOMENT_ROW + 8 * i + 8, :] = moment_ref[
                :8, i * BLOCK:(i + 1) * BLOCK
            ]
        half = 4 * PIECE
        kept_ref[...] = sums_ref[pl.ds(pl.multiple_of(slab_ref[1] * half, 8), half), :]
        sent_ref[...] = sums_ref[pl.ds(pl.multiple_of((1 - slab_ref[1]) * half, 8), half), :]


def regression_sums(slab, moved, weights, bias, payoff, fit, slab_part):
    tiles = slab_part // TILE
    table_at = slab_part // LANES

    def own(step, slab_ref):
        return (0, slab_ref[0] * tiles + step)

    return pl.pallas_call(
        gram_kernel,
        out_shape=(
            pltpu.HBM((512, slab_part), bf16),
            pltpu.HBM((SUM_ROWS // 2, LANES), f32),
            pltpu.HBM((SUM_ROWS // 2, LANES), f32),
        ),
        grid_spec=pltpu.PrefetchScalarGridSpec(
            num_scalar_prefetch=1,
            grid=(tiles,),
            in_specs=[
                pl.BlockSpec((8, 32, TILE), lambda i, s: (0, 0, i)),
                pl.BlockSpec((8, 32, LANES), lambda i, s: (0, 0, table_at)),
                pl.BlockSpec((32, 512), lambda i, s: (0, 0)),
                pl.BlockSpec((512, 1), lambda i, s: (0, 0)),
                pl.BlockSpec((1, TILE), own),
                pl.BlockSpec((1, TILE), own),
            ],
            out_specs=(
                pl.BlockSpec((512, TILE), lambda i, s: (0, i)),
                pl.BlockSpec((SUM_ROWS // 2, LANES), lambda i, s: (0, 0)),
                pl.BlockSpec((SUM_ROWS // 2, LANES), lambda i, s: (0, 0)),
            ),
            scratch_shapes=[
                pltpu.VMEM((512, 512), f32),
                pltpu.VMEM((16, 512), f32),
                pltpu.VMEM((SUM_ROWS, LANES), f32),
            ],
        ),
        compiler_params=pltpu.CompilerParams(vmem_limit_bytes=20 << 20),
        name="regression_sums",
    )(slab, moved, moved, weights, bias, payoff, fit)


def exchange_with_others(x, axes, count, piece_of=None):
    received = []
    for flip in range(1, count):
        sent = x if piece_of is None else piece_of(flip)
        received.append(lax.ppermute(sent, axes, [(i, i ^ flip) for i in range(count)]))
    return received


def sum_over_cores_and_z(kept, sent, beside):
    z = lax.axis_index("z")
    mine = (kept + exchange_with_others(sent, "core", 2)[0]).reshape(4, PIECE, LANES)

    def piece_of(flip):
        return lax.dynamic_index_in_dim(mine, z ^ flip, 0, False)

    parts, beside = lax.optimization_barrier((exchange_with_others(None, "z", 4, piece_of), beside))
    return (piece_of(0) + parts[0]) + (parts[1] + parts[2]), beside


def sum_of_exchange(share, axes):
    parts = exchange_with_others(share, axes, 4)
    return (share + parts[0]) + (parts[1] + parts[2])


def gathered_sum(share):
    column = jnp.stack([share] + exchange_with_others(share, "z", 4))
    return column, exchange_with_others(column, "core", 2)[0]


def lane_column(x, j):
    return jnp.broadcast_to(x[:, j:j + 1], (8, LANES))


def sublane_row(x, j):
    return jnp.broadcast_to(x[j:j + 1, :], (8, LANES))


def pivot_rows(panel, base, lane, sub):
    inside = (lane >= base) & (lane < base + 8)
    columns = [lane_column(panel, base + j) for j in range(8)]
    d = {(i, j): sublane_row(columns[j], i) for j in range(8) for i in range(j, 8)}
    marked = jnp.where(inside, jnp.where(lane - base == sub, 1.0, 0.0), panel)
    y = [sublane_row(marked, j) for j in range(8)]
    lower = {}
    inverse = []
    for j in range(8):
        inverse.append(1.0 / d[j, j])
        for i in range(j + 1, 8):
            lower[i, j] = d[i, j] * inverse[j]
        for k in range(j + 1, 8):
            for i in range(k, 8):
                d[i, k] = d[i, k] - lower[i, j] * d[k, j]
        for i in range(j + 1, 8):
            y[i] = y[i] - lower[i, j] * y[j]
    y = [y[j] * inverse[j] for j in range(8)]
    for j in range(7, -1, -1):
        for i in range(j):
            y[i] = y[i] - lower[j, i] * y[j]
    return y


def eliminated(x, rows, base, lane):
    inside = (lane >= base) & (lane < base + 8)
    t = [lane_column(x, base + j) * rows[j] for j in range(8)]
    total = ((t[0] + t[1]) + (t[2] + t[3])) + ((t[4] + t[5]) + (t[6] + t[7]))
    return jnp.where(inside, 0.0, x) - total


def inverse_of_block(rows):
    lane = lax.broadcasted_iota(jnp.int32, (8, LANES), 1)
    sub = lax.broadcasted_iota(jnp.int32, (8, LANES), 0)
    rows = list(rows)
    for g in range(16):
        pivots = pivot_rows(rows[g], 8 * g, lane, sub)
        for t in range(1, 16):
            h = (g + t) % 16
            rows[h] = eliminated(rows[h], pivots, 8 * g, lane)
        own = pivots[0]
        for j in range(1, 8):
            own = jnp.where(sub == j, pivots[j], own)
        rows[g] = own
    return rows


def solve_kernel(at_ref, near_ref, far_ref, basis_ref, out_ref, sums_ref, system_ref, *, scale):
    core = at_ref[0]
    z = at_ref[1]
    for flip in range(4):
        at = pl.multiple_of((core * 4 + (z ^ flip)) * PIECE, 8)
        sums_ref[pl.ds(at, PIECE), :] = near_ref[flip]
        at = pl.multiple_of(((1 - core) * 4 + (z ^ flip)) * PIECE, 8)
        sums_ref[pl.ds(at, PIECE), :] = far_ref[flip]
    diagonal = (
        lax.broadcasted_iota(jnp.int32, (BLOCK, BLOCK), 0)
        == lax.broadcasted_iota(jnp.int32, (BLOCK, BLOCK), 1)
    )
    for at, (i, j) in enumerate(GRAM_BLOCKS):
        block = sums_ref[at * BLOCK:(at + 1) * BLOCK, :] * scale
        if i == j:
            block = block + jnp.where(diagonal, RIDGE, 0.0)
        else:
            system_ref[j * BLOCK:(j + 1) * BLOCK, i * BLOCK:(i + 1) * BLOCK] = block.T
        system_ref[i * BLOCK:(i + 1) * BLOCK, j * BLOCK:(j + 1) * BLOCK] = block
    for i in range(4):
        row = sums_ref[MOMENT_ROW + 8 * i:MOMENT_ROW + 8 * i + 1, :] * scale
        system_ref[i * BLOCK:(i + 1) * BLOCK, 512:] = jnp.broadcast_to(row, (BLOCK, BLOCK)).T

    for i in range(4):
        lo = i * BLOCK
        inverse = inverse_of_block(
            [system_ref[lo + 8 * g:lo + 8 * g + 8, lo:lo + BLOCK] for g in range(16)]
        )
        inverse = jnp.concatenate(inverse, axis=0)
        solved = exact_dot(inverse, system_ref[lo:lo + BLOCK, lo + BLOCK:])
        for j in range(4):
            if j != i:
                system_ref[j * BLOCK:(j + 1) * BLOCK, lo + BLOCK:] -= exact_dot(
                    system_ref[j * BLOCK:(j + 1) * BLOCK, lo:lo + BLOCK], solved
                )
        system_ref[lo:lo + BLOCK, lo + BLOCK:] = solved
    width = basis_ref.shape[1]
    for lo in range(0, width, 512):
        parts = [jnp.zeros((8, 512), f32) for _ in range(4)]
        for b in range(64):
            coefficient = jnp.tile(system_ref[8 * b:8 * b + 8, 512:], (1, 4))
            parts[b % 4] += coefficient * basis_ref[8 * b:8 * b + 8, lo:lo + 512].astype(f32)
        out_ref[:, lo:lo + 512] = jnp.sum(
            (parts[0] + parts[1]) + (parts[2] + parts[3]), axis=0, keepdims=True
        )


def solve_continuation(near, far, basis, path_count):
    at = jnp.stack([lax.axis_index("core"), lax.axis_index("z")]).astype(jnp.int32)
    whole = pl.BlockSpec((4, PIECE, LANES), lambda i, s: (0, 0, 0))
    return pl.pallas_call(
        lambda *refs: solve_kernel(*refs, scale=1.0 / path_count),
        out_shape=jax.ShapeDtypeStruct((1, basis.shape[1]), f32),
        grid_spec=pltpu.PrefetchScalarGridSpec(
            num_scalar_prefetch=1,
            grid=(1,),
            in_specs=[whole, whole, pl.BlockSpec(basis.shape, lambda i, s: (0, 0))],
            out_specs=pl.BlockSpec((1, basis.shape[1]), lambda i, s: (0, 0)),
            scratch_shapes=[
                pltpu.VMEM((SUM_ROWS, LANES), f32),
                pltpu.VMEM((512, 512 + LANES), f32),
            ],
        ),
        compiler_params=pltpu.CompilerParams(vmem_limit_bytes=20 << 20),
        name="solve_continuation",
    )(at, near, far, basis)


def in_hbm(x):
    return pltpu.with_memory_space_constraint(x, pltpu.HBM)


def increments_kernel(moved_ref, mixer_ref, basket_ref, sent_ref, weights_ref, buffer_ref, copied):
    copies = []
    for tile in range(moved_ref.shape[2] // INCREMENT_TILE):
        span = pl.ds(tile * INCREMENT_TILE, INCREMENT_TILE)
        adjoint = moved_ref[:, :, span].reshape(256, INCREMENT_TILE).astype(f32)
        for date in range(STEPS - 1, -1, -1):
            gain = TIME_STEP * jnp.dot(
                mixer_ref[...], adjoint.astype(bf16), preferred_element_type=f32
            )
            buffer_ref[tile, :, date] = gain.astype(bf16).reshape(8, 32, INCREMENT_TILE)
            if date:
                adjoint = adjoint + gain
        copies.append(
            pltpu.make_async_copy(buffer_ref.at[tile], sent_ref.at[:, :, :, span], copied.at[tile])
        )
        copies[-1].start()
    lane = lax.broadcasted_iota(jnp.int32, (256, LANES), 1)
    weight = jnp.broadcast_to(basket_ref[...], (256, LANES))
    table = weight
    for later in range(1, STEPS):
        gain = sum(
            jnp.dot(mixer_ref[...], part, preferred_element_type=f32) for part in three_terms(weight)
        )
        weight = weight + TIME_STEP * gain
        table = jnp.where(lane == later, weight, table)
    weights_ref[...] = table
    for copy in copies:
        copy.wait()


def increments(moved, mixer, basket, slab_part):
    tiles = slab_part // INCREMENT_TILE
    return pl.pallas_call(
        increments_kernel,
        out_shape=(
            pltpu.HBM((8, STEPS, 32, slab_part), bf16),
            jax.ShapeDtypeStruct((256, LANES), f32),
        ),
        out_specs=(
            pl.BlockSpec(memory_space=pltpu.HBM),
            pl.BlockSpec(memory_space=pltpu.VMEM),
        ),
        scratch_shapes=[
            pltpu.VMEM((tiles, 8, STEPS, 32, INCREMENT_TILE), bf16),
            pltpu.SemaphoreType.DMA((tiles,)),
        ],
        compiler_params=pltpu.CompilerParams(vmem_limit_bytes=20 << 20),
        name="increments",
    )(moved, mixer, basket)


def surface_kernel(slab_ref, *refs, near):
    step = pl.program_id(0)
    own = slab_ref[0]
    if near:
        (continuation_ref, cotangent_ref, gain_ref, shock_ref, weight_ref, exercise_ref, bucket_ref,
         delta_ref, total_ref) = refs

        @pl.when(step == 0)
        def _():
            total_ref[...] = jnp.zeros(total_ref.shape, f32)
    else:
        (far_refs, (before_ref, _, cotangent_ref, gain_ref, shock_ref, weight_ref, exercise_ref,
                    bucket_ref, delta_ref, share_ref, continuation_ref, total_ref)) = refs[:3], refs[3:]

        @pl.when(step == 0)
        def _():
            for flip in range(3):
                continuation_ref[2 * flip + 2:2 * flip + 4, :] = far_refs[flip][...]
            total_ref[...] = before_ref[...]

    continuation = continuation_ref[pl.ds(slab_of_step(step, own, near) ^ own, 1), :]
    held = [exercise_ref[date:date + 1, :].astype(f32) * continuation for date in range(STEPS)]
    weights = [weight_ref[:, later:later + 1] for later in range(STEPS)]
    strikes = lax.broadcasted_iota(jnp.int32, (STRIKE_ROWS, DATE_TILE), 0).astype(f32).astype(bf16)
    base = cotangent_ref[...].astype(f32)
    total = total_ref[...]
    for date in range(STEPS - 1, -1, -1):
        base = base + gain_ref[0, date].astype(f32)
        adjoint = base
        for later in range(STEPS - date):
            adjoint = adjoint + held[date + later] * weights[later]
        terms = (adjoint * shock_ref[date].astype(f32)).astype(bf16).astype(f32)
        bucket = bucket_ref[date:date + 1, :]
        column = (bucket & (STRIKE_ROWS - 1)).astype(f32).astype(bf16)
        chosen = jnp.where(strikes == column, jnp.bfloat16(1), jnp.bfloat16(0))
        group = bucket >> STRIKE_BITS
        terms = jnp.concatenate(
            [jnp.where(group == g, terms, 0.0).astype(bf16) for g in range(NK // STRIKE_ROWS)], axis=0
        )
        total = total + lax.dot_general(
            chosen, terms, (((1,), (1,)), ((), ())), preferred_element_type=f32
        )
    delta_ref[...] = adjoint
    total_ref[...] = total

    if not near:
        @pl.when(step == pl.num_programs(0) - 1)
        def _():
            owners = STRIKE_ROWS // 16
            for g in range(NK // STRIKE_ROWS):
                grouped = total[:, 32 * g:32 * g + 32].reshape(owners, 16, 32)
                for q in range(4):
                    share_ref[g * owners:(g + 1) * owners, :, 32 * q:32 * q + 32] = grouped[
                        :, 4 * q:4 * q + 4, :
                    ]


def slab_of_step(step, own, near):
    pair = own >> 1
    return 2 * pair + step if near else 2 * ((pair + 1 + (step >> 1)) & 3) + (step & 1)


def surface_call(slab, continuations, before, cotangent, gains, shocks, weights, exercise, bucket):
    near = before is None
    local_paths = cotangent.shape[1]
    sums_shape = (STRIKE_ROWS, 32 * (NK // STRIKE_ROWS))

    def whole(shape):
        return pl.BlockSpec(shape, lambda i, s: (0,) * len(shape))

    def at(i, s):
        return slab_of_step(i, s[0], near)

    delta_spec = pl.BlockSpec((32, DATE_TILE), lambda i, s: (0, at(i, s)))
    delta_shape = jax.ShapeDtypeStruct((32, local_paths), f32)
    shared_specs = [
        pl.BlockSpec((32, DATE_TILE), lambda i, s: (0, at(i, s))),
        pl.BlockSpec((1, STEPS, 32, DATE_TILE), lambda i, s: (at(i, s), 0, 0, 0)),
        pl.BlockSpec((STEPS, 32, DATE_TILE), lambda i, s: (0, 0, at(i, s))),
        pl.BlockSpec((32, LANES), lambda i, s: (s[0], 0)),
        pl.BlockSpec((STEPS, DATE_TILE), lambda i, s: (0, at(i, s))),
        pl.BlockSpec((STEPS, DATE_TILE), lambda i, s: (0, at(i, s))),
    ]
    rows = whole((2, DATE_TILE))
    if near:
        first_specs, first = [rows], continuations
        outs = (delta_shape, jax.ShapeDtypeStruct(sums_shape, f32))
        out_specs = (delta_spec, whole(sums_shape))
        scratch = []
    else:
        delta, total = before
        first_specs = [rows] * 3 + [whole(sums_shape), pl.BlockSpec(memory_space=pl.ANY)]
        first = [*continuations, total, delta]
        outs = (delta_shape, jax.ShapeDtypeStruct((16, 4, LANES), f32))
        out_specs = (delta_spec, whole((16, 4, LANES)))
        scratch = [pltpu.VMEM((8, DATE_TILE), f32), pltpu.VMEM(sums_shape, f32)]
    return pl.pallas_call(
        lambda *refs: surface_kernel(*refs, near=near),
        out_shape=outs,
        grid_spec=pltpu.PrefetchScalarGridSpec(
            num_scalar_prefetch=1,
            grid=(2 if near else 6,),
            in_specs=first_specs + shared_specs,
            out_specs=out_specs,
            scratch_shapes=scratch,
        ),
        input_output_aliases={} if near else {5: 0},
        compiler_params=pltpu.CompilerParams(vmem_limit_bytes=32 << 20),
        name="surface_near" if near else "surface_far",
    )(slab, *first, cotangent, gains, in_hbm(shocks), weights, exercise, bucket)


def surface_and_delta(slab, continuations, *rest):
    before = surface_call(slab, continuations[:1], None, *rest)
    return surface_call(slab, continuations[1:], before, *rest)


def per_device(prices, loadings, basis_w, basis_bias, payoff, in_fit, cotangent, shocks, corr_gen,
               basket, exercise, bucket):
    local_paths = prices.shape[1]
    slab_part = local_paths // 8
    path_count = float(local_paths * 16)
    slab = lax.axis_index(STOCK_AXES).astype(jnp.int32).reshape(1)

    pieces = jnp.moveaxis(prices.reshape(32, 8, slab_part), 1, 0)
    table = jnp.broadcast_to(jnp.pad(loadings, ((0, 0), (0, LANES - 32)))[None], (8, 32, LANES))
    moved_prices = lax.all_to_all(
        jnp.concatenate([pieces, table], axis=2), STOCK_AXES, 0, 0, tiled=True
    )
    slabs = jnp.moveaxis(cotangent.reshape(32, 8, slab_part), 1, 0)
    small = (basis_w, basis_bias[:, None], payoff[None, :], in_fit[None, :],
             basket[:, None])
    slabs, moved_prices, small = lax.optimization_barrier((slabs, moved_prices, small))
    basis_w, bias, payoff, in_fit, basket = small
    moved = lax.all_to_all(slabs, STOCK_AXES, 0, 0, tiled=True)
    basis_w = in_hbm(basis_w)
    in_fit = in_hbm(in_fit)
    place = jnp.stack([slab[0], lax.axis_index("core").astype(jnp.int32)])
    basis, kept, other = regression_sums(
        place, moved_prices, basis_w, bias, payoff, in_fit, slab_part
    )
    share, moved = sum_over_cores_and_z(kept, other, moved)
    sent, weights = increments(moved, corr_gen, basket, slab_part)
    share = sum_of_exchange(share, "x")
    parts = exchange_with_others(share, ("ylo", "yhi"), 4)
    parts, sent = lax.optimization_barrier((parts, sent))
    share = (share + parts[0]) + (parts[1] + parts[2])
    gains = lax.all_to_all(sent, STOCK_AXES, 0, 0, tiled=True)
    near, far = gathered_sum(share)
    continuation = solve_continuation(near, far, basis, path_count)
    pair = jnp.concatenate([continuation] + exchange_with_others(continuation, "yhi", 2), axis=0)
    continuations = [pair] + exchange_with_others(pair, "x", 4)
    delta, surface = surface_and_delta(
        slab, continuations, cotangent, gains, shocks, weights, exercise, bucket
    )
    surface = lax.all_to_all(surface, PATH_AXES, 0, 0, tiled=True)
    surface = jnp.sum(surface, axis=0).reshape(4, 4, 32)
    surface = jnp.transpose(surface, (2, 1, 0)).reshape(32, 16)
    return delta, surface


def solution(mesh):
    fine = Mesh(mesh.devices.reshape(FINE), ALL_AXES)
    stocks, paths = STOCK_AXES, PATH_AXES
    return jax.shard_map(
        per_device,
        mesh=fine,
        in_specs=(
            P(stocks, paths),
            P(stocks, None),
            P(),
            P(),
            P(paths),
            P(paths),
            P(stocks, paths),
            P(None, stocks, paths),
            P(),
            P(),
            P(None, paths),
            P(None, paths),
        ),
        out_specs=(P(stocks, paths), P(stocks, paths)),
        check_vma=False,
    )
```

```python
import jax
import jax.numpy as jnp
from jax import lax
from jax.experimental import pallas as pl
from jax.experimental.pallas import tpu as pltpu
from jax.sharding import Mesh
from jax.sharding import PartitionSpec as P

NK = 256
STEPS = 4
TIME_STEP = 0.25
RIDGE = 0.1
LANES = 128
BLOCK = 128
TILE = 2048
INCREMENT_TILE = 1024
DATE_TILE = 2048
STRIKE_BITS = 7
STRIKE_ROWS = 1 << STRIKE_BITS
PATH_AXES = ("z", "ylo", "core")
STOCK_AXES = ("x", "yhi")
ALL_AXES = PATH_AXES + STOCK_AXES
FINE = (4, 2, 2, 4, 2)
f32 = jnp.float32
bf16 = jnp.bfloat16


def three_terms(x):
    high = x.astype(bf16)
    rest = x - high.astype(f32)
    middle = rest.astype(bf16)
    low = (rest - middle.astype(f32)).astype(bf16)
    return high, middle, low


def left_terms(x, axis):
    high, middle, low = three_terms(x)
    return jnp.concatenate([high, high, middle, high, low, middle], axis=axis)


def right_terms(x, axis):
    high, middle, low = three_terms(x)
    return jnp.concatenate([high, middle, high, low, high, middle], axis=axis)


def exact_dot(left, right):
    return jnp.dot(left_terms(left, 1), right_terms(right, 0), preferred_element_type=f32)


GRAM_BLOCKS = tuple((i, j) for i in range(4) for j in range(i + 1))
MOMENT_ROW = len(GRAM_BLOCKS) * BLOCK
SUM_ROWS = 1344
PIECE = SUM_ROWS // 8


def gram_kernel(slab_ref, moved_ref, table_ref, weight_ref, bias_ref, payoff_ref, fit_ref,
                basis_ref, kept_ref, sent_ref, gram_ref, moment_ref, sums_ref):
    step = pl.program_id(0)
    tile = moved_ref[...].reshape(256, TILE)
    loads = table_ref[...].reshape(256, LANES)[:, :32]
    factors = lax.dot_general(loads, tile, (((0,), (0,)), ((), ())), preferred_element_type=f32)
    raised = lax.dot_general(
        left_terms(weight_ref[...], 0), right_terms(factors, 0), (((0,), (0,)), ((), ())), preferred_element_type=f32
    )
    basis = jnp.tanh(raised + bias_ref[...]).astype(bf16)
    basis_ref[...] = basis
    picked = basis * fit_ref[...].astype(f32).astype(bf16)
    paid = jnp.broadcast_to(payoff_ref[...].astype(f32), (16, TILE)).astype(bf16)
    contract = (((1,), (1,)), ((), ()))
    first = lax.dot_general(picked[:256], basis[:256], contract, preferred_element_type=f32)
    second = lax.dot_general(picked[256:], basis, contract, preferred_element_type=f32)
    moment = lax.dot_general(paid, picked, contract, preferred_element_type=f32)

    @pl.when(step == 0)
    def _():
        gram_ref[:256, :256] = first
        gram_ref[256:, :] = second
        moment_ref[...] = moment

    @pl.when(step > 0)
    def _():
        gram_ref[:256, :256] += first
        gram_ref[256:, :] += second
        moment_ref[...] += moment

    @pl.when(step == pl.num_programs(0) - 1)
    def _():
        for at, (i, j) in enumerate(GRAM_BLOCKS):
            sums_ref[at * BLOCK:(at + 1) * BLOCK, :] = gram_ref[
                i * BLOCK:(i + 1) * BLOCK, j * BLOCK:(j + 1) * BLOCK
            ]
        sums_ref[MOMENT_ROW:, :] = jnp.zeros((SUM_ROWS - MOMENT_ROW, LANES), f32)
        for i in range(4):
            sums_ref[MOMENT_ROW + 8 * i:MOMENT_ROW + 8 * i + 8, :] = moment_ref[
                :8, i * BLOCK:(i + 1) * BLOCK
            ]
        half = 4 * PIECE
        kept_ref[...] = sums_ref[pl.ds(pl.multiple_of(slab_ref[1] * half, 8), half), :]
        sent_ref[...] = sums_ref[pl.ds(pl.multiple_of((1 - slab_ref[1]) * half, 8), half), :]


def regression_sums(slab, moved, weights, bias, payoff, fit, slab_part):
    tiles = slab_part // TILE
    table_at = slab_part // LANES

    def own(step, slab_ref):
        return (0, slab_ref[0] * tiles + step)

    return pl.pallas_call(
        gram_kernel,
        out_shape=(
            pltpu.HBM((512, slab_part), bf16),
            pltpu.HBM((SUM_ROWS // 2, LANES), f32),
            pltpu.HBM((SUM_ROWS // 2, LANES), f32),
        ),
        grid_spec=pltpu.PrefetchScalarGridSpec(
            num_scalar_prefetch=1,
            grid=(tiles,),
            in_specs=[
                pl.BlockSpec((8, 32, TILE), lambda i, s: (0, 0, i)),
                pl.BlockSpec((8, 32, LANES), lambda i, s: (0, 0, table_at)),
                pl.BlockSpec((32, 512), lambda i, s: (0, 0)),
                pl.BlockSpec((512, 1), lambda i, s: (0, 0)),
                pl.BlockSpec((1, TILE), own),
                pl.BlockSpec((1, TILE), own),
            ],
            out_specs=(
                pl.BlockSpec((512, TILE), lambda i, s: (0, i)),
                pl.BlockSpec((SUM_ROWS // 2, LANES), lambda i, s: (0, 0)),
                pl.BlockSpec((SUM_ROWS // 2, LANES), lambda i, s: (0, 0)),
            ),
            scratch_shapes=[
                pltpu.VMEM((512, 512), f32),
                pltpu.VMEM((16, 512), f32),
                pltpu.VMEM((SUM_ROWS, LANES), f32),
            ],
        ),
        compiler_params=pltpu.CompilerParams(vmem_limit_bytes=20 << 20),
        name="regression_sums",
    )(slab, moved, moved, weights, bias, payoff, fit)


def exchange_with_others(x, axes, count, piece_of=None):
    received = []
    for flip in range(1, count):
        sent = x if piece_of is None else piece_of(flip)
        received.append(lax.ppermute(sent, axes, [(i, i ^ flip) for i in range(count)]))
    return received


def sum_over_cores_and_z(kept, sent, beside):
    z = lax.axis_index("z")
    mine = (kept + exchange_with_others(sent, "core", 2)[0]).reshape(4, PIECE, LANES)

    def piece_of(flip):
        return lax.dynamic_index_in_dim(mine, z ^ flip, 0, False)

    parts, beside = lax.optimization_barrier((exchange_with_others(None, "z", 4, piece_of), beside))
    return (piece_of(0) + parts[0]) + (parts[1] + parts[2]), beside


def sum_of_exchange(share, axes):
    parts = exchange_with_others(share, axes, 4)
    return (share + parts[0]) + (parts[1] + parts[2])


def gathered_sum(share):
    column = jnp.stack([share] + exchange_with_others(share, "z", 4))
    return column, exchange_with_others(column, "core", 2)[0]


def lane_column(x, j):
    return jnp.broadcast_to(x[:, j:j + 1], (8, LANES))


def sublane_row(x, j):
    return jnp.broadcast_to(x[j:j + 1, :], (8, LANES))


def pivot_rows(panel, base, lane, sub):
    inside = (lane >= base) & (lane < base + 8)
    columns = [lane_column(panel, base + j) for j in range(8)]
    d = {(i, j): sublane_row(columns[j], i) for j in range(8) for i in range(j, 8)}
    marked = jnp.where(inside, jnp.where(lane - base == sub, 1.0, 0.0), panel)
    y = [sublane_row(marked, j) for j in range(8)]
    lower = {}
    inverse = []
    for j in range(8):
        inverse.append(1.0 / d[j, j])
        for i in range(j + 1, 8):
            lower[i, j] = d[i, j] * inverse[j]
        for k in range(j + 1, 8):
            for i in range(k, 8):
                d[i, k] = d[i, k] - lower[i, j] * d[k, j]
        for i in range(j + 1, 8):
            y[i] = y[i] - lower[i, j] * y[j]
    y = [y[j] * inverse[j] for j in range(8)]
    for j in range(7, -1, -1):
        for i in range(j):
            y[i] = y[i] - lower[j, i] * y[j]
    return y


def eliminated(x, rows, base, lane):
    inside = (lane >= base) & (lane < base + 8)
    t = [lane_column(x, base + j) * rows[j] for j in range(8)]
    total = ((t[0] + t[1]) + (t[2] + t[3])) + ((t[4] + t[5]) + (t[6] + t[7]))
    return jnp.where(inside, 0.0, x) - total


def inverse_of_block(rows):
    lane = lax.broadcasted_iota(jnp.int32, (8, LANES), 1)
    sub = lax.broadcasted_iota(jnp.int32, (8, LANES), 0)
    rows = list(rows)
    for g in range(16):
        pivots = pivot_rows(rows[g], 8 * g, lane, sub)
        for t in range(1, 16):
            h = (g + t) % 16
            rows[h] = eliminated(rows[h], pivots, 8 * g, lane)
        own = pivots[0]
        for j in range(1, 8):
            own = jnp.where(sub == j, pivots[j], own)
        rows[g] = own
    return rows


def solve_kernel(at_ref, near_ref, far_ref, basis_ref, out_ref, sums_ref, system_ref, *, scale):
    core = at_ref[0]
    z = at_ref[1]
    for flip in range(4):
        at = pl.multiple_of((core * 4 + (z ^ flip)) * PIECE, 8)
        sums_ref[pl.ds(at, PIECE), :] = near_ref[flip]
        at = pl.multiple_of(((1 - core) * 4 + (z ^ flip)) * PIECE, 8)
        sums_ref[pl.ds(at, PIECE), :] = far_ref[flip]
    diagonal = (
        lax.broadcasted_iota(jnp.int32, (BLOCK, BLOCK), 0)
        == lax.broadcasted_iota(jnp.int32, (BLOCK, BLOCK), 1)
    )
    for at, (i, j) in enumerate(GRAM_BLOCKS):
        block = sums_ref[at * BLOCK:(at + 1) * BLOCK, :] * scale
        if i == j:
            block = block + jnp.where(diagonal, RIDGE, 0.0)
        else:
            system_ref[j * BLOCK:(j + 1) * BLOCK, i * BLOCK:(i + 1) * BLOCK] = block.T
        system_ref[i * BLOCK:(i + 1) * BLOCK, j * BLOCK:(j + 1) * BLOCK] = block
    for i in range(4):
        row = sums_ref[MOMENT_ROW + 8 * i:MOMENT_ROW + 8 * i + 1, :] * scale
        system_ref[i * BLOCK:(i + 1) * BLOCK, 512:] = jnp.broadcast_to(row, (BLOCK, BLOCK)).T

    for i in range(4):
        lo = i * BLOCK
        inverse = inverse_of_block(
            [system_ref[lo + 8 * g:lo + 8 * g + 8, lo:lo + BLOCK] for g in range(16)]
        )
        inverse = jnp.concatenate(inverse, axis=0)
        solved = exact_dot(inverse, system_ref[lo:lo + BLOCK, lo + BLOCK:])
        for j in range(4):
            if j != i:
                system_ref[j * BLOCK:(j + 1) * BLOCK, lo + BLOCK:] -= exact_dot(
                    system_ref[j * BLOCK:(j + 1) * BLOCK, lo:lo + BLOCK], solved
                )
        system_ref[lo:lo + BLOCK, lo + BLOCK:] = solved
    width = basis_ref.shape[1]
    for lo in range(0, width, 512):
        parts = [jnp.zeros((8, 512), f32) for _ in range(4)]
        for b in range(64):
            coefficient = jnp.tile(system_ref[8 * b:8 * b + 8, 512:], (1, 4))
            parts[b % 4] += coefficient * basis_ref[8 * b:8 * b + 8, lo:lo + 512].astype(f32)
        out_ref[:, lo:lo + 512] = jnp.sum(
            (parts[0] + parts[1]) + (parts[2] + parts[3]), axis=0, keepdims=True
        )


def solve_continuation(near, far, basis, path_count):
    at = jnp.stack([lax.axis_index("core"), lax.axis_index("z")]).astype(jnp.int32)
    whole = pl.BlockSpec((4, PIECE, LANES), lambda i, s: (0, 0, 0))
    return pl.pallas_call(
        lambda *refs: solve_kernel(*refs, scale=1.0 / path_count),
        out_shape=jax.ShapeDtypeStruct((1, basis.shape[1]), f32),
        grid_spec=pltpu.PrefetchScalarGridSpec(
            num_scalar_prefetch=1,
            grid=(1,),
            in_specs=[whole, whole, pl.BlockSpec(basis.shape, lambda i, s: (0, 0))],
            out_specs=pl.BlockSpec((1, basis.shape[1]), lambda i, s: (0, 0)),
            scratch_shapes=[
                pltpu.VMEM((SUM_ROWS, LANES), f32),
                pltpu.VMEM((512, 512 + LANES), f32),
            ],
        ),
        compiler_params=pltpu.CompilerParams(vmem_limit_bytes=20 << 20),
        name="solve_continuation",
    )(at, near, far, basis)


def in_hbm(x):
    return pltpu.with_memory_space_constraint(x, pltpu.HBM)


def increments_kernel(moved_ref, mixer_ref, basket_ref, sent_ref, weights_ref, buffer_ref, copied):
    copies = []
    for tile in range(moved_ref.shape[2] // INCREMENT_TILE):
        span = pl.ds(tile * INCREMENT_TILE, INCREMENT_TILE)
        adjoint = moved_ref[:, :, span].reshape(256, INCREMENT_TILE).astype(f32)
        for date in range(STEPS - 1, -1, -1):
            gain = TIME_STEP * jnp.dot(
                mixer_ref[...], adjoint.astype(bf16), preferred_element_type=f32
            )
            buffer_ref[tile, :, date] = gain.astype(bf16).reshape(8, 32, INCREMENT_TILE)
            if date:
                adjoint = adjoint + gain
        copies.append(
            pltpu.make_async_copy(buffer_ref.at[tile], sent_ref.at[:, :, :, span], copied.at[tile])
        )
        copies[-1].start()
    lane = lax.broadcasted_iota(jnp.int32, (256, LANES), 1)
    weight = jnp.broadcast_to(basket_ref[...], (256, LANES))
    table = weight
    for later in range(1, STEPS):
        gain = sum(
            jnp.dot(mixer_ref[...], part, preferred_element_type=f32) for part in three_terms(weight)
        )
        weight = weight + TIME_STEP * gain
        table = jnp.where(lane == later, weight, table)
    weights_ref[...] = table
    for copy in copies:
        copy.wait()


def increments(moved, mixer, basket, slab_part):
    tiles = slab_part // INCREMENT_TILE
    return pl.pallas_call(
        increments_kernel,
        out_shape=(
            pltpu.HBM((8, STEPS, 32, slab_part), bf16),
            jax.ShapeDtypeStruct((256, LANES), f32),
        ),
        out_specs=(
            pl.BlockSpec(memory_space=pltpu.HBM),
            pl.BlockSpec(memory_space=pltpu.VMEM),
        ),
        scratch_shapes=[
            pltpu.VMEM((tiles, 8, STEPS, 32, INCREMENT_TILE), bf16),
            pltpu.SemaphoreType.DMA((tiles,)),
        ],
        compiler_params=pltpu.CompilerParams(vmem_limit_bytes=20 << 20),
        name="increments",
    )(moved, mixer, basket)


def surface_kernel(slab_ref, *refs):
    continuation_refs = refs[:4]
    (cotangent_ref, gain_ref, shock_ref, weight_ref, exercise_ref, bucket_ref, delta_ref, share_ref,
     continuation_ref, total_ref) = refs[4:]
    step = pl.program_id(0)

    @pl.when(step == 0)
    def _():
        for flip in range(8):
            continuation_ref[pl.ds(slab_ref[0] ^ flip, 1), :] = continuation_refs[flip // 2][
                flip % 2:flip % 2 + 1, :
            ]
        total_ref[...] = jnp.zeros(total_ref.shape, f32)

    continuation = continuation_ref[pl.ds(step, 1), :]
    held = [exercise_ref[date:date + 1, :].astype(f32) * continuation for date in range(STEPS)]
    weights = [weight_ref[:, later:later + 1] for later in range(STEPS)]
    strikes = lax.broadcasted_iota(jnp.int32, (STRIKE_ROWS, DATE_TILE), 0).astype(f32).astype(bf16)
    base = cotangent_ref[...].astype(f32)
    total = total_ref[...]
    for date in range(STEPS - 1, -1, -1):
        base = base + gain_ref[0, date].astype(f32)
        adjoint = base
        for later in range(STEPS - date):
            adjoint = adjoint + held[date + later] * weights[later]
        terms = adjoint * shock_ref[date].astype(f32)
        bucket = bucket_ref[date:date + 1, :]
        column = (bucket & (STRIKE_ROWS - 1)).astype(f32).astype(bf16)
        chosen = jnp.where(strikes == column, jnp.bfloat16(1), jnp.bfloat16(0))
        group = bucket >> STRIKE_BITS
        terms = jnp.concatenate(
            [jnp.where(group == g, terms, 0.0).astype(bf16) for g in range(NK // STRIKE_ROWS)], axis=0
        )
        total = total + lax.dot_general(
            chosen, terms, (((1,), (1,)), ((), ())), preferred_element_type=f32
        )
    delta_ref[...] = adjoint
    total_ref[...] = total

    @pl.when(step == pl.num_programs(0) - 1)
    def _():
        owners = STRIKE_ROWS // 16
        for g in range(NK // STRIKE_ROWS):
            grouped = total[:, 32 * g:32 * g + 32].reshape(owners, 16, 32)
            for q in range(4):
                share_ref[g * owners:(g + 1) * owners, :, 32 * q:32 * q + 32] = grouped[
                    :, 4 * q:4 * q + 4, :
                ]


def surface_and_delta(slab, continuations, cotangent, gains, shocks, weights, exercise, bucket):
    local_paths = cotangent.shape[1]
    whole = pl.BlockSpec((2, DATE_TILE), lambda i, s: (0, 0))
    return pl.pallas_call(
        surface_kernel,
        out_shape=(
            jax.ShapeDtypeStruct((32, local_paths), f32),
            jax.ShapeDtypeStruct((16, 4, LANES), f32),
        ),
        grid_spec=pltpu.PrefetchScalarGridSpec(
            num_scalar_prefetch=1,
            grid=(local_paths // DATE_TILE,),
            in_specs=[whole] * 4 + [
                pl.BlockSpec((32, DATE_TILE), lambda i, s: (0, i)),
                pl.BlockSpec((1, STEPS, 32, DATE_TILE), lambda i, s: (i, 0, 0, 0)),
                pl.BlockSpec((STEPS, 32, DATE_TILE), lambda i, s: (0, 0, i)),
                pl.BlockSpec((32, LANES), lambda i, s: (s[0], 0)),
                pl.BlockSpec((STEPS, DATE_TILE), lambda i, s: (0, i)),
                pl.BlockSpec((STEPS, DATE_TILE), lambda i, s: (0, i)),
            ],
            out_specs=(
                pl.BlockSpec((32, DATE_TILE), lambda i, s: (0, i)),
                pl.BlockSpec((16, 4, LANES), lambda i, s: (0, 0, 0)),
            ),
            scratch_shapes=[pltpu.VMEM((8, DATE_TILE), f32), pltpu.VMEM((STRIKE_ROWS, 32 * (NK // STRIKE_ROWS)), f32)],
        ),
        compiler_params=pltpu.CompilerParams(vmem_limit_bytes=32 << 20),
        name="surface_and_delta",
    )(slab, *continuations, cotangent, gains, in_hbm(shocks), weights, exercise, bucket)


def per_device(prices, loadings, basis_w, basis_bias, payoff, in_fit, cotangent, shocks, corr_gen,
               basket, exercise, bucket):
    local_paths = prices.shape[1]
    slab_part = local_paths // 8
    path_count = float(local_paths * 16)
    slab = lax.axis_index(STOCK_AXES).astype(jnp.int32).reshape(1)

    pieces = jnp.moveaxis(prices.reshape(32, 8, slab_part), 1, 0)
    table = jnp.broadcast_to(jnp.pad(loadings, ((0, 0), (0, LANES - 32)))[None], (8, 32, LANES))
    moved_prices = lax.all_to_all(
        jnp.concatenate([pieces, table], axis=2), STOCK_AXES, 0, 0, tiled=True
    )
    slabs = jnp.moveaxis(cotangent.reshape(32, 8, slab_part), 1, 0)
    small = (basis_w, basis_bias[:, None], payoff[None, :], in_fit[None, :],
             basket[:, None])
    slabs, moved_prices, small = lax.optimization_barrier((slabs, moved_prices, small))
    basis_w, bias, payoff, in_fit, basket = small
    moved = lax.all_to_all(slabs, STOCK_AXES, 0, 0, tiled=True)
    basis_w = in_hbm(basis_w)
    in_fit = in_hbm(in_fit)
    place = jnp.stack([slab[0], lax.axis_index("core").astype(jnp.int32)])
    basis, kept, other = regression_sums(
        place, moved_prices, basis_w, bias, payoff, in_fit, slab_part
    )
    share, moved = sum_over_cores_and_z(kept, other, moved)
    sent, weights = increments(moved, corr_gen, basket, slab_part)
    share = sum_of_exchange(share, ("ylo", "yhi"))
    parts = exchange_with_others(share, "x", 4)
    parts, sent = lax.optimization_barrier((parts, sent))
    share = (share + parts[0]) + (parts[1] + parts[2])
    gains = lax.all_to_all(sent, STOCK_AXES, 0, 0, tiled=True)
    near, far = gathered_sum(share)
    continuation = solve_continuation(near, far, basis, path_count)
    pair = jnp.concatenate([continuation] + exchange_with_others(continuation, "yhi", 2), axis=0)
    continuations = [pair] + exchange_with_others(pair, "x", 4)
    delta, surface = surface_and_delta(
        slab, continuations, cotangent, gains, shocks, weights, exercise, bucket
    )
    surface = lax.all_to_all(surface, PATH_AXES, 0, 0, tiled=True)
    surface = jnp.sum(surface, axis=0).reshape(4, 4, 32)
    surface = jnp.transpose(surface, (2, 1, 0)).reshape(32, 16)
    return delta, surface


def solution(mesh):
    fine = Mesh(mesh.devices.reshape(FINE), ALL_AXES)
    stocks, paths = STOCK_AXES, PATH_AXES
    return jax.shard_map(
        per_device,
        mesh=fine,
        in_specs=(
            P(stocks, paths),
            P(stocks, None),
            P(),
            P(),
            P(paths),
            P(paths),
            P(stocks, paths),
            P(None, stocks, paths),
            P(),
            P(),
            P(None, paths),
            P(None, paths),
        ),
        out_specs=(P(stocks, paths), P(stocks, paths)),
        check_vma=False,
    )
```

```python
import jax
import jax.numpy as jnp
from jax import lax
from jax.experimental import pallas as pl
from jax.experimental.pallas import tpu as pltpu
from jax.sharding import Mesh
from jax.sharding import PartitionSpec as P

NK = 256
STEPS = 4
TIME_STEP = 0.25
RIDGE = 0.1
LANES = 128
BLOCK = 128
TILE = 2048
INCREMENT_TILE = 1024
DATE_TILE = 2048
STRIKE_BITS = 7
STRIKE_ROWS = 1 << STRIKE_BITS
PATH_AXES = ("z", "ylo", "core")
STOCK_AXES = ("x", "yhi")
ALL_AXES = PATH_AXES + STOCK_AXES
FINE = (4, 2, 2, 4, 2)
f32 = jnp.float32
bf16 = jnp.bfloat16


def three_terms(x):
    high = x.astype(bf16)
    rest = x - high.astype(f32)
    middle = rest.astype(bf16)
    low = (rest - middle.astype(f32)).astype(bf16)
    return high, middle, low


def left_terms(x, axis):
    high, middle, low = three_terms(x)
    return jnp.concatenate([high, high, middle, high, low, middle], axis=axis)


def right_terms(x, axis):
    high, middle, low = three_terms(x)
    return jnp.concatenate([high, middle, high, low, high, middle], axis=axis)


def exact_dot(left, right):
    return jnp.dot(left_terms(left, 1), right_terms(right, 0), preferred_element_type=f32)


GRAM_BLOCKS = tuple((i, j) for i in range(4) for j in range(i + 1))
MOMENT_ROW = len(GRAM_BLOCKS) * BLOCK
SUM_ROWS = 1344
PIECE = SUM_ROWS // 8


def gram_kernel(slab_ref, moved_ref, table_ref, weight_ref, bias_ref, payoff_ref, fit_ref,
                basis_ref, kept_ref, sent_ref, gram_ref, moment_ref, sums_ref):
    step = pl.program_id(0)
    tile = moved_ref[...].reshape(256, TILE)
    loads = table_ref[...].reshape(256, LANES)[:, :32]
    factors = lax.dot_general(loads, tile, (((0,), (0,)), ((), ())), preferred_element_type=f32)
    raised = lax.dot_general(
        left_terms(weight_ref[...], 0), right_terms(factors, 0), (((0,), (0,)), ((), ())), preferred_element_type=f32
    )
    basis = jnp.tanh(raised + bias_ref[...]).astype(bf16)
    basis_ref[...] = basis
    picked = basis * fit_ref[...].astype(f32).astype(bf16)
    paid = jnp.broadcast_to(payoff_ref[...].astype(f32), (16, TILE)).astype(bf16)
    contract = (((1,), (1,)), ((), ()))
    first = lax.dot_general(picked[:256], basis[:256], contract, preferred_element_type=f32)
    second = lax.dot_general(picked[256:], basis, contract, preferred_element_type=f32)
    moment = lax.dot_general(paid, picked, contract, preferred_element_type=f32)

    @pl.when(step == 0)
    def _():
        gram_ref[:256, :256] = first
        gram_ref[256:, :] = second
        moment_ref[...] = moment

    @pl.when(step > 0)
    def _():
        gram_ref[:256, :256] += first
        gram_ref[256:, :] += second
        moment_ref[...] += moment

    @pl.when(step == pl.num_programs(0) - 1)
    def _():
        for at, (i, j) in enumerate(GRAM_BLOCKS):
            sums_ref[at * BLOCK:(at + 1) * BLOCK, :] = gram_ref[
                i * BLOCK:(i + 1) * BLOCK, j * BLOCK:(j + 1) * BLOCK
            ]
        sums_ref[MOMENT_ROW:, :] = jnp.zeros((SUM_ROWS - MOMENT_ROW, LANES), f32)
        for i in range(4):
            sums_ref[MOMENT_ROW + 8 * i:MOMENT_ROW + 8 * i + 8, :] = moment_ref[
                :8, i * BLOCK:(i + 1) * BLOCK
            ]
        half = 4 * PIECE
        kept_ref[...] = sums_ref[pl.ds(pl.multiple_of(slab_ref[1] * half, 8), half), :]
        sent_ref[...] = sums_ref[pl.ds(pl.multiple_of((1 - slab_ref[1]) * half, 8), half), :]


def regression_sums(slab, moved, weights, bias, payoff, fit, slab_part):
    tiles = slab_part // TILE
    table_at = slab_part // LANES

    def own(step, slab_ref):
        return (0, slab_ref[0] * tiles + step)

    return pl.pallas_call(
        gram_kernel,
        out_shape=(
            pltpu.HBM((512, slab_part), bf16),
            pltpu.HBM((SUM_ROWS // 2, LANES), f32),
            pltpu.HBM((SUM_ROWS // 2, LANES), f32),
        ),
        grid_spec=pltpu.PrefetchScalarGridSpec(
            num_scalar_prefetch=1,
            grid=(tiles,),
            in_specs=[
                pl.BlockSpec((8, 32, TILE), lambda i, s: (0, 0, i)),
                pl.BlockSpec((8, 32, LANES), lambda i, s: (0, 0, table_at)),
                pl.BlockSpec((32, 512), lambda i, s: (0, 0)),
                pl.BlockSpec((512, 1), lambda i, s: (0, 0)),
                pl.BlockSpec((1, TILE), own),
                pl.BlockSpec((1, TILE), own),
            ],
            out_specs=(
                pl.BlockSpec((512, TILE), lambda i, s: (0, i)),
                pl.BlockSpec((SUM_ROWS // 2, LANES), lambda i, s: (0, 0)),
                pl.BlockSpec((SUM_ROWS // 2, LANES), lambda i, s: (0, 0)),
            ),
            scratch_shapes=[
                pltpu.VMEM((512, 512), f32),
                pltpu.VMEM((16, 512), f32),
                pltpu.VMEM((SUM_ROWS, LANES), f32),
            ],
        ),
        compiler_params=pltpu.CompilerParams(vmem_limit_bytes=20 << 20),
        name="regression_sums",
    )(slab, moved, moved, weights, bias, payoff, fit)


def exchange_with_others(x, axes, count, piece_of=None):
    received = []
    for flip in range(1, count):
        sent = x if piece_of is None else piece_of(flip)
        received.append(lax.ppermute(sent, axes, [(i, i ^ flip) for i in range(count)]))
    return received


def sum_over_cores_and_z(kept, sent, beside):
    z = lax.axis_index("z")
    kept = kept.reshape(4, PIECE, LANES)
    received = exchange_with_others(sent, "core", 2)[0].reshape(4, PIECE, LANES)

    def piece_of(flip):
        at = z ^ flip
        return lax.dynamic_index_in_dim(kept, at, 0, False) + lax.dynamic_index_in_dim(
            received, at, 0, False
        )

    parts, beside = lax.optimization_barrier((exchange_with_others(None, "z", 4, piece_of), beside))
    return (piece_of(0) + parts[0]) + (parts[1] + parts[2]), beside


def sum_of_exchange(share, axes):
    parts = exchange_with_others(share, axes, 4)
    return (share + parts[0]) + (parts[1] + parts[2])


def gathered_sum(share):
    column = jnp.stack([share] + exchange_with_others(share, "z", 4))
    return column, exchange_with_others(column, "core", 2)[0]


def lane_column(x, j):
    return jnp.broadcast_to(x[:, j:j + 1], (8, LANES))


def sublane_row(x, j):
    return jnp.broadcast_to(x[j:j + 1, :], (8, LANES))


def pivot_rows(panel, base, lane, sub):
    inside = (lane >= base) & (lane < base + 8)
    columns = [lane_column(panel, base + j) for j in range(8)]
    d = {(i, j): sublane_row(columns[j], i) for j in range(8) for i in range(j, 8)}
    marked = jnp.where(inside, jnp.where(lane - base == sub, 1.0, 0.0), panel)
    y = [sublane_row(marked, j) for j in range(8)]
    lower = {}
    inverse = []
    for j in range(8):
        inverse.append(1.0 / d[j, j])
        for i in range(j + 1, 8):
            lower[i, j] = d[i, j] * inverse[j]
        for k in range(j + 1, 8):
            for i in range(k, 8):
                d[i, k] = d[i, k] - lower[i, j] * d[k, j]
        for i in range(j + 1, 8):
            y[i] = y[i] - lower[i, j] * y[j]
    y = [y[j] * inverse[j] for j in range(8)]
    for j in range(7, -1, -1):
        for i in range(j):
            y[i] = y[i] - lower[j, i] * y[j]
    return y


def eliminated(x, rows, base, lane):
    inside = (lane >= base) & (lane < base + 8)
    t = [lane_column(x, base + j) * rows[j] for j in range(8)]
    total = ((t[0] + t[1]) + (t[2] + t[3])) + ((t[4] + t[5]) + (t[6] + t[7]))
    return jnp.where(inside, 0.0, x) - total


def inverse_of_block(rows):
    lane = lax.broadcasted_iota(jnp.int32, (8, LANES), 1)
    sub = lax.broadcasted_iota(jnp.int32, (8, LANES), 0)
    rows = list(rows)
    for g in range(16):
        pivots = pivot_rows(rows[g], 8 * g, lane, sub)
        for t in range(1, 16):
            h = (g + t) % 16
            rows[h] = eliminated(rows[h], pivots, 8 * g, lane)
        own = pivots[0]
        for j in range(1, 8):
            own = jnp.where(sub == j, pivots[j], own)
        rows[g] = own
    return rows


def solve_kernel(at_ref, near_ref, far_ref, basis_ref, out_ref, sums_ref, system_ref, *, scale):
    core = at_ref[0]
    z = at_ref[1]
    for flip in range(4):
        at = pl.multiple_of((core * 4 + (z ^ flip)) * PIECE, 8)
        sums_ref[pl.ds(at, PIECE), :] = near_ref[flip]
        at = pl.multiple_of(((1 - core) * 4 + (z ^ flip)) * PIECE, 8)
        sums_ref[pl.ds(at, PIECE), :] = far_ref[flip]
    diagonal = (
        lax.broadcasted_iota(jnp.int32, (BLOCK, BLOCK), 0)
        == lax.broadcasted_iota(jnp.int32, (BLOCK, BLOCK), 1)
    )
    for at, (i, j) in enumerate(GRAM_BLOCKS):
        block = sums_ref[at * BLOCK:(at + 1) * BLOCK, :] * scale
        if i == j:
            block = block + jnp.where(diagonal, RIDGE, 0.0)
        else:
            system_ref[j * BLOCK:(j + 1) * BLOCK, i * BLOCK:(i + 1) * BLOCK] = block.T
        system_ref[i * BLOCK:(i + 1) * BLOCK, j * BLOCK:(j + 1) * BLOCK] = block
    for i in range(4):
        row = sums_ref[MOMENT_ROW + 8 * i:MOMENT_ROW + 8 * i + 1, :] * scale
        system_ref[i * BLOCK:(i + 1) * BLOCK, 512:] = jnp.broadcast_to(row, (BLOCK, BLOCK)).T

    for i in range(4):
        lo = i * BLOCK
        inverse = inverse_of_block(
            [system_ref[lo + 8 * g:lo + 8 * g + 8, lo:lo + BLOCK] for g in range(16)]
        )
        inverse = jnp.concatenate(inverse, axis=0)
        solved = exact_dot(inverse, system_ref[lo:lo + BLOCK, lo + BLOCK:])
        for j in range(4):
            if j != i:
                system_ref[j * BLOCK:(j + 1) * BLOCK, lo + BLOCK:] -= exact_dot(
                    system_ref[j * BLOCK:(j + 1) * BLOCK, lo:lo + BLOCK], solved
                )
        system_ref[lo:lo + BLOCK, lo + BLOCK:] = solved
    width = basis_ref.shape[1]
    for lo in range(0, width, 512):
        parts = [jnp.zeros((8, 512), f32) for _ in range(4)]
        for b in range(64):
            coefficient = jnp.tile(system_ref[8 * b:8 * b + 8, 512:], (1, 4))
            parts[b % 4] += coefficient * basis_ref[8 * b:8 * b + 8, lo:lo + 512].astype(f32)
        out_ref[:, lo:lo + 512] = jnp.sum(
            (parts[0] + parts[1]) + (parts[2] + parts[3]), axis=0, keepdims=True
        )


def solve_continuation(near, far, basis, path_count):
    at = jnp.stack([lax.axis_index("core"), lax.axis_index("z")]).astype(jnp.int32)
    whole = pl.BlockSpec((4, PIECE, LANES), lambda i, s: (0, 0, 0))
    return pl.pallas_call(
        lambda *refs: solve_kernel(*refs, scale=1.0 / path_count),
        out_shape=jax.ShapeDtypeStruct((1, basis.shape[1]), f32),
        grid_spec=pltpu.PrefetchScalarGridSpec(
            num_scalar_prefetch=1,
            grid=(1,),
            in_specs=[whole, whole, pl.BlockSpec(basis.shape, lambda i, s: (0, 0))],
            out_specs=pl.BlockSpec((1, basis.shape[1]), lambda i, s: (0, 0)),
            scratch_shapes=[
                pltpu.VMEM((SUM_ROWS, LANES), f32),
                pltpu.VMEM((512, 512 + LANES), f32),
            ],
        ),
        compiler_params=pltpu.CompilerParams(vmem_limit_bytes=20 << 20),
        name="solve_continuation",
    )(at, near, far, basis)


def in_hbm(x):
    return pltpu.with_memory_space_constraint(x, pltpu.HBM)


def increments_kernel(moved_ref, mixer_ref, basket_ref, sent_ref, weights_ref, buffer_ref, copied):
    copies = []
    for tile in range(moved_ref.shape[2] // INCREMENT_TILE):
        span = pl.ds(tile * INCREMENT_TILE, INCREMENT_TILE)
        adjoint = moved_ref[:, :, span].reshape(256, INCREMENT_TILE).astype(f32)
        for date in range(STEPS - 1, -1, -1):
            gain = TIME_STEP * jnp.dot(
                mixer_ref[...], adjoint.astype(bf16), preferred_element_type=f32
            )
            buffer_ref[tile, :, date] = gain.astype(bf16).reshape(8, 32, INCREMENT_TILE)
            if date:
                adjoint = adjoint + gain
        copies.append(
            pltpu.make_async_copy(buffer_ref.at[tile], sent_ref.at[:, :, :, span], copied.at[tile])
        )
        copies[-1].start()
    lane = lax.broadcasted_iota(jnp.int32, (256, LANES), 1)
    weight = jnp.broadcast_to(basket_ref[...], (256, LANES))
    table = weight
    for later in range(1, STEPS):
        gain = sum(
            jnp.dot(mixer_ref[...], part, preferred_element_type=f32) for part in three_terms(weight)
        )
        weight = weight + TIME_STEP * gain
        table = jnp.where(lane == later, weight, table)
    weights_ref[...] = table
    for copy in copies:
        copy.wait()


def increments(moved, mixer, basket, slab_part):
    tiles = slab_part // INCREMENT_TILE
    return pl.pallas_call(
        increments_kernel,
        out_shape=(
            pltpu.HBM((8, STEPS, 32, slab_part), bf16),
            jax.ShapeDtypeStruct((256, LANES), f32),
        ),
        out_specs=(
            pl.BlockSpec(memory_space=pltpu.HBM),
            pl.BlockSpec(memory_space=pltpu.VMEM),
        ),
        scratch_shapes=[
            pltpu.VMEM((tiles, 8, STEPS, 32, INCREMENT_TILE), bf16),
            pltpu.SemaphoreType.DMA((tiles,)),
        ],
        compiler_params=pltpu.CompilerParams(vmem_limit_bytes=20 << 20),
        name="increments",
    )(moved, mixer, basket)


def surface_kernel(slab_ref, *refs):
    continuation_refs = refs[:4]
    (cotangent_ref, gain_ref, shock_ref, weight_ref, exercise_ref, bucket_ref, delta_ref, share_ref,
     continuation_ref, total_ref) = refs[4:]
    step = pl.program_id(0)

    @pl.when(step == 0)
    def _():
        for flip in range(8):
            continuation_ref[pl.ds(slab_ref[0] ^ flip, 1), :] = continuation_refs[flip // 2][
                flip % 2:flip % 2 + 1, :
            ]
        total_ref[...] = jnp.zeros(total_ref.shape, f32)

    continuation = continuation_ref[pl.ds(step, 1), :]
    held = [exercise_ref[date:date + 1, :].astype(f32) * continuation for date in range(STEPS)]
    weights = [weight_ref[:, later:later + 1] for later in range(STEPS)]
    strikes = lax.broadcasted_iota(jnp.int32, (STRIKE_ROWS, DATE_TILE), 0).astype(f32).astype(bf16)
    base = cotangent_ref[...].astype(f32)
    total = total_ref[...]
    for date in range(STEPS - 1, -1, -1):
        base = base + gain_ref[0, date].astype(f32)
        adjoint = base
        for later in range(STEPS - date):
            adjoint = adjoint + held[date + later] * weights[later]
        terms = adjoint * shock_ref[date].astype(f32)
        bucket = bucket_ref[date:date + 1, :]
        column = (bucket & (STRIKE_ROWS - 1)).astype(f32).astype(bf16)
        chosen = jnp.where(strikes == column, jnp.bfloat16(1), jnp.bfloat16(0))
        group = bucket >> STRIKE_BITS
        terms = jnp.concatenate(
            [jnp.where(group == g, terms, 0.0).astype(bf16) for g in range(NK // STRIKE_ROWS)], axis=0
        )
        total = total + lax.dot_general(
            chosen, terms, (((1,), (1,)), ((), ())), preferred_element_type=f32
        )
    delta_ref[...] = adjoint
    total_ref[...] = total

    @pl.when(step == pl.num_programs(0) - 1)
    def _():
        owners = STRIKE_ROWS // 16
        for g in range(NK // STRIKE_ROWS):
            grouped = total[:, 32 * g:32 * g + 32].reshape(owners, 16, 32)
            for q in range(4):
                share_ref[g * owners:(g + 1) * owners, :, 32 * q:32 * q + 32] = grouped[
                    :, 4 * q:4 * q + 4, :
                ]


def surface_and_delta(slab, continuations, cotangent, gains, shocks, weights, exercise, bucket):
    local_paths = cotangent.shape[1]
    whole = pl.BlockSpec((2, DATE_TILE), lambda i, s: (0, 0))
    return pl.pallas_call(
        surface_kernel,
        out_shape=(
            jax.ShapeDtypeStruct((32, local_paths), f32),
            jax.ShapeDtypeStruct((16, 4, LANES), f32),
        ),
        grid_spec=pltpu.PrefetchScalarGridSpec(
            num_scalar_prefetch=1,
            grid=(local_paths // DATE_TILE,),
            in_specs=[whole] * 4 + [
                pl.BlockSpec((32, DATE_TILE), lambda i, s: (0, i)),
                pl.BlockSpec((1, STEPS, 32, DATE_TILE), lambda i, s: (i, 0, 0, 0)),
                pl.BlockSpec((STEPS, 32, DATE_TILE), lambda i, s: (0, 0, i)),
                pl.BlockSpec((32, LANES), lambda i, s: (s[0], 0)),
                pl.BlockSpec((STEPS, DATE_TILE), lambda i, s: (0, i)),
                pl.BlockSpec((STEPS, DATE_TILE), lambda i, s: (0, i)),
            ],
            out_specs=(
                pl.BlockSpec((32, DATE_TILE), lambda i, s: (0, i)),
                pl.BlockSpec((16, 4, LANES), lambda i, s: (0, 0, 0)),
            ),
            scratch_shapes=[pltpu.VMEM((8, DATE_TILE), f32), pltpu.VMEM((STRIKE_ROWS, 32 * (NK // STRIKE_ROWS)), f32)],
        ),
        compiler_params=pltpu.CompilerParams(vmem_limit_bytes=32 << 20),
        name="surface_and_delta",
    )(slab, *continuations, cotangent, gains, in_hbm(shocks), weights, exercise, bucket)


def per_device(prices, loadings, basis_w, basis_bias, payoff, in_fit, cotangent, shocks, corr_gen,
               basket, exercise, bucket):
    local_paths = prices.shape[1]
    slab_part = local_paths // 8
    path_count = float(local_paths * 16)
    slab = lax.axis_index(STOCK_AXES).astype(jnp.int32).reshape(1)

    pieces = jnp.moveaxis(prices.reshape(32, 8, slab_part), 1, 0)
    table = jnp.broadcast_to(jnp.pad(loadings, ((0, 0), (0, LANES - 32)))[None], (8, 32, LANES))
    moved_prices = lax.all_to_all(
        jnp.concatenate([pieces, table], axis=2), STOCK_AXES, 0, 0, tiled=True
    )
    slabs = jnp.moveaxis(cotangent.reshape(32, 8, slab_part), 1, 0)
    small = (basis_w, basis_bias[:, None], payoff[None, :], in_fit[None, :],
             basket[:, None])
    slabs, moved_prices, small = lax.optimization_barrier((slabs, moved_prices, small))
    basis_w, bias, payoff, in_fit, basket = small
    moved = lax.all_to_all(slabs, STOCK_AXES, 0, 0, tiled=True)
    basis_w = in_hbm(basis_w)
    in_fit = in_hbm(in_fit)
    place = jnp.stack([slab[0], lax.axis_index("core").astype(jnp.int32)])
    basis, kept, other = regression_sums(
        place, moved_prices, basis_w, bias, payoff, in_fit, slab_part
    )
    share, moved = sum_over_cores_and_z(kept, other, moved)
    sent, weights = increments(moved, corr_gen, basket, slab_part)
    share = sum_of_exchange(share, ("ylo", "yhi"))
    parts = exchange_with_others(share, "x", 4)
    parts, sent = lax.optimization_barrier((parts, sent))
    share = (share + parts[0]) + (parts[1] + parts[2])
    gains = lax.all_to_all(sent, STOCK_AXES, 0, 0, tiled=True)
    near, far = gathered_sum(share)
    continuation = solve_continuation(near, far, basis, path_count)
    pair = jnp.concatenate([continuation] + exchange_with_others(continuation, "yhi", 2), axis=0)
    continuations = [pair] + exchange_with_others(pair, "x", 4)
    delta, surface = surface_and_delta(
        slab, continuations, cotangent, gains, shocks, weights, exercise, bucket
    )
    surface = lax.all_to_all(surface, PATH_AXES, 0, 0, tiled=True)
    surface = jnp.sum(surface, axis=0).reshape(4, 4, 32)
    surface = jnp.transpose(surface, (2, 1, 0)).reshape(32, 16)
    return delta, surface


def solution(mesh):
    fine = Mesh(mesh.devices.reshape(FINE), ALL_AXES)
    stocks, paths = STOCK_AXES, PATH_AXES
    return jax.shard_map(
        per_device,
        mesh=fine,
        in_specs=(
            P(stocks, paths),
            P(stocks, None),
            P(),
            P(),
            P(paths),
            P(paths),
            P(stocks, paths),
            P(None, stocks, paths),
            P(),
            P(),
            P(None, paths),
            P(None, paths),
        ),
        out_specs=(P(stocks, paths), P(stocks, paths)),
        check_vma=False,
    )
```
